32 devices in a mesh: fsdp: 8 (over z, y), tensor: 4 (over x, core).
Axes of the slice: x: 2, y: 2, z: 4, core: 2. Of those that a mesh axis runs over, the one named last changes fastest.
Arguments:
- tokens: bfloat16 [64, 1024, 1024], P('fsdp', 'tensor'), may hold values from -6 to 6
- cotangent: bfloat16 [64, 1024, 1024], P('fsdp', 'tensor'), may hold values from -6 to 6
- routed_index: int32 [64, 128], P('fsdp'), may hold values from 0 to 1023, as said below
- query_weight: bfloat16 [1024, 1024], P('fsdp', 'tensor'), may hold values from -0.1875 to 0.1875
- key_weight: bfloat16 [1024, 1024], P('fsdp', 'tensor'), may hold values from -0.1875 to 0.1875
- value_weight: bfloat16 [1024, 1024], P('fsdp', 'tensor'), may hold values from -0.1875 to 0.1875
- output_weight: bfloat16 [1024, 1024], P('tensor', 'fsdp'), may hold values from -0.5 to 0.5
- up_weight: bfloat16 [1024, 4096], P('fsdp', 'tensor'), may hold values from -0.1875 to 0.1875
- down_weight: bfloat16 [4096, 1024], P('tensor', 'fsdp'), may hold values from -0.09375 to 0.09375
- router_weight: bfloat16 [1024], P('fsdp'), may hold values from -0.1875 to 0.1875
- attn_gain: bfloat16 [1024], P('fsdp'), may hold values from 0.5 to 1.5
- mlp_gain: bfloat16 [1024], P('fsdp'), may hold values from 0.5 to 1.5
Outputs:
- mixed: bfloat16 [64, 1024, 1024], P('fsdp', 'tensor')
- token_grad: bfloat16 [64, 1024, 1024], P('fsdp', 'tensor')
- query_weight_grad: float32 [1024, 1024], P('fsdp', 'tensor')
- key_weight_grad: float32 [1024, 1024], P('fsdp', 'tensor')
- value_weight_grad: float32 [1024, 1024], P('fsdp', 'tensor')
- output_weight_grad: float32 [1024, 1024], P('tensor', 'fsdp')
- up_weight_grad: float32 [1024, 4096], P('fsdp', 'tensor')
- down_weight_grad: float32 [4096, 1024], P('tensor', 'fsdp')
- router_weight_grad: float32 [1024], P('fsdp')
- attn_gain_grad: float32 [1024], P('fsdp')
- mlp_gain_grad: float32 [1024], P('fsdp')
The draws below stay inside these ranges and needn't reach their ends.
Inputs may be any that keep to these rules, and one draw needn't show every extreme that they name: `routed_index`: each row holds 128 distinct positions of one sequence in ascending order; its first is 0 and its last is 1023.
All inputs are finite; a program needn't handle non-finite values.
Results may differ from the reference program's by a relative error of at most 0.011.
Values may be sent and summed in bfloat16 or wider, within the bound.
No kernel may reach another device: no remote copies, remote signals or barrier semaphores. Data moves between devices by JAX's collectives and lax.ppermute only.
A program may use at most 192 MiB of HBM per device.

```python
import math
import jax
import jax.numpy as jnp
from jax import lax

D = 1024
HEADS = 16
HEAD_DIM = 64
FF = 4096
SEQ_LEN = 1024
BLOCK = 256
ROUTED = 128
SEQS = 64


def draw_routed_index(key, part):
    seq_keys = jax.random.split(jax.random.fold_in(key, 11), SEQS)

    def pick_one(one_key):
        ordering = jax.random.permutation(one_key, SEQ_LEN)
        picked = jnp.sort(ordering[:ROUTED]).astype(jnp.int32)
        picked = picked.at[0].set(0)
        return picked.at[ROUTED - 1].set(SEQ_LEN - 1)
    return jax.vmap(pick_one)(seq_keys).astype(jnp.int32)


def strengthened(array, stream_key, source, target, blocks, factor):
    owner, partner = [(jnp.arange(array.shape[position]) // (array.shape[position] // blocks)).reshape([-1 if axis == position else 1 for axis in range(array.ndim)]) for position in (source, target)]
    chosen = jax.random.permutation(stream_key, blocks)[partner]
    strong = (owner == chosen) | (owner == (partner + blocks // 2) % blocks)
    return jnp.where(strong, factor * array, array)


def levels(rng, shape, cuts, least, top_value):
    def one(axis_at, shards_of):
        steps = jax.random.uniform(jax.random.fold_in(jax.random.fold_in(rng, 6), axis_at), (shards_of,), jnp.float32, least / len(cuts), top_value / len(cuts))
        return jnp.repeat(jnp.exp(steps), shape[axis_at] // shards_of).reshape((-1,) + (1,) * (len(shape) - axis_at - 1))

    level = one(*cuts[0])
    for cut in cuts[1:]:
        level = level * one(*cut)
    return level


def normal_values(own_key, extent, scale, limit, cuts=(), held_as=jnp.bfloat16):
    level = levels(own_key, extent, cuts, -0.22, 0.18) if cuts else 1.0
    array = jax.random.normal(own_key, extent, jnp.float32) * scale * level
    return jnp.minimum(jnp.maximum(array, -limit), limit).astype(held_as)


def bell_draw_with(stream_key, dims, spread, bound, shards, heavy, dtype=jnp.bfloat16):
    drawn = spread * jax.random.normal(stream_key, dims, jnp.float32)
    if shards:
        drawn = drawn * levels(stream_key, dims, shards, -0.22, 0.18)
    return jnp.clip(strengthened(drawn, jax.random.fold_in(stream_key, 3), *heavy), -bound, bound).astype(dtype)


def setup_inputs(seed: int = 0) -> dict:
    seeds = jax.random.split(jax.random.key(seed), 13)
    tokens = bell_draw_with(seeds[0], (SEQS, SEQ_LEN, D), 1.0, 6.0, ((0, 8), (1, 4)), (0, 2, 8, 2.0))
    cotangent = bell_draw_with(seeds[1], (SEQS, SEQ_LEN, D), 1.0, 6.0, ((0, 8), (1, 4)), (0, 2, 8, 2.0))
    routed_index = draw_routed_index(jax.random.fold_in(seeds[12], 71), 0)
    query_weight = normal_values(seeds[3], (D, D), D ** -0.5, 0.1875, ((0, 8), (1, 4)))
    key_weight = normal_values(seeds[4], (D, D), D ** -0.5, 0.1875, ((0, 8), (1, 4)))
    value_weight = normal_values(seeds[5], (D, D), D ** -0.5, 0.1875, ((0, 8), (1, 4)))
    output_weight = normal_values(seeds[6], (D, D), (D // 8) ** -0.5, 0.5, ((0, 4), (1, 8)))
    up_weight = normal_values(seeds[7], (D, FF), D ** -0.5, 0.1875, ((0, 8), (1, 4)))
    down_weight = normal_values(seeds[8], (FF, D), FF ** -0.5, 0.09375, ((0, 4), (1, 8)))
    router_weight = normal_values(seeds[9], (D,), D ** -0.5, 0.1875, ((0, 8),))
    attn_gain = jnp.clip(1.0 + 0.1 * jax.random.normal(seeds[10], (D,), jnp.float32), 0.5, 1.5).astype(jnp.bfloat16)
    mlp_gain = jnp.clip(1.0 + 0.1 * jax.random.normal(seeds[11], (D,), jnp.float32), 0.5, 1.5).astype(jnp.bfloat16)
    return {"tokens": tokens, "cotangent": cotangent, "routed_index": routed_index, "query_weight": query_weight, "key_weight": key_weight, "value_weight": value_weight, "output_weight": output_weight, "up_weight": up_weight, "down_weight": down_weight, "router_weight": router_weight, "attn_gain": attn_gain, "mlp_gain": mlp_gain}


EPS = 1e-06
NEG = -1e+30
HIGH = lax.Precision.HIGHEST

@jax.custom_vjp
def low(v):
    return lax.optimization_barrier(v.astype(jnp.bfloat16)).astype(jnp.float32)

@jax.custom_vjp
def low_back(v):
    return v

def low_keep(v):
    return (low(v), None)

def low_pass(kept, grad):
    return (grad,)

def back_keep(v):
    return (v, None)

def back_low(kept, grad):
    return (low(grad),)
low.defvjp(low_keep, low_pass)
low_back.defvjp(back_keep, back_low)

def rms_norm(inputs, gain):
    return inputs * lax.rsqrt(lax.optimization_barrier(jnp.mean(inputs * inputs, axis=-1, keepdims=True)) + EPS) * gain

def group_forward(rows_in, index_group, weight_set):
    query_weight, key_weight, value_weight, output_weight, up_weight, down_weight, router_weight, attn_gain, mlp_gain = weight_set
    seq_count = rows_in.shape[0]
    gate_value = jax.nn.sigmoid(jnp.einsum('skd,d->sk', rows_in, router_weight, precision=HIGH))
    first_normed = low(rms_norm(rows_in, attn_gain))

    def project(weight):
        product = jnp.einsum('skd,dc->skc', first_normed, weight, precision=HIGH)
        return low(low_back(product)).reshape(seq_count, ROUTED, HEADS, HEAD_DIM)
    query_heads = project(query_weight)
    key_heads = project(key_weight)
    value_heads = project(value_weight)
    blocks = index_group // BLOCK
    allowed = blocks[:, None, :] <= blocks[:, :, None]
    scores = low_back(jnp.einsum('sqhe,skhe->shqk', query_heads, key_heads, precision=HIGH) * HEAD_DIM ** (-0.5))
    scores = jnp.where(allowed[:, None], scores, NEG)
    attn_probs = low(jax.nn.softmax(scores, axis=-1))
    context = low(low_back(jnp.einsum('shqk,skhe->sqhe', attn_probs, value_heads, precision=HIGH)))
    context = context.reshape(seq_count, ROUTED, D)
    attn_out = low_back(jnp.einsum('skc,cd->skd', context, output_weight, precision=HIGH))
    hidden = rows_in + attn_out
    second_normed = low(rms_norm(hidden, mlp_gain))
    up_value = low_back(jnp.einsum('skd,df->skf', second_normed, up_weight, precision=HIGH))
    activated = low(jax.nn.gelu(up_value))
    mlp_out = low_back(jnp.einsum('skf,fd->skd', activated, down_weight, precision=HIGH))
    return rows_in + gate_value[:, :, None] * (attn_out + mlp_out)

def routed_forward(routed_rows, index_all, weight_set):
    group_size = math.gcd(SEQS, 32)
    row_groups = routed_rows.reshape(-1, group_size, ROUTED, D)
    index_groups = index_all.reshape(-1, group_size, ROUTED)
    step_fn = jax.checkpoint(lambda rows_in, index_group: group_forward(rows_in, index_group, weight_set))

    def scan_step(carry, item):
        return (carry, step_fn(item[0], item[1]))
    carry_end, outputs = lax.scan(scan_step, jnp.zeros((), jnp.float32), (row_groups, index_groups))
    return outputs.reshape(SEQS, ROUTED, D)

def reference(tokens, cotangent, routed_index, query_weight, key_weight, value_weight, output_weight, up_weight, down_weight, router_weight, attn_gain, mlp_gain):
    seq_ids = jnp.arange(SEQS).astype(jnp.int32)[:, None]
    positions = routed_index.astype(jnp.int32)
    routed_rows = jnp.take_along_axis(tokens, positions[:, :, None], axis=1).astype(jnp.float32)
    routed_cot = jnp.take_along_axis(cotangent, positions[:, :, None], axis=1).astype(jnp.float32)
    weight_set = tuple((weight_item.astype(jnp.float32) for weight_item in (query_weight, key_weight, value_weight, output_weight, up_weight, down_weight, router_weight, attn_gain, mlp_gain)))

    def closed(rows_in, weights_in):
        return routed_forward(rows_in, positions, weights_in)
    out_rows, pullback = jax.vjp(closed, routed_rows, weight_set)
    rows_grad, weight_grads = pullback(routed_cot)
    mixed = tokens.at[seq_ids, positions].set(out_rows.astype(jnp.bfloat16))
    token_grad = cotangent.at[seq_ids, positions].set(rows_grad.astype(jnp.bfloat16))
    return (mixed, token_grad, weight_grads[0], weight_grads[1], weight_grads[2], weight_grads[3], weight_grads[4], weight_grads[5], weight_grads[6], weight_grads[7], weight_grads[8])
```

```python
import functools

import jax
import jax.numpy as jnp
from jax import lax
from jax.experimental import pallas as pl
from jax.experimental.pallas import tpu as pltpu
from jax.sharding import PartitionSpec as P

HEAD_DIM = 64
BLOCK = 256
EPS = 1e-06
NEG = -1e30
F32 = jnp.float32
BF16 = jnp.bfloat16
GELU_C = 0.7978845608028654
GELU_A = 0.044715

VMEM_SPEC = pl.BlockSpec(memory_space=pltpu.VMEM)
SMEM_SPEC = pl.BlockSpec(memory_space=pltpu.SMEM)
PARAMS = pltpu.CompilerParams(vmem_limit_bytes=48 << 20)


def mm(a, b):
    return jnp.dot(a, b, preferred_element_type=F32)


def mm_t(a, b):
    return lax.dot_general(a, b, (((1,), (1,)), ((), ())), preferred_element_type=F32)


def t_mm(a, b):
    return lax.dot_general(a, b, (((0,), (0,)), ((), ())), preferred_element_type=F32)


def shape(dims, dtype):
    return jax.ShapeDtypeStruct(dims, dtype)


def cost(flops, bytes_accessed):
    return pl.CostEstimate(
        flops=int(flops), bytes_accessed=int(bytes_accessed), transcendentals=0
    )


def tiles(total, width, step):
    def body(j, carry):
        step(pl.ds(pl.multiple_of(j * width, width), width), j)
        return carry

    lax.fori_loop(0, total // width, body, 0)


def pick_kernel(order, onehot, values, out):
    out[...] = mm(onehot[0], values[0]).astype(BF16)


def pick_rows(values, onehot, order):
    count = order.shape[0]
    _, routed, span = onehot.shape
    width = values.shape[2]
    return pl.pallas_call(
        pick_kernel,
        grid_spec=pltpu.PrefetchScalarGridSpec(
            num_scalar_prefetch=1,
            grid=(count,),
            in_specs=[
                pl.BlockSpec((1, routed, span), lambda i, o: (o[i], 0, 0)),
                pl.BlockSpec((1, span, width), lambda i, o: (o[i], 0, 0)),
            ],
            out_specs=pl.BlockSpec((routed, width), lambda i, o: (i, 0)),
        ),
        out_shape=shape((count * routed, width), BF16),
        compiler_params=PARAMS,
        cost_estimate=cost(2 * count * routed * span * width, count * (span + routed) * width * 2),
        name="pick_rows",
    )(order, onehot, values)


def place_kernel(order, onehot_t, r0, r1, r2, r3, base, out):
    piece = pl.program_id(0) // 2
    rows = jnp.where(
        piece < 2,
        jnp.where(piece == 0, r0[...], r1[...]),
        jnp.where(piece == 2, r2[...], r3[...]),
    )
    hot = onehot_t[0]
    taken = jnp.sum(hot.astype(F32), axis=1, keepdims=True) > 0.0
    placed = mm(hot, rows)
    out[0] = jnp.where(taken, placed, base[0].astype(F32)).astype(BF16)


def place_rows(base, onehot_t, pieces, order):
    seqs, span, width = base.shape
    routed = onehot_t.shape[2]
    per = seqs // 4

    def piece_spec(m):
        return pl.BlockSpec(
            (routed, width), lambda i, o: (jnp.clip(i - m * per, 0, per - 1), 0)
        )

    return pl.pallas_call(
        place_kernel,
        grid_spec=pltpu.PrefetchScalarGridSpec(
            num_scalar_prefetch=1,
            grid=(seqs,),
            in_specs=[pl.BlockSpec((1, span, routed), lambda i, o: (o[i], 0, 0))]
            + [piece_spec(m) for m in range(4)]
            + [pl.BlockSpec((1, span, width), lambda i, o: (o[i], 0, 0))],
            out_specs=pl.BlockSpec((1, span, width), lambda i, o: (o[i], 0, 0)),
        ),
        out_shape=shape(base.shape, BF16),
        compiler_params=PARAMS,
        cost_estimate=cost(2 * seqs * routed * span * width, 2 * seqs * span * width * 2),
        name="place_rows",
    )(order, onehot_t, *pieces, base)


def row_call(body, name, inputs, outputs, rows, width, steps=2):
    block = rows // steps
    in_specs = []
    for array, kind in inputs:
        if kind == "w":
            in_specs.append(pl.BlockSpec(array.shape, lambda i: (0, 0)))
        else:
            in_specs.append(pl.BlockSpec((block, array.shape[1]), lambda i: (i, 0)))
    out_specs = []
    out_shapes = []
    for dims, dtype, kind in outputs:
        out_shapes.append(shape(dims, dtype))
        if kind == "w":
            out_specs.append(pl.BlockSpec(dims, lambda i: (0, 0)))
        else:
            out_specs.append(pl.BlockSpec((block, dims[1]), lambda i: (i, 0)))
    return pl.pallas_call(
        body,
        grid=(steps,),
        in_specs=in_specs,
        out_specs=out_specs,
        out_shape=out_shapes,
        compiler_params=PARAMS,
        cost_estimate=cost(20 * rows * width, 2 * rows * width * (len(inputs) + len(outputs))),
        name=name,
    )(*[array for array, _ in inputs])


def row_mean(x):
    return jnp.mean(x, axis=-1, keepdims=True)


def total3(a, b, c):
    return a[...].astype(F32) + b[...].astype(F32) + c[...].astype(F32)


def lanes(col):
    return jnp.broadcast_to(col, (col.shape[0], 128))


def fold(x):
    return jnp.sum(x.reshape(-1, 8, x.shape[1]), axis=0)


def accumulate(ref, value):
    @pl.when(pl.program_id(0) == 0)
    def _():
        ref[...] = value

    @pl.when(pl.program_id(0) > 0)
    def _():
        ref[...] += value


def first_norm_body(a, b, c, vec, rows_out, normed_out, gate_out):
    rows = total3(a, b, c)
    rows_out[...] = rows.astype(BF16)
    logit = jnp.sum(rows * vec[0:1, :], axis=-1, keepdims=True)
    gate_out[...] = lanes(jax.nn.sigmoid(logit))
    scale = lax.rsqrt(row_mean(rows * rows) + EPS)
    normed_out[...] = (rows * scale * vec[1:2, :]).astype(BF16)


def cot_body(a, b, c, gate, cot_out, grad_out):
    cot = total3(a, b, c)
    cot_out[...] = cot.astype(BF16)
    grad_out[...] = (cot * gate[:, 0:1]).astype(BF16)


def second_norm_body(rows, a, b, c, vec, attn_out, normed_out):
    attn = total3(a, b, c)
    attn_out[...] = attn
    hidden = rows[...].astype(F32) + attn
    scale = lax.rsqrt(row_mean(hidden * hidden) + EPS)
    normed_out[...] = (hidden * scale * vec[2:3, :]).astype(BF16)


def second_back_body(rows, attn, cot, gate, a, b, c, vec, grad_out, hidden_out, gain_out):
    second_grad = total3(a, b, c)
    hidden = rows[...].astype(F32) + attn[...]
    scale = lax.rsqrt(row_mean(hidden * hidden) + EPS)
    normal = hidden * scale
    grad = second_grad * vec[2:3, :]
    hidden_grad = scale * (grad - normal * row_mean(grad * normal))
    hidden_out[...] = hidden_grad
    grad_out[...] = (cot[...].astype(F32) * gate[:, 0:1] + hidden_grad).astype(BF16)
    accumulate(gain_out, fold(second_grad * normal))


def out_body(rows, attn, cot, gate, a, b, c, rows_out, gate_grad_out, router_out):
    branch = attn[...] + total3(a, b, c)
    x = rows[...].astype(F32)
    g = gate[:, 0:1]
    rows_out[...] = (x + g * branch).astype(BF16)
    gate_grad = jnp.sum(cot[...].astype(F32) * branch, axis=-1, keepdims=True) * g * (1.0 - g)
    gate_grad_out[...] = lanes(gate_grad)
    accumulate(router_out, fold(x * gate_grad))


def first_back_body(
    rows, cot, gate_grad, hidden_grad, a, b, c, vec, router_part, second_part, grad_out, vec_out, acc
):
    first_grad = total3(a, b, c)
    x = rows[...].astype(F32)
    scale = lax.rsqrt(row_mean(x * x) + EPS)
    normal = x * scale
    grad = first_grad * vec[1:2, :]
    norm_grad = scale * (grad - normal * row_mean(grad * normal))
    grad_out[...] = (
        cot[...].astype(F32) + gate_grad[:, 0:1] * vec[0:1, :] + hidden_grad[...] + norm_grad
    ).astype(BF16)
    accumulate(acc, fold(first_grad * normal))

    @pl.when(pl.program_id(0) == pl.num_programs(0) - 1)
    def _():
        vec_out[0:1, :] = jnp.sum(router_part[...], axis=0, keepdims=True)
        vec_out[1:2, :] = jnp.sum(acc[...], axis=0, keepdims=True)
        vec_out[2:3, :] = jnp.sum(second_part[...], axis=0, keepdims=True)
        vec_out[3:8, :] = jnp.zeros_like(vec_out[3:8, :])


def assemble_kernel(places, *refs):
    *pieces, out = refs
    for number, piece in enumerate(pieces):
        depth = piece.shape[0]
        start = pl.multiple_of(places[number] * depth, depth)
        out[pl.ds(start, depth), :] = piece[...]


def assemble(pieces, places):
    depth, width = pieces[0].shape
    return pl.pallas_call(
        assemble_kernel,
        in_specs=[SMEM_SPEC] + [VMEM_SPEC] * len(pieces),
        out_specs=VMEM_SPEC,
        out_shape=shape((depth * len(pieces), width), BF16),
        compiler_params=PARAMS,
        cost_estimate=cost(0, 4 * depth * len(pieces) * width),
        name="assemble",
    )(places, *pieces)


def head_masks(width):
    lane = lax.broadcasted_iota(jnp.int32, (1, width), 1) // HEAD_DIM
    return [(lane == h).astype(BF16) for h in range(width // HEAD_DIM)]


def spread(x, masks):
    return jnp.concatenate([x * mask for mask in masks], axis=0)


def side_by_side(x, count):
    rows = x.shape[0] // count
    return jnp.concatenate([x[h * rows : (h + 1) * rows] for h in range(count)], axis=1)


def seq_probs(q4, k, bias, count):
    scores = mm_t(q4, k) * (HEAD_DIM**-0.5)
    scores = scores + jnp.concatenate([bias] * count, axis=0)
    top = jnp.max(scores, axis=-1, keepdims=True)
    weight = jnp.exp(scores - top)
    return weight / jnp.sum(weight, axis=-1, keepdims=True)


def attn_fwd_kernel(order, xa, xb, w, bias, qkv, ctx, pa, pb):
    half = xa.shape[0]
    local = ctx.shape[1]
    routed = bias.shape[1]
    heads = local // HEAD_DIM
    masks = head_masks(local)

    def project(cols, j):
        qkv[0:half, cols] = mm(xa[...], w[:, cols]).astype(BF16)
        qkv[half : 2 * half, cols] = mm(xb[...], w[:, cols]).astype(BF16)

    tiles(3 * local, local, project)

    def seq(rows, s):
        q = qkv[rows, 0:local]
        k = qkv[rows, local : 2 * local]
        v = qkv[rows, 2 * local : 3 * local]
        probs = seq_probs(spread(q, masks), k, bias[order[s]], heads).astype(BF16)
        ctx[rows, :] = mm(side_by_side(probs, heads), spread(v, masks)).astype(BF16)

    tiles(2 * half, routed, seq)

    def emit(cols, j):
        wo = w[cols, 3 * local : 4 * local]
        pa[:, cols] = mm_t(ctx[0:half, :], wo).astype(BF16)
        pb[:, cols] = mm_t(ctx[half : 2 * half, :], wo).astype(BF16)

    tiles(pa.shape[1], 256, emit)


def attn_fwd(xa, xb, w, bias, order, local):
    rows, width = xa.shape
    return pl.pallas_call(
        attn_fwd_kernel,
        in_specs=[SMEM_SPEC] + [VMEM_SPEC] * 4,
        out_specs=[VMEM_SPEC] * 4,
        out_shape=[
            shape((2 * rows, 3 * local), BF16),
            shape((2 * rows, local), BF16),
            shape((rows, width), BF16),
            shape((rows, width), BF16),
        ],
        compiler_params=PARAMS,
        cost_estimate=cost(16 * rows * width * local * 2, 8 * rows * width + 2 * width * width),
        name="attn_fwd",
    )(order, xa, xb, w, bias)


def attn_bwd_kernel(order, ga, gb, w, qkv, bias, dqkv, fa, fb, cg):
    half = ga.shape[0]
    local = cg.shape[1]
    routed = bias.shape[1]
    heads = local // HEAD_DIM
    masks = head_masks(local)
    wo = w[:, 3 * local : 4 * local]
    cg[0:half, :] = mm(ga[...], wo).astype(BF16)
    cg[half : 2 * half, :] = mm(gb[...], wo).astype(BF16)

    def seq(rows, s):
        q4 = spread(qkv[rows, 0:local], masks)
        k = qkv[rows, local : 2 * local]
        v = qkv[rows, 2 * local : 3 * local]
        exact = seq_probs(q4, k, bias[order[s]], heads)
        c4 = spread(cg[rows, :], masks)
        prob_grad = mm_t(c4, v)
        dqkv[rows, 2 * local : 3 * local] = t_mm(exact.astype(BF16), c4).astype(BF16)
        inner = jnp.sum(exact * prob_grad, axis=-1, keepdims=True)
        score_grad = (exact * (prob_grad - inner)).astype(BF16)
        scale = HEAD_DIM**-0.5
        dq = mm(side_by_side(score_grad, heads), spread(k, masks)) * scale
        dqkv[rows, 0:local] = dq.astype(BF16)
        dqkv[rows, local : 2 * local] = (t_mm(score_grad, q4) * scale).astype(BF16)

    tiles(2 * half, routed, seq)

    def emit(cols, j):
        wj = w[cols, 0 : 3 * local]
        fa[:, cols] = mm_t(dqkv[0:half, :], wj).astype(BF16)
        fb[:, cols] = mm_t(dqkv[half : 2 * half, :], wj).astype(BF16)

    tiles(fa.shape[1], 256, emit)


def attn_bwd(ga, gb, w, qkv, bias, order, local):
    rows, width = ga.shape
    return pl.pallas_call(
        attn_bwd_kernel,
        in_specs=[SMEM_SPEC] + [VMEM_SPEC] * 5,
        out_specs=[VMEM_SPEC] * 3,
        out_shape=[
            shape((2 * rows, 3 * local), BF16),
            shape((rows, width), BF16),
            shape((rows, width), BF16),
        ],
        scratch_shapes=[pltpu.VMEM((2 * rows, local), BF16)],
        compiler_params=PARAMS,
        cost_estimate=cost(24 * rows * width * local * 2, 8 * rows * width + 2 * width * width),
        name="attn_bwd",
    )(order, ga, gb, w, qkv, bias)


def mlp_kernel(na, nb, ga, gb, w, act, ug, da, db, ma, mb):
    rows, width = na.shape
    part, both, ff = w.shape
    depth = both // 2

    def up(cols, j):
        wu = w[:, 0:depth, cols].reshape(width, -1)
        wd = w[:, depth:both, cols].reshape(width, -1)
        for n, g, at in ((na, ga, 0), (nb, gb, rows)):
            x = mm(n[...], wu)
            inner = jnp.tanh(GELU_C * (x + GELU_A * (x * x * x)))
            half_in = 0.5 * (1.0 + inner)
            act[at : at + rows, cols] = (x * half_in).astype(BF16)
            slope = half_in + (0.5 * GELU_C) * x * (1.0 - inner * inner) * (
                1.0 + (3.0 * GELU_A) * (x * x)
            )
            ug[at : at + rows, cols] = (mm(g[...], wd) * slope).astype(BF16)

    tiles(ff, 256, up)
    group = part * 256 // width

    def back(cols, j):
        wu = w[pl.ds(j * group, group), 0:depth, :].reshape(256, -1)
        da[:, cols] = mm_t(ug[0:rows, :], wu).astype(BF16)
        db[:, cols] = mm_t(ug[rows : 2 * rows, :], wu).astype(BF16)

    tiles(width, 256, back)

    def down(cols, j):
        wd = w[pl.ds(j * group, group), depth:both, :].reshape(256, -1)
        ma[:, cols] = mm_t(act[0:rows, :], wd).astype(BF16)
        mb[:, cols] = mm_t(act[rows : 2 * rows, :], wd).astype(BF16)

    tiles(width, 256, down)


def mlp_both(na, nb, ga, gb, w):
    rows, width = na.shape
    ff = w.shape[2]
    return pl.pallas_call(
        mlp_kernel,
        in_specs=[VMEM_SPEC] * 5,
        out_specs=[VMEM_SPEC] * 6,
        out_shape=[shape((2 * rows, ff), BF16)] * 2 + [shape((rows, width), BF16)] * 4,
        compiler_params=PARAMS,
        cost_estimate=cost(16 * rows * width * ff, 24 * rows * width + 4 * width * ff),
        name="mlp",
    )(na, nb, ga, gb, w)


def grads_kernel(info, *refs, jobs, count):
    per_job = []
    at = 0
    for pieces, halves in jobs:
        per_job.append((refs[at : at + pieces], refs[at + pieces : at + pieces + halves]))
        at += pieces + halves
    sends = refs[at : at + count]
    keeps = refs[at + count : at + 2 * count]
    xt = refs[at + 2 * count]
    depth = 128
    low = info[count] == 0
    for o in range(count):
        cols = pl.ds(pl.multiple_of(info[o] * 256, 256), 256)
        row = 0
        lane = 0
        for xs, ys in per_job:
            step = xs[0].shape[0]
            for m, x in enumerate(xs):
                xt[:, m * step : (m + 1) * step] = x[:, cols].T
            wide = ys[0].shape[1]
            if lane + wide > sends[0].shape[1]:
                row, lane = row + depth, 0

            def block(ncols, j, ys=ys, row=row, lane=lane, o=o):
                size = ys[0].shape[0]
                out = mm(xt[:, 0:size], ys[0][:, ncols]) + mm(
                    xt[:, size : 2 * size], ys[1][:, ncols]
                )
                first, second = out[0:depth], out[depth:256]
                dst = pl.ds(pl.multiple_of(j * 256, 256) + lane, 256)
                sends[o][row : row + depth, dst] = jnp.where(low, second, first).astype(BF16)
                keeps[o][row : row + depth, dst] = jnp.where(low, first, second)

            tiles(wide, 256, block)
            lane += wide


def grad_blocks(jobs, info, rows, width, count, name):
    args = [a for xs, ys in jobs for a in list(xs) + list(ys)]
    total = sum(x.shape[0] for x in jobs[0][0])
    out = pl.pallas_call(
        functools.partial(
            grads_kernel, jobs=[(len(xs), len(ys)) for xs, ys in jobs], count=count
        ),
        in_specs=[SMEM_SPEC] + [VMEM_SPEC] * len(args),
        out_specs=[VMEM_SPEC] * (2 * count),
        out_shape=[shape((rows, width), BF16)] * count + [shape((rows, width), F32)] * count,
        scratch_shapes=[pltpu.VMEM((256, total), BF16)],
        compiler_params=PARAMS,
        cost_estimate=cost(4 * count * rows * width * total, 6 * count * rows * width),
        name=name,
    )(info, *args)
    return out[:count], out[count:]


def swap(x, axis, mask):
    size = lax.axis_size(axis)
    return lax.ppermute(x, axis, [(i, i ^ mask) for i in range(size)])


def gather_rows(own):
    second = swap(own, "tensor", 2)
    first = swap(own, "tensor", 1)
    return own, first, second, swap(second, "tensor", 1)


def scatter_far(near, diag):
    got = swap(diag, "tensor", 1)
    return swap((near.astype(F32) + got.astype(F32)).astype(BF16), "tensor", 2)


def z_perm(size, step, shift):
    places = size // step
    return [
        (((f // step + shift) % places) * step + f % step, f) for f in range(size)
    ]


def fsdp_gather(piece):
    size = lax.axis_size("fsdp")
    me = lax.axis_index("fsdp")
    if size != 8:
        return lax.all_gather(piece, "fsdp", axis=0, tiled=True)
    got = [piece] + [lax.ppermute(piece, "fsdp", z_perm(size, 2, o)) for o in (1, 3, 2)]
    near = [me] + [(me + 2 * o) % size for o in (1, 3, 2)]
    pieces = got + [swap(g, "fsdp", 1) for g in got]
    places = jnp.stack(near + [n ^ 1 for n in near])
    return assemble(pieces, places)


def fsdp_finish(sends, keeps, shifts):
    size = lax.axis_size("fsdp")
    got = [swap(s, "fsdp", 1) for s in sends]
    total = None
    parts = []
    for o, keep, g in zip(shifts, keeps, got):
        both = keep + g.astype(F32)
        if o == 0:
            total = both
        else:
            parts.append(lax.ppermute(both.astype(BF16), "fsdp", z_perm(size, 2, 4 - o)))
    for part in parts:
        total = total + part.astype(F32)
    return total


def shards(
    tokens,
    cotangent,
    routed_index,
    query_weight,
    key_weight,
    value_weight,
    output_weight,
    up_weight,
    down_weight,
    router_weight,
    attn_gain,
    mlp_gain,
):
    fsdp = lax.axis_size("fsdp")
    me_f = lax.axis_index("fsdp")
    me_t = lax.axis_index("tensor")
    seqs, span, width = tokens.shape
    routed = routed_index.shape[1]
    per = seqs // lax.axis_size("tensor")
    local = query_weight.shape[1]
    depth = query_weight.shape[0]
    rows = per * routed

    up_down = lax.all_gather(
        jnp.concatenate([up_weight, down_weight.T], axis=0), "fsdp", axis=0, tiled=True
    ).reshape(fsdp, 2 * depth, -1)
    attn_piece = jnp.concatenate(
        [query_weight, key_weight, value_weight, output_weight.T], axis=1
    )
    small = jnp.stack([router_weight, attn_gain, mlp_gain])
    if fsdp == 8:
        vec = jnp.zeros((8, width), BF16)
        vec = lax.dynamic_update_slice(vec, small, (0, me_f * depth))
        for mask in (1, 2, 4):
            vec = vec + swap(vec, "fsdp", mask)
    else:
        vec = lax.all_gather(small, "fsdp", axis=1, tiled=True)
        vec = jnp.concatenate([vec, jnp.zeros((5, width), BF16)], axis=0)
    vec = vec.astype(F32)
    attn_w = fsdp_gather(attn_piece)

    place = routed_index - me_t * span
    positions = jnp.arange(span, dtype=jnp.int32)
    onehot = (place[:, :, None] == positions[None, None, :]).astype(BF16)
    onehot_t = (place[:, None, :] == positions[None, :, None]).astype(BF16)
    blocks = routed_index // BLOCK
    bias = jnp.where(blocks[:, None, :] <= blocks[:, :, None], 0.0, NEG).astype(F32)
    order = jnp.stack([(me_t ^ m) * per + j for m in range(4) for j in range(per)])
    order_keep = jnp.concatenate([order[0:per], order[2 * per : 3 * per]])
    order_send = jnp.concatenate([order[per : 2 * per], order[3 * per :]])
    order_near = order[: 2 * per]
    order_far = order[2 * per :]

    def take(values):
        got = swap(pick_rows(values, onehot, order_send), "tensor", 1)
        keep = pick_rows(values, onehot, order_keep)
        far = swap(keep[rows:] + got[rows:], "tensor", 2)
        return keep, got, far

    row_shape = ((rows, width), BF16, "r")
    f32_shape = ((rows, width), F32, "r")
    gate_shape = ((rows, 128), F32, "r")
    vec_shape = ((8, width), F32, "w")

    def row_step(body, name, ins, outs):
        return row_call(body, name, ins, outs, rows, width)

    def r(*arrays):
        return [(a, "r") for a in arrays]

    tok = take(tokens)
    own_rows, normed, gate = row_step(
        first_norm_body, "first_norm", r(*tok) + [(vec, "w")], [row_shape, row_shape, gate_shape]
    )
    n0, n1, n2, n3 = gather_rows(normed)
    cot, mlp_grad = row_step(
        cot_body, "cot_rows", r(*take(cotangent), gate), [row_shape, row_shape]
    )
    g0, g1, g2, g3 = gather_rows(mlp_grad)

    qkv_far, ctx_far, p2, p3 = attn_fwd(n2, n3, attn_w, bias, order_far, local)
    attn_x = scatter_far(p2, p3)
    qkv_near, ctx_near, p0, p1 = attn_fwd(n0, n1, attn_w, bias, order_near, local)
    attn_c = swap(p1, "tensor", 1)
    attn, second = row_step(
        second_norm_body,
        "second_norm",
        r(own_rows, p0, attn_c, attn_x) + [(vec, "w")],
        [f32_shape, row_shape],
    )
    s0, s1, s2, s3 = gather_rows(second)

    act_far, ug_far, d2, d3, m2, m3 = mlp_both(s2, s3, g2, g3, up_down)
    second_x = scatter_far(d2, d3)
    act_near, ug_near, d0, d1, m0, m1 = mlp_both(s0, s1, g0, g1, up_down)
    second_c = swap(d1, "tensor", 1)
    attn_grad, hidden_grad, second_part = row_step(
        second_back_body,
        "second_back",
        r(own_rows, attn, cot, gate, d0, second_c, second_x) + [(vec, "w")],
        [row_shape, f32_shape, vec_shape],
    )
    a0, a1, a2, a3 = gather_rows(attn_grad)
    mlp_x = scatter_far(m2, m3)
    mlp_c = swap(m1, "tensor", 1)
    out_rows, gate_grad, router_part = row_step(
        out_body,
        "out_rows",
        r(own_rows, attn, cot, gate, m0, mlp_c, mlp_x),
        [row_shape, gate_shape, vec_shape],
    )
    mixed = place_rows(tokens, onehot_t, gather_rows(out_rows), order)

    shifts = (1, 3, 2, 0)
    if fsdp == 8:
        zi = me_f // 2
        info = jnp.stack([(zi + o) % 4 for o in shifts] + [me_f % 2])
        sends, keeps = grad_blocks(
            [
                ((s0, s1, s2, s3), (ug_near, ug_far)),
                ((g0, g1, g2, g3), (act_near, act_far)),
            ],
            info,
            2 * depth,
            up_weight.shape[1],
            4,
            "mlp_grads",
        )
        mlp_sum = fsdp_finish(sends, keeps, shifts)
    else:

        def dense(xs, ys):
            return t_mm(jnp.concatenate(xs, axis=0), jnp.concatenate(ys, axis=0))

        def reduced(x):
            return lax.psum_scatter(x, "fsdp", scatter_dimension=0, tiled=True)

        mlp_sum = jnp.concatenate(
            [
                reduced(dense((s0, s1, s2, s3), (ug_near, ug_far))),
                reduced(dense((g0, g1, g2, g3), (act_near, act_far))),
            ],
            axis=0,
        )

    dqkv_far, f2, f3 = attn_bwd(a2, a3, attn_w, qkv_far, bias, order_far, local)
    first_x = scatter_far(f2, f3)
    dqkv_near, f0, f1 = attn_bwd(a0, a1, attn_w, qkv_near, bias, order_near, local)
    first_c = swap(f1, "tensor", 1)
    half = rows // 2
    grad_rows, vec_part = pl.pallas_call(
        first_back_body,
        grid=(2,),
        in_specs=[
            pl.BlockSpec((half, width), lambda i: (i, 0)),
            pl.BlockSpec((half, width), lambda i: (i, 0)),
            pl.BlockSpec((half, 128), lambda i: (i, 0)),
        ]
        + [pl.BlockSpec((half, width), lambda i: (i, 0))] * 4
        + [pl.BlockSpec((8, width), lambda i: (0, 0))] * 3,
        out_specs=[
            pl.BlockSpec((half, width), lambda i: (i, 0)),
            pl.BlockSpec((8, width), lambda i: (0, 0)),
        ],
        out_shape=[shape((rows, width), BF16), shape((8, width), F32)],
        scratch_shapes=[pltpu.VMEM((8, width), F32)],
        compiler_params=PARAMS,
        cost_estimate=cost(30 * rows * width, 20 * rows * width),
        name="first_back",
    )(own_rows, cot, gate_grad, hidden_grad, f0, first_c, first_x, vec, router_part, second_part)
    token_grad = place_rows(cotangent, onehot_t, gather_rows(grad_rows), order)

    if fsdp == 8:
        sends, keeps = grad_blocks(
            [
                ((n0, n1, n2, n3), (dqkv_near, dqkv_far)),
                ((a0, a1, a2, a3), (ctx_near, ctx_far)),
            ],
            info,
            depth,
            4 * local,
            4,
            "attn_grads",
        )
        attn_sum = fsdp_finish(sends, keeps, shifts)
        vec_sum = vec_part
        for axis, mask in (("tensor", 1), ("tensor", 2), ("fsdp", 1)):
            vec_sum = vec_sum + swap(vec_sum, axis, mask)
        around = [lax.ppermute(vec_sum, "fsdp", z_perm(fsdp, 2, o)) for o in (1, 3, 2)]
        vec_sum = vec_sum + around[0] + around[1] + around[2]
    else:
        attn_sum = jnp.concatenate(
            [
                reduced(dense((n0, n1, n2, n3), (dqkv_near, dqkv_far))),
                reduced(dense((a0, a1, a2, a3), (ctx_near, ctx_far))),
            ],
            axis=1,
        )
        vec_sum = lax.psum(vec_part, ("fsdp", "tensor"))
    vec_own = lax.dynamic_slice(vec_sum, (0, me_f * depth), (3, depth))

    return (
        mixed,
        token_grad,
        attn_sum[:, 0:local],
        attn_sum[:, local : 2 * local],
        attn_sum[:, 2 * local : 3 * local],
        attn_sum[:, 3 * local :].T,
        mlp_sum[0:depth],
        mlp_sum[depth:].T,
        vec_own[0],
        vec_own[1],
        vec_own[2],
    )


def solution(mesh):
    in_specs = (
        P("fsdp", "tensor", None),
        P("fsdp", "tensor", None),
        P("fsdp", None),
        P("fsdp", "tensor"),
        P("fsdp", "tensor"),
        P("fsdp", "tensor"),
        P("tensor", "fsdp"),
        P("fsdp", "tensor"),
        P("tensor", "fsdp"),
        P("fsdp"),
        P("fsdp"),
        P("fsdp"),
    )
    out_specs = (
        P("fsdp", "tensor", None),
        P("fsdp", "tensor", None),
        P("fsdp", "tensor"),
        P("fsdp", "tensor"),
        P("fsdp", "tensor"),
        P("tensor", "fsdp"),
        P("fsdp", "tensor"),
        P("tensor", "fsdp"),
        P("fsdp"),
        P("fsdp"),
        P("fsdp"),
    )
    return jax.shard_map(shards, mesh=mesh, in_specs=in_specs, out_specs=out_specs, check_vma=False)
```

```python
import functools

import jax
import jax.numpy as jnp
from jax import lax
from jax.experimental import pallas as pl
from jax.experimental.pallas import tpu as pltpu
from jax.sharding import PartitionSpec as P

HEAD_DIM = 64
BLOCK = 256
EPS = 1e-06
NEG = -1e30
F32 = jnp.float32
BF16 = jnp.bfloat16
GELU_C = 0.7978845608028654
GELU_A = 0.044715

VMEM_SPEC = pl.BlockSpec(memory_space=pltpu.VMEM)
SMEM_SPEC = pl.BlockSpec(memory_space=pltpu.SMEM)
HBM_SPEC = pl.BlockSpec(memory_space=pltpu.HBM)


def mm(a, b):
    return jnp.dot(a, b, preferred_element_type=F32)


def mm_t(a, b):
    return lax.dot_general(a, b, (((1,), (1,)), ((), ())), preferred_element_type=F32)


def t_mm(a, b):
    return lax.dot_general(a, b, (((0,), (0,)), ((), ())), preferred_element_type=F32)


def shape(dims, dtype):
    return jax.ShapeDtypeStruct(dims, dtype)


def after(value, *others):
    return lax.optimization_barrier((value,) + others)[0]


COST = pl.CostEstimate(flops=1, bytes_accessed=1, transcendentals=0)


def in_hbm(value):
    return pltpu.with_memory_space_constraint(value, pltpu.HBM)


def params(mib):
    return pltpu.CompilerParams(vmem_limit_bytes=max(mib, 48) << 20)


def tiles(total, width, step):
    def body(j, carry):
        step(pl.ds(pl.multiple_of(j * width, width), width), j)
        return carry

    lax.fori_loop(0, total // width, body, 0)


def pick_kernel(order, onehot, values, out, buf, sems):
    routed = onehot.shape[1]
    count = buf.shape[0]
    copies = [
        pltpu.make_async_copy(values.at[order[i]], buf.at[i], sems.at[i]) for i in range(count)
    ]
    for copy in copies:
        copy.start()
    for i, copy in enumerate(copies):
        copy.wait()
        out[i * routed : (i + 1) * routed, :] = mm(onehot[order[i]], buf[i]).astype(BF16)


def pick_rows(values, onehot, order):
    count = order.shape[0]
    _, routed, span = onehot.shape
    width = values.shape[2]
    return pl.pallas_call(
        pick_kernel,
        in_specs=[SMEM_SPEC, VMEM_SPEC, HBM_SPEC],
        out_specs=VMEM_SPEC,
        out_shape=shape((count * routed, width), BF16),
        scratch_shapes=[
            pltpu.VMEM((count, span, width), BF16),
            pltpu.SemaphoreType.DMA((count,)),
        ],
        compiler_params=params(8),
        cost_estimate=COST,
        name="pick_rows",
    )(order, onehot, in_hbm(values))


def place_kernel(order, onehot_t, *refs, blocks):
    out, buf, sums, loads, stores = refs[-5:]
    row_refs = refs[:blocks]
    base = refs[blocks]
    count = buf.shape[0]
    routed = onehot_t.shape[2]
    found = [(ref, at) for ref in row_refs for at in range(0, ref.shape[0], routed)]
    reads = [
        pltpu.make_async_copy(base.at[order[i]], buf.at[i], loads.at[i]) for i in range(count)
    ]
    writes = [
        pltpu.make_async_copy(sums.at[i], out.at[order[i]], stores.at[i]) for i in range(count)
    ]
    for copy in reads:
        copy.start()
    for i in range(count):
        ref, at = found[i]
        rows = ref[at : at + routed, :]
        hot = onehot_t[order[i]]
        keep = 1.0 - jnp.sum(hot.astype(F32), axis=1, keepdims=True)
        reads[i].wait()
        sums[i] = buf[i] * keep.astype(BF16) + mm(hot, rows).astype(BF16)
        writes[i].start()
    for copy in writes:
        copy.wait()


def place_rows(base, onehot_t, rows, order, into=None):
    _, span, width = base.shape
    count = order.shape[0]
    extra = [] if into is None else [into]
    return pl.pallas_call(
        functools.partial(place_kernel, blocks=len(rows)),
        in_specs=[SMEM_SPEC, VMEM_SPEC]
        + [VMEM_SPEC] * len(rows)
        + [HBM_SPEC] * (1 + len(extra)),
        out_specs=HBM_SPEC,
        out_shape=shape(base.shape, BF16),
        scratch_shapes=[
            pltpu.VMEM((count, span, width), BF16),
            pltpu.VMEM((count, span, width), BF16),
            pltpu.SemaphoreType.DMA((count,)),
            pltpu.SemaphoreType.DMA((count,)),
        ],
        input_output_aliases={3 + len(rows): 0} if extra else {},
        compiler_params=params(8),
        cost_estimate=COST,
        name="place_rows",
    )(order, onehot_t, *rows, in_hbm(base), *extra)


def row_call(body, name, inputs, outputs, rows, width, steps=2):
    block = rows // steps
    in_specs = []
    for array, kind in inputs:
        if kind == "w":
            in_specs.append(pl.BlockSpec(array.shape, lambda i: (0, 0)))
        elif kind == "h":
            in_specs.append(pl.BlockSpec((block, array.shape[1]), lambda i: (0, 0)))
        else:
            in_specs.append(pl.BlockSpec((block, array.shape[1]), lambda i: (i, 0)))
    out_specs = []
    out_shapes = []
    for dims, dtype, kind in outputs:
        out_shapes.append(shape(dims, dtype))
        if kind == "w":
            out_specs.append(pl.BlockSpec(dims, lambda i: (0, 0)))
        else:
            out_specs.append(pl.BlockSpec((block, dims[1]), lambda i: (i, 0)))
    return pl.pallas_call(
        body,
        grid=(steps,),
        in_specs=in_specs,
        out_specs=out_specs,
        out_shape=out_shapes,
        compiler_params=params(10),
        cost_estimate=COST,
        name=name,
    )(*[array for array, _ in inputs])


def row_mean(x):
    return jnp.mean(x, axis=-1, keepdims=True)


def total3(a, b0, b1, c):
    b = jnp.where(pl.program_id(0) == 0, b0[...].astype(F32), b1[...].astype(F32))
    return a[...].astype(F32) + b + c[...].astype(F32)


def lanes(col):
    return jnp.broadcast_to(col, (col.shape[0], 128))


def fold(x):
    return jnp.sum(x.reshape(-1, 8, x.shape[1]), axis=0)


def accumulate(ref, value):
    @pl.when(pl.program_id(0) == 0)
    def _():
        ref[...] = value

    @pl.when(pl.program_id(0) > 0)
    def _():
        ref[...] += value


def first_norm_body(a, b0, b1, c, vec, rows_out, normed_out, gate_out):
    rows = total3(a, b0, b1, c)
    rows_out[...] = rows.astype(BF16)
    logit = jnp.sum(rows * vec[0:1, :], axis=-1, keepdims=True)
    gate_out[...] = lanes(jax.nn.sigmoid(logit))
    scale = lax.rsqrt(row_mean(rows * rows) + EPS)
    normed_out[...] = (rows * scale * vec[1:2, :]).astype(BF16)


def cot_body(a, b0, b1, c, gate, cot_out, grad_out):
    cot = total3(a, b0, b1, c)
    cot_out[...] = cot.astype(BF16)
    grad_out[...] = (cot * gate[:, 0:1]).astype(BF16)


def second_norm_body(rows, a, b0, b1, c, vec, attn_out, normed_out):
    attn = total3(a, b0, b1, c)
    attn_out[...] = attn
    hidden = rows[...].astype(F32) + attn
    scale = lax.rsqrt(row_mean(hidden * hidden) + EPS)
    normed_out[...] = (hidden * scale * vec[2:3, :]).astype(BF16)


def second_back_body(rows, attn, cot, gate, a, b0, b1, c, vec, grad_out, hidden_out, gain_out):
    second_grad = total3(a, b0, b1, c)
    hidden = rows[...].astype(F32) + attn[...]
    scale = lax.rsqrt(row_mean(hidden * hidden) + EPS)
    normal = hidden * scale
    grad = second_grad * vec[2:3, :]
    hidden_grad = scale * (grad - normal * row_mean(grad * normal))
    hidden_out[...] = hidden_grad
    grad_out[...] = (cot[...].astype(F32) * gate[:, 0:1] + hidden_grad).astype(BF16)
    accumulate(gain_out, fold(second_grad * normal))


def out_body(rows, attn, cot, gate, a, b0, b1, c, rows_out, gate_grad_out, router_out):
    branch = attn[...] + total3(a, b0, b1, c)
    x = rows[...].astype(F32)
    g = gate[:, 0:1]
    rows_out[...] = (x + g * branch).astype(BF16)
    gate_grad = jnp.sum(cot[...].astype(F32) * branch, axis=-1, keepdims=True) * g * (1.0 - g)
    gate_grad_out[...] = lanes(gate_grad)
    accumulate(router_out, fold(x * gate_grad))


def first_back_body(
    rows, cot, gate_grad, hidden_grad, a, b0, b1, c, vec, router_part, second_part, grad_out, vec_out, acc
):
    first_grad = total3(a, b0, b1, c)
    x = rows[...].astype(F32)
    scale = lax.rsqrt(row_mean(x * x) + EPS)
    normal = x * scale
    grad = first_grad * vec[1:2, :]
    norm_grad = scale * (grad - normal * row_mean(grad * normal))
    grad_out[...] = (
        cot[...].astype(F32) + gate_grad[:, 0:1] * vec[0:1, :] + hidden_grad[...] + norm_grad
    ).astype(BF16)
    accumulate(acc, fold(first_grad * normal))

    @pl.when(pl.program_id(0) == pl.num_programs(0) - 1)
    def _():
        vec_out[0:1, :] = jnp.sum(router_part[...], axis=0, keepdims=True)
        vec_out[1:2, :] = jnp.sum(acc[...], axis=0, keepdims=True)
        vec_out[2:3, :] = jnp.sum(second_part[...], axis=0, keepdims=True)
        vec_out[3:8, :] = jnp.zeros_like(vec_out[3:8, :])


def pack_mlp_kernel(up, down, out, buf, sems):
    depth = up.shape[0]
    copies = [
        pltpu.make_async_copy(up, out.at[0:depth, :], sems.at[0]),
        pltpu.make_async_copy(down, buf, sems.at[1]),
    ]
    for copy in copies:
        copy.start()
    copies[1].wait()
    out[depth : 2 * depth, :] = buf[...].T
    copies[0].wait()


def pack_attn_kernel(q, k, v, o, small, out, buf, sems):
    depth, local = q.shape
    copies = [
        pltpu.make_async_copy(
            x, out.at[0:depth, i * local : (i + 1) * local], sems.at[i]
        )
        for i, x in enumerate((q, k, v))
    ]
    copies.append(pltpu.make_async_copy(o, buf, sems.at[3]))
    for copy in copies:
        copy.start()
    out[depth:, :] = jnp.zeros_like(out[depth:, :])
    out[depth:, 0:depth] = small[...]
    copies[3].wait()
    out[0:depth, 3 * local : 4 * local] = buf[...].T
    for copy in copies[:3]:
        copy.wait()


def pack_mlp(up, down):
    return pl.pallas_call(
        pack_mlp_kernel,
        in_specs=[HBM_SPEC] * 2,
        out_specs=VMEM_SPEC,
        out_shape=shape((2 * up.shape[0], up.shape[1]), BF16),
        scratch_shapes=[pltpu.VMEM(down.shape, BF16), pltpu.SemaphoreType.DMA((2,))],
        compiler_params=params(4),
        cost_estimate=COST,
        name="pack_mlp",
    )(in_hbm(up), in_hbm(down))


def pack_attn(q, k, v, o, small):
    depth, local = q.shape
    return pl.pallas_call(
        pack_attn_kernel,
        in_specs=[HBM_SPEC] * 4 + [VMEM_SPEC],
        out_specs=VMEM_SPEC,
        out_shape=shape((depth + 16, 4 * local), BF16),
        scratch_shapes=[pltpu.VMEM(o.shape, BF16), pltpu.SemaphoreType.DMA((4,))],
        compiler_params=params(4),
        cost_estimate=COST,
        name="pack_attn",
    )(in_hbm(q), in_hbm(k), in_hbm(v), in_hbm(o), small)


def finish_mlp_kernel(total, up_out, down_out):
    depth = up_out.shape[0]
    total = total[...].astype(F32)
    up_out[...] = total[0:depth]
    down_out[...] = total[depth:].T


def finish_attn_kernel(own, got, p1, p2, p3, q_out, k_out, v_out, o_out):
    local = q_out.shape[1]
    total = own[...] + got[...].astype(F32)
    for part in (p1, p2, p3):
        total = total + part[...].astype(F32)
    q_out[...] = total[:, 0:local]
    k_out[...] = total[:, local : 2 * local]
    v_out[...] = total[:, 2 * local : 3 * local]
    o_out[...] = total[:, 3 * local :].T


def finish(body, name, dims, *arrays):
    return pl.pallas_call(
        body,
        in_specs=[VMEM_SPEC] * len(arrays),
        out_specs=[VMEM_SPEC] * len(dims),
        out_shape=[shape(d, F32) for d in dims],
        compiler_params=params(8),
        cost_estimate=COST,
        name=name,
    )(*arrays)


def join_kernel(places, *refs):
    *pieces, out, vec = refs
    depth = out.shape[0] // (len(pieces) - 1)
    vec[...] = jnp.zeros_like(vec)
    for number, piece in enumerate(pieces):
        if number > 0:
            out[(number - 1) * depth : number * depth, :] = piece[0:depth, :]
        place = places[number] * 2 + places[4]
        lanes_at = pl.ds(pl.multiple_of(place * depth, depth), depth)
        vec[:, lanes_at] = piece[depth : depth + 16, 0:depth]


def join(pieces, places, depth):
    width = pieces[0].shape[1]
    return pl.pallas_call(
        join_kernel,
        in_specs=[SMEM_SPEC] + [VMEM_SPEC] * len(pieces),
        out_specs=[VMEM_SPEC] * 2,
        out_shape=[
            shape((depth * (len(pieces) - 1), width), BF16),
            shape((16, width), BF16),
        ],
        compiler_params=params(6),
        cost_estimate=COST,
        name="join",
    )(places, *pieces)


def assemble_kernel(places, near_own, near, far_own, far, out):
    depth = 128
    for side, halves in enumerate(((near_own, near), (far_own, far))):
        for number in range(4):
            ref = halves[min(number, 1)]
            row = max(number - 1, 0) * depth
            place = places[number] * 2 + (places[4] ^ side)
            at = pl.multiple_of(place * depth, depth)
            out[pl.ds(at, depth), :] = ref[row : row + depth, :]


def assemble(near_own, near, far_own, far, places):
    rows, width = near.shape
    return pl.pallas_call(
        assemble_kernel,
        in_specs=[SMEM_SPEC] + [VMEM_SPEC] * 4,
        out_specs=VMEM_SPEC,
        out_shape=shape((rows * 8 // 3, width), BF16),
        compiler_params=params(6),
        cost_estimate=COST,
        name="assemble",
    )(places, near_own, near, far_own, far)


def head_masks(width):
    lane = lax.broadcasted_iota(jnp.int32, (1, width), 1) // HEAD_DIM
    return [(lane == h).astype(BF16) for h in range(width // HEAD_DIM)]


def spread(x, masks):
    return jnp.concatenate([x * mask for mask in masks], axis=0)


def side_by_side(x, count):
    rows = x.shape[0] // count
    return jnp.concatenate([x[h * rows : (h + 1) * rows] for h in range(count)], axis=1)


def seq_probs(q4, k, bias, count):
    scores = mm_t(q4, k) * (HEAD_DIM**-0.5)
    scores = scores + jnp.concatenate([bias] * count, axis=0)
    top = jnp.max(scores, axis=-1, keepdims=True)
    weight = jnp.exp(scores - top)
    return weight / jnp.sum(weight, axis=-1, keepdims=True)


def fill(ref, parts):
    at = 0
    for part in parts:
        ref[at : at + part.shape[0], :] = part[...]
        at += part.shape[0]


def attn_fwd_kernel(order, xa, *refs, parts):
    w, bias, qkv, ctx, pa, pb, xb = refs[parts:]
    fill(xb, refs[:parts])
    half = xa.shape[0]
    local = ctx.shape[1]
    routed = bias.shape[1]
    heads = local // HEAD_DIM
    masks = head_masks(local)

    def project(cols, j):
        qkv[0:half, cols] = mm(xa[...], w[:, cols]).astype(BF16)
        qkv[half : 2 * half, cols] = mm(xb[...], w[:, cols]).astype(BF16)

    tiles(3 * local, local, project)

    def seq(rows, s):
        q = qkv[rows, 0:local]
        k = qkv[rows, local : 2 * local]
        v = qkv[rows, 2 * local : 3 * local]
        probs = seq_probs(spread(q, masks), k, bias[order[s]], heads).astype(BF16)
        ctx[rows, :] = mm(side_by_side(probs, heads), spread(v, masks)).astype(BF16)

    tiles(2 * half, routed, seq)

    def emit(cols, j):
        wo = w[cols, 3 * local : 4 * local]
        pa[:, cols] = mm_t(ctx[0:half, :], wo).astype(BF16)
        pb[:, cols] = mm_t(ctx[half : 2 * half, :], wo).astype(BF16)

    tiles(pa.shape[1], 256, emit)


def attn_fwd(xa, xb, w, bias, order, local):
    rows, width = xa.shape
    return pl.pallas_call(
        functools.partial(attn_fwd_kernel, parts=len(xb)),
        in_specs=[SMEM_SPEC] + [VMEM_SPEC] * (3 + len(xb)),
        out_specs=[VMEM_SPEC] * 4,
        out_shape=[
            shape((2 * rows, 3 * local), BF16),
            shape((2 * rows, local), BF16),
            shape((rows, width), BF16),
            shape((rows, width), BF16),
        ],
        scratch_shapes=[pltpu.VMEM((rows, width), BF16)],
        compiler_params=params(12),
        cost_estimate=COST,
        name="attn_fwd",
    )(order, xa, *xb, w, bias)


def attn_bwd_kernel(order, ga, *refs, parts):
    w, qkv, bias, dqkv, fa, fb, cg, gb = refs[parts:]
    fill(gb, refs[:parts])
    half = ga.shape[0]
    local = cg.shape[1]
    routed = bias.shape[1]
    heads = local // HEAD_DIM
    masks = head_masks(local)
    wo = w[:, 3 * local : 4 * local]
    cg[0:half, :] = mm(ga[...], wo).astype(BF16)
    cg[half : 2 * half, :] = mm(gb[...], wo).astype(BF16)

    def seq(rows, s):
        q4 = spread(qkv[rows, 0:local], masks)
        k = qkv[rows, local : 2 * local]
        v = qkv[rows, 2 * local : 3 * local]
        exact = seq_probs(q4, k, bias[order[s]], heads)
        c4 = spread(cg[rows, :], masks)
        prob_grad = mm_t(c4, v)
        dqkv[rows, 2 * local : 3 * local] = t_mm(exact.astype(BF16), c4).astype(BF16)
        inner = jnp.sum(exact * prob_grad, axis=-1, keepdims=True)
        score_grad = (exact * (prob_grad - inner)).astype(BF16)
        scale = HEAD_DIM**-0.5
        dq = mm(side_by_side(score_grad, heads), spread(k, masks)) * scale
        dqkv[rows, 0:local] = dq.astype(BF16)
        dqkv[rows, local : 2 * local] = (t_mm(score_grad, q4) * scale).astype(BF16)

    tiles(2 * half, routed, seq)

    def emit(cols, j):
        wj = w[cols, 0 : 3 * local]
        fa[:, cols] = mm_t(dqkv[0:half, :], wj).astype(BF16)
        fb[:, cols] = mm_t(dqkv[half : 2 * half, :], wj).astype(BF16)

    tiles(fa.shape[1], 256, emit)


def attn_bwd(ga, gb, w, qkv, bias, order, local):
    rows, width = ga.shape
    return pl.pallas_call(
        functools.partial(attn_bwd_kernel, parts=len(gb)),
        in_specs=[SMEM_SPEC] + [VMEM_SPEC] * (4 + len(gb)),
        out_specs=[VMEM_SPEC] * 3,
        out_shape=[
            shape((2 * rows, 3 * local), BF16),
            shape((rows, width), BF16),
            shape((rows, width), BF16),
        ],
        scratch_shapes=[pltpu.VMEM((2 * rows, local), BF16), pltpu.VMEM((rows, width), BF16)],
        compiler_params=params(12),
        cost_estimate=COST,
        name="attn_bwd",
    )(order, ga, *gb, w, qkv, bias)


def mlp_kernel(na, ga, *refs, parts):
    w, act, ug, da, db, ma, mb, nb, gb = refs[2 * parts :]
    fill(nb, refs[:parts])
    fill(gb, refs[parts : 2 * parts])
    rows, width = na.shape
    part, both, ff = w.shape
    depth = both // 2

    def up(cols, j):
        wu = w[:, 0:depth, cols].reshape(width, -1)
        wd = w[:, depth:both, cols].reshape(width, -1)
        for n, g, at in ((na, ga, 0), (nb, gb, rows)):
            x = mm(n[...], wu)
            inner = jnp.tanh(GELU_C * (x + GELU_A * (x * x * x)))
            half_in = 0.5 * (1.0 + inner)
            act[at : at + rows, cols] = (x * half_in).astype(BF16)
            slope = half_in + (0.5 * GELU_C) * x * (1.0 - inner * inner) * (
                1.0 + (3.0 * GELU_A) * (x * x)
            )
            ug[at : at + rows, cols] = (mm(g[...], wd) * slope).astype(BF16)

    tiles(ff, 256, up)
    group = part * 256 // width

    def back(cols, j):
        wu = w[pl.ds(j * group, group), 0:depth, :].reshape(256, -1)
        da[:, cols] = mm_t(ug[0:rows, :], wu).astype(BF16)
        db[:, cols] = mm_t(ug[rows : 2 * rows, :], wu).astype(BF16)

    tiles(width, 256, back)

    def down(cols, j):
        wd = w[pl.ds(j * group, group), depth:both, :].reshape(256, -1)
        ma[:, cols] = mm_t(act[0:rows, :], wd).astype(BF16)
        mb[:, cols] = mm_t(act[rows : 2 * rows, :], wd).astype(BF16)

    tiles(width, 256, down)


def mlp_both(na, nb, ga, gb, w):
    rows, width = na.shape
    ff = w.shape[2]
    return pl.pallas_call(
        functools.partial(mlp_kernel, parts=len(nb)),
        in_specs=[VMEM_SPEC] * (3 + 2 * len(nb)),
        out_specs=[VMEM_SPEC] * 6,
        out_shape=[shape((2 * rows, ff), BF16)] * 2 + [shape((rows, width), BF16)] * 4,
        scratch_shapes=[pltpu.VMEM((rows, width), BF16)] * 2,
        compiler_params=params(16),
        cost_estimate=COST,
        name="mlp",
    )(na, ga, *nb, *gb, w)


def turn(xt, pieces, cols):
    at = 0
    for piece in pieces:
        size = piece.shape[0]
        xt[:, at : at + size] = piece[:, cols].T
        at += size


def mlp_grads_kernel(*refs, depth, pieces):
    normed, grads = refs[:pieces], refs[pieces : 2 * pieces]
    un, uf, an, af, out, xt = refs[2 * pieces :]
    half = un.shape[0]
    width = normed[0].shape[1]
    group = 256 // depth

    def columns(cols, z):
        for side, (xs, near, far) in enumerate(((normed, un, uf), (grads, an, af))):
            turn(xt, xs, cols)

            def block(ncols, j, near=near, far=far, side=side):
                total = mm(xt[:, 0:half], near[:, ncols])
                total = total + mm(xt[:, half:], far[:, ncols])
                for i in range(group):
                    at = pl.multiple_of((z * group + i) * 2 * depth + side * depth, depth)
                    part = total[i * depth : (i + 1) * depth]
                    out[pl.ds(at, depth), ncols] = part.astype(BF16)

            tiles(near.shape[1], 256, block)

    tiles(width, 256, columns)


def mlp_grads(normed, grads, ug, act, depth):
    width = normed[0].shape[1]
    rows, ff = ug[0].shape
    return pl.pallas_call(
        functools.partial(mlp_grads_kernel, depth=depth, pieces=len(normed)),
        in_specs=[VMEM_SPEC] * (2 * len(normed) + 4),
        out_specs=VMEM_SPEC,
        out_shape=shape((2 * width, ff), BF16),
        scratch_shapes=[pltpu.VMEM((256, 2 * rows), BF16)],
        compiler_params=params(20),
        cost_estimate=COST,
        name="mlp_grads",
    )(*normed, *grads, *ug, *act)


def attn_grads_kernel(info, *refs, pieces):
    normed, grads = refs[:pieces], refs[pieces : 2 * pieces]
    dn, df, cn, cf, first, others, *keeps, xt = refs[2 * pieces :]
    half = dn.shape[0]
    local = cn.shape[1]
    depth = first.shape[0]
    count = len(keeps)
    low = info[count] == 0
    for o in range(count):
        cols = pl.ds(pl.multiple_of(info[o] * 256, 256), 256)
        send, row = (first, 0) if o == 0 else (others, (o - 1) * depth)
        for lane, wide, xs, near, far in (
            (0, 3 * local, normed, dn, df),
            (3 * local, local, grads, cn, cf),
        ):
            turn(xt, xs, cols)

            def block(ncols, j, near=near, far=far, lane=lane, send=send, row=row, o=o):
                total = mm(xt[:, 0:half], near[:, ncols])
                total = total + mm(xt[:, half:], far[:, ncols])
                one, two = total[0:depth], total[depth : 2 * depth]
                dst = pl.ds(pl.multiple_of(j * 256, 256) + lane, 256)
                send[row : row + depth, dst] = jnp.where(low, two, one).astype(BF16)
                keeps[o][:, dst] = jnp.where(low, one, two)

            tiles(wide, 256, block)


def attn_grads(normed, grads, dqkv, ctx, info, depth):
    rows, local = ctx[0].shape
    count = info.shape[0] - 1
    first, others, *keeps = pl.pallas_call(
        functools.partial(attn_grads_kernel, pieces=len(normed)),
        in_specs=[SMEM_SPEC] + [VMEM_SPEC] * (2 * len(normed) + 4),
        out_specs=[VMEM_SPEC] * (2 + count),
        out_shape=[
            shape((depth, 4 * local), BF16),
            shape(((count - 1) * depth, 4 * local), BF16),
        ]
        + [shape((depth, 4 * local), F32)] * count,
        scratch_shapes=[pltpu.VMEM((256, 2 * rows), BF16)],
        compiler_params=params(14),
        cost_estimate=COST,
        name="attn_grads",
    )(info, *normed, *grads, *dqkv, *ctx)
    return first, others, keeps


def swap(x, axis, mask):
    size = lax.axis_size(axis)
    return lax.ppermute(x, axis, [(i, i ^ mask) for i in range(size)])


def halves(x):
    step = x.shape[0] // 2
    return x[:step], x[step:]


def pair_swap(x):
    return tuple(swap(h, "tensor", 1) for h in halves(x))


def pair_sum(near, diag):
    return jnp.concatenate(
        [
            (n.astype(F32) + g.astype(F32)).astype(BF16)
            for n, g in zip(halves(near), pair_swap(diag))
        ],
        axis=0,
    )


def z_perm(size, shift):
    places = size // 2
    return [((f // 2 + shift) % places * 2 + f % 2, f) for f in range(size)]


def z_move(x, shift):
    return lax.ppermute(x, "fsdp", z_perm(lax.axis_size("fsdp"), shift))


SHIFTS = (2, 1, 3)


def shards(
    tokens,
    cotangent,
    routed_index,
    query_weight,
    key_weight,
    value_weight,
    output_weight,
    up_weight,
    down_weight,
    router_weight,
    attn_gain,
    mlp_gain,
):
    fsdp = lax.axis_size("fsdp")
    grid = fsdp == 8
    me_f = lax.axis_index("fsdp")
    me_t = lax.axis_index("tensor")
    seqs, span, width = tokens.shape
    routed = routed_index.shape[1]
    per = seqs // lax.axis_size("tensor")
    local = query_weight.shape[1]
    depth = query_weight.shape[0]
    ff = up_weight.shape[1]
    rows = per * routed

    place = routed_index - me_t * span
    positions = jnp.arange(span, dtype=jnp.int32)
    onehot = (place[:, :, None] == positions[None, None, :]).astype(BF16)
    order = jnp.stack([(me_t ^ m) * per + j for m in range(4) for j in range(per)])
    order_keep = jnp.concatenate([order[0:per], order[2 * per : 3 * per]])
    order_send = jnp.concatenate([order[per : 2 * per], order[3 * per :]])
    order_near = order[: 2 * per]
    order_far = order[2 * per :]

    row_shape = ((rows, width), BF16, "r")
    f32_shape = ((rows, width), F32, "r")
    gate_shape = ((rows, 128), F32, "r")
    vec_shape = ((8, width), F32, "w")

    def row_step(body, name, ins, outs):
        return row_call(body, name, ins, outs, rows, width)

    def r(*arrays):
        found = []
        for a in arrays:
            found += [(h, "h") for h in a] if isinstance(a, tuple) else [(a, "r")]
        return found

    zi = me_f // 2
    yi = me_f % 2

    small = jnp.stack([router_weight, attn_gain, mlp_gain])
    if grid:
        small = jnp.concatenate([small, jnp.zeros((13, depth), BF16)], axis=0)
        attn_piece = pack_attn(query_weight, key_weight, value_weight, output_weight, small)
        z_pieces = [z_move(attn_piece, o) for o in SHIFTS]
        far_own = swap(attn_piece, "fsdp", 1)
        z_at = jnp.stack([zi] + [(zi + o) % (fsdp // 2) for o in SHIFTS] + [yi])
    else:
        attn_piece = jnp.concatenate(
            [query_weight, key_weight, value_weight, output_weight.T], axis=1
        )
        z_pieces = []
        vec = lax.all_gather(small, "fsdp", axis=1, tiled=True)
        vec = jnp.concatenate([vec, jnp.zeros((5, width), BF16)], axis=0).astype(F32)
    tok_send = pick_rows(tokens, onehot, after(order_send, attn_piece))
    tok_got = pair_swap(tok_send)
    tok_keep = pick_rows(tokens, onehot, after(order_keep, tok_send))
    tok_sum = tok_keep[rows:] + tok_got[1]
    tok_far = [swap(h, "tensor", 2) for h in halves(tok_sum)]
    cot_send = pick_rows(cotangent, onehot, after(order_send, tok_sum))
    cot_got = pair_swap(cot_send)
    cot_keep = pick_rows(cotangent, onehot, after(order_keep, cot_send))
    cot_sum = cot_keep[rows:] + cot_got[1]
    cot_far = [swap(h, "tensor", 2) for h in halves(cot_sum)]
    if grid:
        mlp_piece = pack_mlp(up_weight, after(down_weight, cot_keep))
        gated = [after(z, mlp_piece, *tok_far, *cot_far) for z in z_pieces]
        near_w, vec_near = join([attn_piece] + gated, z_at, depth)
        vec = vec_near + swap(vec_near, "fsdp", 1)
        far_w = swap(after(near_w, vec), "fsdp", 1)
        vec = vec[0:8].astype(F32)
        mlp_piece = after(mlp_piece, near_w)
    else:
        mlp_piece = jnp.concatenate([up_weight, down_weight.T], axis=0)
    up_down = lax.all_gather(mlp_piece, "fsdp", axis=0, tiled=True)
    up_down = up_down.reshape(fsdp, 2 * depth, ff)

    def with_halves(body):
        def whole(keep, got, far0, far1, *rest):
            far = jnp.where(pl.program_id(0) == 0, far0[...], far1[...])
            return body(keep, got, got, far, *rest)

        return whole

    own_rows, n0, gate = row_step(
        with_halves(first_norm_body),
        "first_norm",
        [(tok_keep, "r"), (tok_got[0], "r")] + r(tuple(tok_far)) + [(vec, "w")],
        [row_shape, row_shape, gate_shape],
    )
    n2 = swap(n0, "tensor", 2)
    n1 = swap(n0, "tensor", 1)
    cot, g0 = row_step(
        with_halves(cot_body),
        "cot_rows",
        [(cot_keep, "r"), (cot_got[0], "r")] + r(tuple(cot_far)) + [(after(gate, n0), "r")],
        [row_shape, row_shape],
    )
    g2 = swap(after(g0, n2), "tensor", 2)
    g1 = swap(g0, "tensor", 1)
    blocks = after(routed_index, g0) // BLOCK
    bias = jnp.where(blocks[:, None, :] <= blocks[:, :, None], 0.0, NEG).astype(F32)
    if grid:
        attn_w = assemble(attn_piece, after(near_w, g0), far_own, far_w, z_at)
    else:
        attn_w = lax.all_gather(attn_piece, "fsdp", axis=0, tiled=True)
    n3 = pair_swap(after(n2, attn_w))

    qkv_far, ctx_far, p2, p3 = attn_fwd(n2, n3, attn_w, bias, order_far, local)
    attn_sum = pair_sum(p2, p3)
    attn_x = swap(attn_sum, "tensor", 2)
    qkv_near, ctx_near, p0, p1 = attn_fwd(
        after(n0, attn_sum), (n1,), attn_w, bias, order_near, local
    )
    attn_c = pair_swap(p1)
    attn, s0 = row_step(
        second_norm_body,
        "second_norm",
        r(own_rows, p0, attn_c, attn_x) + [(vec, "w")],
        [f32_shape, row_shape],
    )
    s2 = swap(s0, "tensor", 2)
    s1 = swap(s0, "tensor", 1)
    s3 = pair_swap(s2)
    g3 = pair_swap(after(g2, s0))

    act_far, ug_far, d2, d3, m2, m3 = mlp_both(s2, s3, g2, g3, up_down)
    second_sum = pair_sum(d2, d3)
    second_x = swap(second_sum, "tensor", 2)
    act_near, ug_near, d0, d1, m0, m1 = mlp_both(
        after(s0, second_sum), (s1,), g0, (g1,), up_down
    )
    second_c = pair_swap(d1)

    attn_grad, hidden_grad, second_part = row_step(
        second_back_body,
        "second_back",
        r(own_rows, attn, cot, gate, d0, second_c, second_x) + [(vec, "w")],
        [row_shape, f32_shape, vec_shape],
    )
    a0 = attn_grad
    a2 = swap(a0, "tensor", 2)
    a1 = swap(a0, "tensor", 1)
    mlp_all = mlp_grads(
        (after(s0, a0), s1, s2, *s3),
        (g0, g1, g2, *g3),
        (ug_near, ug_far),
        (act_near, act_far),
        depth,
    )
    a2 = after(a2, mlp_all)
    mlp_total = lax.psum_scatter(after(mlp_all, a2), "fsdp", scatter_dimension=0, tiled=True)
    a3 = pair_swap(a2)
    mlp_c = pair_swap(after(m1, mlp_all))
    mlp_sum = pair_sum(m2, after(m3, mlp_all))
    mlp_x = swap(after(mlp_sum, a2), "tensor", 2)

    def to_z(keep, got, shift):
        return z_move((keep + got.astype(F32)).astype(BF16), 4 - shift)

    dqkv_far, f2, f3 = attn_bwd(a2, a3, attn_w, qkv_far, bias, order_far, local)
    first_sum = pair_sum(f2, f3)
    first_x = swap(first_sum, "tensor", 2)
    dqkv_near, f0, f1 = attn_bwd(
        after(a0, first_sum), (a1,), attn_w, qkv_near, bias, order_near, local
    )
    first_c = pair_swap(f1)
    out_rows, gate_grad, router_part = row_step(
        out_body,
        "out_rows",
        r(own_rows, attn, cot, gate, m0, mlp_c, after(mlp_x, f1)),
        [row_shape, gate_shape, vec_shape],
    )
    o2 = swap(out_rows, "tensor", 2)
    o1 = swap(out_rows, "tensor", 1)

    attn_args = (
        (n0, n1, n2, *n3),
        (a0, a1, a2, *a3),
        (dqkv_near, dqkv_far),
        (ctx_near, ctx_far),
    )
    if grid:
        info = jnp.stack([(zi + o) % (fsdp // 2) for o in SHIFTS + (0,)] + [yi])
        first_b, other_b, keeps = attn_grads(*attn_args, after(info, out_rows), depth)
        first_y = swap(first_b, "fsdp", 1)
        other_y = swap(other_b, "fsdp", 1)
        first_x = after(first_x, first_b)

    half = rows // 2
    grad_rows, vec_part = pl.pallas_call(
        first_back_body,
        grid=(2,),
        in_specs=[
            pl.BlockSpec((half, width), lambda i: (i, 0)),
            pl.BlockSpec((half, width), lambda i: (i, 0)),
            pl.BlockSpec((half, 128), lambda i: (i, 0)),
        ]
        + [pl.BlockSpec((half, width), lambda i: (i, 0))] * 2
        + [pl.BlockSpec((half, width), lambda i: (0, 0))] * 2
        + [pl.BlockSpec((half, width), lambda i: (i, 0))]
        + [pl.BlockSpec((8, width), lambda i: (0, 0))] * 3,
        out_specs=[
            pl.BlockSpec((half, width), lambda i: (i, 0)),
            pl.BlockSpec((8, width), lambda i: (0, 0)),
        ],
        out_shape=[shape((rows, width), BF16), shape((8, width), F32)],
        scratch_shapes=[pltpu.VMEM((8, width), F32)],
        compiler_params=params(12),
        cost_estimate=COST,
        name="first_back",
    )(own_rows, cot, gate_grad, hidden_grad, f0, *first_c, first_x, vec, router_part, second_part)
    t2 = swap(grad_rows, "tensor", 2)
    t1 = swap(grad_rows, "tensor", 1)
    onehot_t = (
        after(place, grad_rows)[:, None, :] == positions[None, :, None]
    ).astype(BF16)
    o3 = pair_swap(after(o2, grad_rows))
    mixed = place_rows(tokens, onehot_t, [after(out_rows, grad_rows), o1], order_near)
    if grid:
        z_first = to_z(keeps[0], after(first_y, grad_rows), SHIFTS[0])
    mixed = place_rows(tokens, onehot_t, [o2, *o3], order_far, mixed)
    near_gate = mixed
    if grid:
        other_y = after(other_y, near_gate)
        z_second = to_z(keeps[1], other_y[0:depth], SHIFTS[1])
        z_third = to_z(keeps[2], other_y[depth : 2 * depth], SHIFTS[2])
    token_grad = place_rows(cotangent, onehot_t, [after(grad_rows, near_gate), t1], order_near)
    t3 = pair_swap(after(t2, token_grad))
    token_grad = place_rows(cotangent, onehot_t, [t2, *t3], order_far, token_grad)
    up_grad, down_grad = finish(
        finish_mlp_kernel, "finish_mlp", [(depth, ff), (ff, depth)], after(mlp_total, token_grad)
    )

    if grid:
        vec_sum = vec_part
        for axis, mask in (("tensor", 1), ("tensor", 2)):
            vec_sum = vec_sum + swap(vec_sum, axis, mask)
        vec_sum = vec_sum + after(swap(vec_sum, "fsdp", 1), token_grad)
        vec_sum = vec_sum + z_move(vec_sum, 1) + z_move(vec_sum, 3) + z_move(vec_sum, 2)
        wide = (depth, local)
        attn_out = finish(
            finish_attn_kernel,
            "finish_attn",
            [wide, wide, wide, (local, depth)],
            keeps[3],
            after(other_y[2 * depth :], token_grad),
            z_first,
            z_second,
            z_third,
        )
    else:

        def reduced(xs, ys):
            x = t_mm(jnp.concatenate(xs, axis=0), jnp.concatenate(ys, axis=0))
            return lax.psum_scatter(x, "fsdp", scatter_dimension=0, tiled=True)

        qkv_grad = reduced(attn_args[0], attn_args[2])
        o_grad = reduced(attn_args[1], attn_args[3])
        attn_out = jnp.split(qkv_grad, 3, axis=1) + [o_grad.T]
        vec_sum = lax.psum(vec_part, ("fsdp", "tensor"))
    vec_own = lax.dynamic_slice(vec_sum, (0, me_f * depth), (3, depth))

    return (mixed, token_grad, *attn_out, up_grad, down_grad, vec_own[0], vec_own[1], vec_own[2])


def solution(mesh):
    in_specs = (
        P("fsdp", "tensor", None),
        P("fsdp", "tensor", None),
        P("fsdp", None),
        P("fsdp", "tensor"),
        P("fsdp", "tensor"),
        P("fsdp", "tensor"),
        P("tensor", "fsdp"),
        P("fsdp", "tensor"),
        P("tensor", "fsdp"),
        P("fsdp"),
        P("fsdp"),
        P("fsdp"),
    )
    out_specs = (
        P("fsdp", "tensor", None),
        P("fsdp", "tensor", None),
        P("fsdp", "tensor"),
        P("fsdp", "tensor"),
        P("fsdp", "tensor"),
        P("tensor", "fsdp"),
        P("fsdp", "tensor"),
        P("tensor", "fsdp"),
        P("fsdp"),
        P("fsdp"),
        P("fsdp"),
    )
    return jax.shard_map(shards, mesh=mesh, in_specs=in_specs, out_specs=out_specs, check_vma=False)
```

```python
import functools

import jax
import jax.numpy as jnp
from jax import lax
from jax.experimental import pallas as pl
from jax.experimental.pallas import tpu as pltpu
from jax.sharding import PartitionSpec as P

HEAD_DIM = 64
BLOCK = 256
EPS = 1e-06
NEG = -1e30
F32 = jnp.float32
BF16 = jnp.bfloat16
GELU_C = 0.7978845608028654
GELU_A = 0.044715

VMEM_SPEC = pl.BlockSpec(memory_space=pltpu.VMEM)
SMEM_SPEC = pl.BlockSpec(memory_space=pltpu.SMEM)
HBM_SPEC = pl.BlockSpec(memory_space=pltpu.HBM)


def mm(a, b):
    return jnp.dot(a, b, preferred_element_type=F32)


def mm_t(a, b):
    return lax.dot_general(a, b, (((1,), (1,)), ((), ())), preferred_element_type=F32)


def t_mm(a, b):
    return lax.dot_general(a, b, (((0,), (0,)), ((), ())), preferred_element_type=F32)


def shape(dims, dtype):
    return jax.ShapeDtypeStruct(dims, dtype)


def after(value, *others):
    return lax.optimization_barrier((value,) + others)[0]


COST = pl.CostEstimate(flops=1, bytes_accessed=1, transcendentals=0)


def in_hbm(value):
    return pltpu.with_memory_space_constraint(value, pltpu.HBM)


def params(mib):
    return pltpu.CompilerParams(vmem_limit_bytes=max(mib, 40) << 20)


def tiles(total, width, step):
    def body(j, carry):
        step(pl.ds(pl.multiple_of(j * width, width), width), j)
        return carry

    lax.fori_loop(0, total // width, body, 0)


def pick_kernel(order, onehot, values, out, buf, sems):
    routed = onehot.shape[1]
    count = buf.shape[0]
    copies = [
        pltpu.make_async_copy(values.at[order[i]], buf.at[i], sems.at[i]) for i in range(count)
    ]
    for copy in copies:
        copy.start()
    for i, copy in enumerate(copies):
        copy.wait()
        out[i * routed : (i + 1) * routed, :] = mm(onehot[order[i]], buf[i]).astype(BF16)


def pick_rows(values, onehot, order):
    count = order.shape[0]
    _, routed, span = onehot.shape
    width = values.shape[2]
    return pl.pallas_call(
        pick_kernel,
        in_specs=[SMEM_SPEC, VMEM_SPEC, HBM_SPEC],
        out_specs=VMEM_SPEC,
        out_shape=shape((count * routed, width), BF16),
        scratch_shapes=[
            pltpu.VMEM((count, span, width), BF16),
            pltpu.SemaphoreType.DMA((count,)),
        ],
        compiler_params=params(8),
        cost_estimate=COST,
        name="pick_rows",
    )(order, onehot, in_hbm(values))


def place_kernel(order, onehot_t, *refs, blocks):
    out, buf, sums, loads, stores = refs[-5:]
    row_refs = refs[:blocks]
    base = refs[blocks]
    count = buf.shape[0]
    routed = onehot_t.shape[2]
    found = [(ref, at) for ref in row_refs for at in range(0, ref.shape[0], routed)]
    reads = [
        pltpu.make_async_copy(base.at[order[i]], buf.at[i], loads.at[i]) for i in range(count)
    ]
    writes = [
        pltpu.make_async_copy(sums.at[i], out.at[order[i]], stores.at[i]) for i in range(count)
    ]
    for copy in reads:
        copy.start()
    for i in range(count):
        ref, at = found[i]
        rows = ref[at : at + routed, :]
        hot = onehot_t[order[i]]
        keep = 1.0 - jnp.sum(hot.astype(F32), axis=1, keepdims=True)
        reads[i].wait()
        sums[i] = buf[i] * keep.astype(BF16) + mm(hot, rows).astype(BF16)
        writes[i].start()
    for copy in writes:
        copy.wait()


def place_rows(base, onehot_t, rows, order, into=None):
    _, span, width = base.shape
    count = order.shape[0]
    extra = [] if into is None else [into]
    return pl.pallas_call(
        functools.partial(place_kernel, blocks=len(rows)),
        in_specs=[SMEM_SPEC, VMEM_SPEC]
        + [VMEM_SPEC] * len(rows)
        + [HBM_SPEC] * (1 + len(extra)),
        out_specs=HBM_SPEC,
        out_shape=shape(base.shape, BF16),
        scratch_shapes=[
            pltpu.VMEM((count, span, width), BF16),
            pltpu.VMEM((count, span, width), BF16),
            pltpu.SemaphoreType.DMA((count,)),
            pltpu.SemaphoreType.DMA((count,)),
        ],
        input_output_aliases={3 + len(rows): 0} if extra else {},
        compiler_params=params(8),
        cost_estimate=COST,
        name="place_rows",
    )(order, onehot_t, *rows, in_hbm(base), *extra)


def row_call(body, name, inputs, outputs, rows, width, steps=2):
    block = rows // steps
    in_specs = []
    for array, kind in inputs:
        if kind == "w":
            in_specs.append(pl.BlockSpec(array.shape, lambda i: (0, 0)))
        elif kind == "h":
            in_specs.append(pl.BlockSpec((block, array.shape[1]), lambda i: (0, 0)))
        else:
            in_specs.append(pl.BlockSpec((block, array.shape[1]), lambda i: (i, 0)))
    out_specs = []
    out_shapes = []
    for dims, dtype, kind in outputs:
        out_shapes.append(shape(dims, dtype))
        if kind == "w":
            out_specs.append(pl.BlockSpec(dims, lambda i: (0, 0)))
        else:
            out_specs.append(pl.BlockSpec((block, dims[1]), lambda i: (i, 0)))
    return pl.pallas_call(
        body,
        grid=(steps,),
        in_specs=in_specs,
        out_specs=out_specs,
        out_shape=out_shapes,
        compiler_params=params(10),
        cost_estimate=COST,
        name=name,
    )(*[array for array, _ in inputs])


def row_mean(x):
    return jnp.mean(x, axis=-1, keepdims=True)


def total3(a, b0, b1, c):
    b = jnp.where(pl.program_id(0) == 0, b0[...].astype(F32), b1[...].astype(F32))
    return a[...].astype(F32) + b + c[...].astype(F32)


def lanes(col):
    return jnp.broadcast_to(col, (col.shape[0], 128))


def fold(x):
    return jnp.sum(x.reshape(-1, 8, x.shape[1]), axis=0)


def accumulate(ref, value):
    @pl.when(pl.program_id(0) == 0)
    def _():
        ref[...] = value

    @pl.when(pl.program_id(0) > 0)
    def _():
        ref[...] += value


def first_norm_body(a, b0, b1, c, vec, rows_out, normed_out, gate_out):
    rows = total3(a, b0, b1, c)
    rows_out[...] = rows.astype(BF16)
    logit = jnp.sum(rows * vec[0:1, :], axis=-1, keepdims=True)
    gate_out[...] = lanes(jax.nn.sigmoid(logit))
    scale = lax.rsqrt(row_mean(rows * rows) + EPS)
    normed_out[...] = (rows * scale * vec[1:2, :]).astype(BF16)


def cot_body(a, b0, b1, c, gate, cot_out, grad_out):
    cot = total3(a, b0, b1, c)
    cot_out[...] = cot.astype(BF16)
    grad_out[...] = (cot * gate[:, 0:1]).astype(BF16)


def second_norm_body(rows, a, b0, b1, c, vec, attn_out, normed_out):
    attn = total3(a, b0, b1, c)
    attn_out[...] = attn
    hidden = rows[...].astype(F32) + attn
    scale = lax.rsqrt(row_mean(hidden * hidden) + EPS)
    normed_out[...] = (hidden * scale * vec[2:3, :]).astype(BF16)


def second_back_body(rows, attn, cot, gate, a, b0, b1, c, vec, grad_out, hidden_out, gain_out):
    second_grad = total3(a, b0, b1, c)
    hidden = rows[...].astype(F32) + attn[...]
    scale = lax.rsqrt(row_mean(hidden * hidden) + EPS)
    normal = hidden * scale
    grad = second_grad * vec[2:3, :]
    hidden_grad = scale * (grad - normal * row_mean(grad * normal))
    hidden_out[...] = hidden_grad
    grad_out[...] = (cot[...].astype(F32) * gate[:, 0:1] + hidden_grad).astype(BF16)
    accumulate(gain_out, fold(second_grad * normal))


def out_body(rows, attn, cot, gate, a, b0, b1, c, rows_out, gate_grad_out, router_out):
    branch = attn[...] + total3(a, b0, b1, c)
    x = rows[...].astype(F32)
    g = gate[:, 0:1]
    rows_out[...] = (x + g * branch).astype(BF16)
    gate_grad = jnp.sum(cot[...].astype(F32) * branch, axis=-1, keepdims=True) * g * (1.0 - g)
    gate_grad_out[...] = lanes(gate_grad)
    accumulate(router_out, fold(x * gate_grad))


def first_back_body(
    rows, cot, gate_grad, hidden_grad, a, b0, b1, c, vec, router_part, second_part, grad_out, vec_out, acc
):
    first_grad = total3(a, b0, b1, c)
    x = rows[...].astype(F32)
    scale = lax.rsqrt(row_mean(x * x) + EPS)
    normal = x * scale
    grad = first_grad * vec[1:2, :]
    norm_grad = scale * (grad - normal * row_mean(grad * normal))
    grad_out[...] = (
        cot[...].astype(F32) + gate_grad[:, 0:1] * vec[0:1, :] + hidden_grad[...] + norm_grad
    ).astype(BF16)
    accumulate(acc, fold(first_grad * normal))

    @pl.when(pl.program_id(0) == pl.num_programs(0) - 1)
    def _():
        vec_out[0:1, :] = jnp.sum(router_part[...], axis=0, keepdims=True)
        vec_out[1:2, :] = jnp.sum(acc[...], axis=0, keepdims=True)
        vec_out[2:3, :] = jnp.sum(second_part[...], axis=0, keepdims=True)
        vec_out[3:8, :] = jnp.zeros_like(vec_out[3:8, :])


def pack_mlp_kernel(up, down, out, buf, sems):
    depth = up.shape[0]
    copies = [
        pltpu.make_async_copy(up, out.at[0:depth, :], sems.at[0]),
        pltpu.make_async_copy(down, buf, sems.at[1]),
    ]
    for copy in copies:
        copy.start()
    copies[1].wait()
    out[depth : 2 * depth, :] = buf[...].T
    copies[0].wait()


def pack_attn_kernel(q, k, v, o, small, out, buf, sems):
    depth, local = q.shape
    copies = [
        pltpu.make_async_copy(
            x, out.at[0:depth, i * local : (i + 1) * local], sems.at[i]
        )
        for i, x in enumerate((q, k, v))
    ]
    copies.append(pltpu.make_async_copy(o, buf, sems.at[3]))
    for copy in copies:
        copy.start()
    out[depth:, :] = jnp.zeros_like(out[depth:, :])
    out[depth:, 0:depth] = small[...]
    copies[3].wait()
    out[0:depth, 3 * local : 4 * local] = buf[...].T
    for copy in copies[:3]:
        copy.wait()


def pack_mlp(up, down):
    return pl.pallas_call(
        pack_mlp_kernel,
        in_specs=[HBM_SPEC] * 2,
        out_specs=VMEM_SPEC,
        out_shape=shape((2 * up.shape[0], up.shape[1]), BF16),
        scratch_shapes=[pltpu.VMEM(down.shape, BF16), pltpu.SemaphoreType.DMA((2,))],
        compiler_params=params(4),
        cost_estimate=COST,
        name="pack_mlp",
    )(in_hbm(up), in_hbm(down))


def pack_attn(q, k, v, o, small):
    depth, local = q.shape
    return pl.pallas_call(
        pack_attn_kernel,
        in_specs=[HBM_SPEC] * 4 + [VMEM_SPEC],
        out_specs=VMEM_SPEC,
        out_shape=shape((depth + 16, 4 * local), BF16),
        scratch_shapes=[pltpu.VMEM(o.shape, BF16), pltpu.SemaphoreType.DMA((4,))],
        compiler_params=params(4),
        cost_estimate=COST,
        name="pack_attn",
    )(in_hbm(q), in_hbm(k), in_hbm(v), in_hbm(o), small)


def finish_mlp_kernel(total, up_out, down_out):
    depth = up_out.shape[0]
    total = total[...].astype(F32)
    up_out[...] = total[0:depth]
    down_out[...] = total[depth:].T


def finish_attn_kernel(own, got, p1, p2, p3, q_out, k_out, v_out, o_out):
    local = q_out.shape[1]
    total = own[...] + got[...].astype(F32)
    for part in (p1, p2, p3):
        total = total + part[...].astype(F32)
    q_out[...] = total[:, 0:local]
    k_out[...] = total[:, local : 2 * local]
    v_out[...] = total[:, 2 * local : 3 * local]
    o_out[...] = total[:, 3 * local :].T


def finish(body, name, dims, *arrays):
    return pl.pallas_call(
        body,
        in_specs=[VMEM_SPEC] * len(arrays),
        out_specs=[VMEM_SPEC] * len(dims),
        out_shape=[shape(d, F32) for d in dims],
        compiler_params=params(8),
        cost_estimate=COST,
        name=name,
    )(*arrays)


def join_kernel(places, *refs):
    *pieces, out, vec = refs
    depth = out.shape[0] // (len(pieces) - 1)
    vec[...] = jnp.zeros_like(vec)
    for number, piece in enumerate(pieces):
        if number > 0:
            out[(number - 1) * depth : number * depth, :] = piece[0:depth, :]
        place = places[number] * 2 + places[4]
        lanes_at = pl.ds(pl.multiple_of(place * depth, depth), depth)
        vec[:, lanes_at] = piece[depth : depth + 16, 0:depth]


def join(pieces, places, depth):
    width = pieces[0].shape[1]
    return pl.pallas_call(
        join_kernel,
        in_specs=[SMEM_SPEC] + [VMEM_SPEC] * len(pieces),
        out_specs=[VMEM_SPEC] * 2,
        out_shape=[
            shape((depth * (len(pieces) - 1), width), BF16),
            shape((16, width), BF16),
        ],
        compiler_params=params(6),
        cost_estimate=COST,
        name="join",
    )(places, *pieces)


def assemble_kernel(places, near_own, near, far_own, far, out):
    depth = 128
    for side, halves in enumerate(((near_own, near), (far_own, far))):
        for number in range(4):
            ref = halves[min(number, 1)]
            row = max(number - 1, 0) * depth
            place = places[number] * 2 + (places[4] ^ side)
            at = pl.multiple_of(place * depth, depth)
            out[pl.ds(at, depth), :] = ref[row : row + depth, :]


def assemble(near_own, near, far_own, far, places):
    rows, width = near.shape
    return pl.pallas_call(
        assemble_kernel,
        in_specs=[SMEM_SPEC] + [VMEM_SPEC] * 4,
        out_specs=VMEM_SPEC,
        out_shape=shape((rows * 8 // 3, width), BF16),
        compiler_params=params(6),
        cost_estimate=COST,
        name="assemble",
    )(places, near_own, near, far_own, far)


def head_masks(width):
    lane = lax.broadcasted_iota(jnp.int32, (1, width), 1) // HEAD_DIM
    return [(lane == h).astype(BF16) for h in range(width // HEAD_DIM)]


def spread(x, masks):
    return jnp.concatenate([x * mask for mask in masks], axis=0)


def side_by_side(x, count):
    rows = x.shape[0] // count
    return jnp.concatenate([x[h * rows : (h + 1) * rows] for h in range(count)], axis=1)


def seq_probs(q4, k, bias, count):
    scores = mm_t(q4, k) * (HEAD_DIM**-0.5)
    scores = scores + jnp.concatenate([bias] * count, axis=0)
    top = jnp.max(scores, axis=-1, keepdims=True)
    weight = jnp.exp(scores - top)
    return weight / jnp.sum(weight, axis=-1, keepdims=True)


def fill(ref, parts):
    at = 0
    for part in parts:
        ref[at : at + part.shape[0], :] = part[...]
        at += part.shape[0]


def attn_fwd_kernel(order, *refs, parts):
    w, bias, qkv, ctx, pa, pb, x = refs[parts:]
    fill(x, refs[:parts])
    half = pa.shape[0]
    local = ctx.shape[1]
    routed = bias.shape[1]
    heads = local // HEAD_DIM
    masks = head_masks(local)

    def project(cols, j):
        qkv[:, cols] = mm(x[...], w[:, cols]).astype(BF16)

    tiles(3 * local, local, project)

    def seq(rows, s):
        q = qkv[rows, 0:local]
        k = qkv[rows, local : 2 * local]
        v = qkv[rows, 2 * local : 3 * local]
        probs = seq_probs(spread(q, masks), k, bias[order[s]], heads).astype(BF16)
        ctx[rows, :] = mm(side_by_side(probs, heads), spread(v, masks)).astype(BF16)

    tiles(qkv.shape[0], routed, seq)

    def emit(cols, j):
        part = mm_t(ctx[...], w[cols, 3 * local : 4 * local]).astype(BF16)
        pa[:, cols] = part[0:half]
        pb[:, cols] = part[half:]

    tiles(pa.shape[1], 256, emit)


def attn_fwd(xa, xb, w, bias, order, local):
    rows, width = xa.shape
    return pl.pallas_call(
        functools.partial(attn_fwd_kernel, parts=1 + len(xb)),
        in_specs=[SMEM_SPEC] + [VMEM_SPEC] * (3 + len(xb)),
        out_specs=[VMEM_SPEC] * 4,
        out_shape=[
            shape((2 * rows, 3 * local), BF16),
            shape((2 * rows, local), BF16),
            shape((rows, width), BF16),
            shape((rows, width), BF16),
        ],
        scratch_shapes=[pltpu.VMEM((2 * rows, width), BF16)],
        compiler_params=params(12),
        cost_estimate=COST,
        name="attn_fwd",
    )(order, xa, *xb, w, bias)


def attn_bwd_kernel(order, *refs, parts):
    w, qkv, bias, dqkv, fa, fb, cg, g = refs[parts:]
    fill(g, refs[:parts])
    half = fa.shape[0]
    local = cg.shape[1]
    routed = bias.shape[1]
    heads = local // HEAD_DIM
    masks = head_masks(local)
    cg[...] = mm(g[...], w[:, 3 * local : 4 * local]).astype(BF16)

    def seq(rows, s):
        q4 = spread(qkv[rows, 0:local], masks)
        k = qkv[rows, local : 2 * local]
        v = qkv[rows, 2 * local : 3 * local]
        exact = seq_probs(q4, k, bias[order[s]], heads)
        c4 = spread(cg[rows, :], masks)
        prob_grad = mm_t(c4, v)
        dqkv[rows, 2 * local : 3 * local] = t_mm(exact.astype(BF16), c4).astype(BF16)
        inner = jnp.sum(exact * prob_grad, axis=-1, keepdims=True)
        score_grad = (exact * (prob_grad - inner)).astype(BF16)
        scale = HEAD_DIM**-0.5
        dq = mm(side_by_side(score_grad, heads), spread(k, masks)) * scale
        dqkv[rows, 0:local] = dq.astype(BF16)
        dqkv[rows, local : 2 * local] = (t_mm(score_grad, q4) * scale).astype(BF16)

    tiles(qkv.shape[0], routed, seq)

    def emit(cols, j):
        part = mm_t(dqkv[...], w[cols, 0 : 3 * local]).astype(BF16)
        fa[:, cols] = part[0:half]
        fb[:, cols] = part[half:]

    tiles(fa.shape[1], 256, emit)


def attn_bwd(ga, gb, w, qkv, bias, order, local):
    rows, width = ga.shape
    return pl.pallas_call(
        functools.partial(attn_bwd_kernel, parts=1 + len(gb)),
        in_specs=[SMEM_SPEC] + [VMEM_SPEC] * (4 + len(gb)),
        out_specs=[VMEM_SPEC] * 3,
        out_shape=[
            shape((2 * rows, 3 * local), BF16),
            shape((rows, width), BF16),
            shape((rows, width), BF16),
        ],
        scratch_shapes=[
            pltpu.VMEM((2 * rows, local), BF16),
            pltpu.VMEM((2 * rows, width), BF16),
        ],
        compiler_params=params(12),
        cost_estimate=COST,
        name="attn_bwd",
    )(order, ga, *gb, w, qkv, bias)


def mlp_kernel(*refs, parts):
    w, act, ug, da, db, ma, mb, n, g = refs[2 * parts :]
    fill(n, refs[:parts])
    fill(g, refs[parts : 2 * parts])
    rows, width = da.shape
    part, both, ff = w.shape
    depth = both // 2

    def up(cols, j):
        x = mm(n[...], w[:, 0:depth, cols].reshape(width, -1))
        inner = jnp.tanh(GELU_C * (x + GELU_A * (x * x * x)))
        half_in = 0.5 * (1.0 + inner)
        act[:, cols] = (x * half_in).astype(BF16)
        slope = half_in + (0.5 * GELU_C) * x * (1.0 - inner * inner) * (
            1.0 + (3.0 * GELU_A) * (x * x)
        )
        grad = mm(g[...], w[:, depth:both, cols].reshape(width, -1))
        ug[:, cols] = (grad * slope).astype(BF16)

    tiles(ff, 256, up)
    group = part * 256 // width

    def back(cols, j):
        wu = w[pl.ds(j * group, group), 0:depth, :].reshape(256, -1)
        out = mm_t(ug[...], wu).astype(BF16)
        da[:, cols] = out[0:rows]
        db[:, cols] = out[rows:]

    tiles(width, 256, back)

    def down(cols, j):
        wd = w[pl.ds(j * group, group), depth:both, :].reshape(256, -1)
        out = mm_t(act[...], wd).astype(BF16)
        ma[:, cols] = out[0:rows]
        mb[:, cols] = out[rows:]

    tiles(width, 256, down)


def mlp_both(na, nb, ga, gb, w):
    rows, width = na.shape
    ff = w.shape[2]
    return pl.pallas_call(
        functools.partial(mlp_kernel, parts=1 + len(nb)),
        in_specs=[VMEM_SPEC] * (3 + 2 * len(nb)),
        out_specs=[VMEM_SPEC] * 6,
        out_shape=[shape((2 * rows, ff), BF16)] * 2 + [shape((rows, width), BF16)] * 4,
        scratch_shapes=[pltpu.VMEM((2 * rows, width), BF16)] * 2,
        compiler_params=params(16),
        cost_estimate=COST,
        name="mlp",
    )(na, *nb, ga, *gb, w)


def turn(xt, pieces, cols):
    at = 0
    for piece in pieces:
        size = piece.shape[0]
        xt[:, at : at + size] = piece[:, cols].T
        at += size


def mlp_grads_kernel(*refs, depth, pieces):
    normed, grads = refs[:pieces], refs[pieces : 2 * pieces]
    un, uf, an, af, out, xt = refs[2 * pieces :]
    half = un.shape[0]
    width = normed[0].shape[1]
    for side, (xs, near, far) in enumerate(((normed, un, uf), (grads, an, af))):
        tiles(
            width,
            256,
            lambda cols, j, xs=xs: turn(
                xt.at[pl.ds(pl.multiple_of(j * 256, 256), 256), :], xs, cols
            ),
        )

        def block(ncols, j, near=near, far=far, side=side):
            total = mm(xt[:, 0:half], near[:, ncols]) + mm(xt[:, half:], far[:, ncols])
            for f in range(width // depth):
                at = (2 * f + side) * depth
                out[at : at + depth, ncols] = total[f * depth : (f + 1) * depth].astype(BF16)

        tiles(near.shape[1], 256, block)


def mlp_grads(normed, grads, ug, act, depth):
    width = normed[0].shape[1]
    rows, ff = ug[0].shape
    return pl.pallas_call(
        functools.partial(mlp_grads_kernel, depth=depth, pieces=len(normed)),
        in_specs=[VMEM_SPEC] * (2 * len(normed) + 4),
        out_specs=VMEM_SPEC,
        out_shape=shape((2 * width, ff), BF16),
        scratch_shapes=[pltpu.VMEM((width, 2 * rows), BF16)],
        compiler_params=params(20),
        cost_estimate=COST,
        name="mlp_grads",
    )(*normed, *grads, *ug, *act)


def attn_grads_kernel(info, *refs, pieces):
    normed, grads = refs[:pieces], refs[pieces : 2 * pieces]
    dn, df, cn, cf, first, others, *keeps, xt = refs[2 * pieces :]
    half = dn.shape[0]
    local = cn.shape[1]
    depth = first.shape[0]
    count = len(keeps)
    low = info[count] == 0
    for lane, wide, xs, near, far in (
        (0, 3 * local, normed, dn, df),
        (3 * local, local, grads, cn, cf),
    ):
        for o in range(count):
            cols = pl.ds(pl.multiple_of(info[o] * 256, 256), 256)
            turn(xt.at[o * 256 : (o + 1) * 256, :], xs, cols)

        def block(ncols, j, near=near, far=far, lane=lane):
            total = mm(xt[:, 0:half], near[:, ncols]) + mm(xt[:, half:], far[:, ncols])
            dst = pl.ds(pl.multiple_of(j * 256, 256) + lane, 256)
            for o in range(count):
                one = total[o * 256 : o * 256 + depth]
                two = total[o * 256 + depth : (o + 1) * 256]
                send, row = (first, 0) if o == 0 else (others, (o - 1) * depth)
                send[row : row + depth, dst] = jnp.where(low, two, one).astype(BF16)
                keeps[o][:, dst] = jnp.where(low, one, two)

        tiles(wide, 256, block)


def attn_grads(normed, grads, dqkv, ctx, info, depth):
    rows, local = ctx[0].shape
    count = info.shape[0] - 1
    first, others, *keeps = pl.pallas_call(
        functools.partial(attn_grads_kernel, pieces=len(normed)),
        in_specs=[SMEM_SPEC] + [VMEM_SPEC] * (2 * len(normed) + 4),
        out_specs=[VMEM_SPEC] * (2 + count),
        out_shape=[
            shape((depth, 4 * local), BF16),
            shape(((count - 1) * depth, 4 * local), BF16),
        ]
        + [shape((depth, 4 * local), F32)] * count,
        scratch_shapes=[pltpu.VMEM((count * 256, 2 * rows), BF16)],
        compiler_params=params(14),
        cost_estimate=COST,
        name="attn_grads",
    )(info, *normed, *grads, *dqkv, *ctx)
    return first, others, keeps


def swap(x, axis, mask):
    size = lax.axis_size(axis)
    return lax.ppermute(x, axis, [(i, i ^ mask) for i in range(size)])


def halves(x):
    step = x.shape[0] // 2
    return x[:step], x[step:]


def pair_swap(x):
    return tuple(swap(h, "tensor", 1) for h in halves(x))


def pair_sum(near, diag):
    return jnp.concatenate(
        [
            (n.astype(F32) + g.astype(F32)).astype(BF16)
            for n, g in zip(halves(near), pair_swap(diag))
        ],
        axis=0,
    )


def z_perm(size, shift):
    places = size // 2
    return [((f // 2 + shift) % places * 2 + f % 2, f) for f in range(size)]


def z_move(x, shift):
    return lax.ppermute(x, "fsdp", z_perm(lax.axis_size("fsdp"), shift))


SHIFTS = (2, 1, 3)


def shards(
    tokens,
    cotangent,
    routed_index,
    query_weight,
    key_weight,
    value_weight,
    output_weight,
    up_weight,
    down_weight,
    router_weight,
    attn_gain,
    mlp_gain,
):
    fsdp = lax.axis_size("fsdp")
    grid = fsdp == 8
    me_f = lax.axis_index("fsdp")
    me_t = lax.axis_index("tensor")
    seqs, span, width = tokens.shape
    routed = routed_index.shape[1]
    per = seqs // lax.axis_size("tensor")
    local = query_weight.shape[1]
    depth = query_weight.shape[0]
    ff = up_weight.shape[1]
    rows = per * routed

    place = routed_index - me_t * span
    positions = jnp.arange(span, dtype=jnp.int32)
    onehot = (place[:, :, None] == positions[None, None, :]).astype(BF16)
    order = jnp.stack([(me_t ^ m) * per + j for m in range(4) for j in range(per)])
    order_keep = jnp.concatenate([order[0:per], order[2 * per : 3 * per]])
    order_send = jnp.concatenate([order[per : 2 * per], order[3 * per :]])
    order_near = order[: 2 * per]
    order_far = order[2 * per :]

    row_shape = ((rows, width), BF16, "r")
    f32_shape = ((rows, width), F32, "r")
    gate_shape = ((rows, 128), F32, "r")
    vec_shape = ((8, width), F32, "w")

    def row_step(body, name, ins, outs):
        return row_call(body, name, ins, outs, rows, width)

    def r(*arrays):
        found = []
        for a in arrays:
            found += [(h, "h") for h in a] if isinstance(a, tuple) else [(a, "r")]
        return found

    zi = me_f // 2
    yi = me_f % 2

    small = jnp.stack([router_weight, attn_gain, mlp_gain])
    if grid:
        small = jnp.concatenate([small, jnp.zeros((13, depth), BF16)], axis=0)
        attn_piece = pack_attn(query_weight, key_weight, value_weight, output_weight, small)
        z_pieces = [z_move(attn_piece, o) for o in SHIFTS]
        far_own = swap(attn_piece, "fsdp", 1)
        z_at = jnp.stack([zi] + [(zi + o) % (fsdp // 2) for o in SHIFTS] + [yi])
    else:
        attn_piece = jnp.concatenate(
            [query_weight, key_weight, value_weight, output_weight.T], axis=1
        )
        z_pieces = []
        vec = lax.all_gather(small, "fsdp", axis=1, tiled=True)
        vec = jnp.concatenate([vec, jnp.zeros((5, width), BF16)], axis=0).astype(F32)
    tok_send = pick_rows(tokens, onehot, after(order_send, attn_piece))
    tok_got = pair_swap(tok_send)
    tok_keep = pick_rows(tokens, onehot, after(order_keep, tok_send))
    tok_sum = tok_keep[rows:] + tok_got[1]
    tok_far = [swap(h, "tensor", 2) for h in halves(tok_sum)]
    cot_send = pick_rows(cotangent, onehot, after(order_send, tok_sum))
    cot_got = pair_swap(cot_send)
    cot_keep = pick_rows(cotangent, onehot, after(order_keep, cot_send))
    cot_sum = cot_keep[rows:] + cot_got[1]
    cot_far = [swap(h, "tensor", 2) for h in halves(cot_sum)]
    if grid:
        mlp_piece = pack_mlp(up_weight, after(down_weight, cot_keep))
        gated = [after(z, mlp_piece, *tok_far, *cot_far) for z in z_pieces]
        near_w, vec_near = join([attn_piece] + gated, z_at, depth)
        vec = vec_near + swap(vec_near, "fsdp", 1)
        far_w = swap(after(near_w, vec), "fsdp", 1)
        vec = vec[0:8].astype(F32)
        mlp_piece = after(mlp_piece, near_w)
    else:
        mlp_piece = jnp.concatenate([up_weight, down_weight.T], axis=0)
    up_down = lax.all_gather(mlp_piece, "fsdp", axis=0, tiled=True)
    up_down = up_down.reshape(fsdp, 2 * depth, ff)

    def with_halves(body):
        def whole(keep, got, far0, far1, *rest):
            far = jnp.where(pl.program_id(0) == 0, far0[...], far1[...])
            return body(keep, got, got, far, *rest)

        return whole

    own_rows, n0, gate = row_step(
        with_halves(first_norm_body),
        "first_norm",
        [(tok_keep, "r"), (tok_got[0], "r")] + r(tuple(tok_far)) + [(vec, "w")],
        [row_shape, row_shape, gate_shape],
    )
    n2 = swap(n0, "tensor", 2)
    n1 = swap(n0, "tensor", 1)
    cot, g0 = row_step(
        with_halves(cot_body),
        "cot_rows",
        [(cot_keep, "r"), (cot_got[0], "r")] + r(tuple(cot_far)) + [(after(gate, n0), "r")],
        [row_shape, row_shape],
    )
    g2 = swap(after(g0, n2), "tensor", 2)
    g1 = swap(g0, "tensor", 1)
    blocks = after(routed_index, g0) // BLOCK
    bias = jnp.where(blocks[:, None, :] <= blocks[:, :, None], 0.0, NEG).astype(F32)
    if grid:
        attn_w = assemble(attn_piece, after(near_w, g0), far_own, far_w, z_at)
    else:
        attn_w = lax.all_gather(attn_piece, "fsdp", axis=0, tiled=True)
    n3 = pair_swap(after(n2, attn_w))

    qkv_far, ctx_far, p2, p3 = attn_fwd(
        after(n2, g2), n3, attn_w, bias, order_far, local
    )
    attn_sum = pair_sum(p2, p3)
    attn_x = swap(attn_sum, "tensor", 2)
    qkv_near, ctx_near, p0, p1 = attn_fwd(
        after(n0, attn_sum), (n1,), attn_w, bias, order_near, local
    )
    attn_c = pair_swap(p1)
    attn, s0 = row_step(
        second_norm_body,
        "second_norm",
        r(own_rows, p0, attn_c, attn_x) + [(vec, "w")],
        [f32_shape, row_shape],
    )
    s2 = swap(s0, "tensor", 2)
    s1 = swap(s0, "tensor", 1)
    s3 = pair_swap(s2)
    g3 = pair_swap(after(g2, s0))

    act_far, ug_far, d2, d3, m2, m3 = mlp_both(s2, s3, g2, g3, up_down)
    second_sum = pair_sum(d2, d3)
    second_x = swap(second_sum, "tensor", 2)
    act_near, ug_near, d0, d1, m0, m1 = mlp_both(
        after(s0, second_sum), (s1,), g0, (g1,), up_down
    )
    second_c = pair_swap(d1)

    attn_grad, hidden_grad, second_part = row_step(
        second_back_body,
        "second_back",
        r(own_rows, attn, cot, gate, d0, second_c, second_x) + [(vec, "w")],
        [row_shape, f32_shape, vec_shape],
    )
    a0 = attn_grad
    a2 = swap(a0, "tensor", 2)
    a1 = swap(a0, "tensor", 1)
    mlp_all = mlp_grads(
        (after(s0, a0), s1, s2, *s3),
        (g0, g1, g2, *g3),
        (ug_near, ug_far),
        (act_near, act_far),
        depth,
    )
    a2 = after(a2, mlp_all)
    mlp_total = lax.psum_scatter(after(mlp_all, a2), "fsdp", scatter_dimension=0, tiled=True)
    a3 = pair_swap(a2)
    mlp_c = pair_swap(after(m1, mlp_all))
    mlp_sum = pair_sum(m2, after(m3, mlp_all))
    mlp_x = swap(after(mlp_sum, a2), "tensor", 2)

    def to_z(keep, got, shift):
        return z_move((keep + got.astype(F32)).astype(BF16), 4 - shift)

    dqkv_far, f2, f3 = attn_bwd(a2, a3, attn_w, qkv_far, bias, order_far, local)
    first_sum = pair_sum(f2, f3)
    first_x = swap(first_sum, "tensor", 2)
    dqkv_near, f0, f1 = attn_bwd(
        after(a0, first_sum), (a1,), attn_w, qkv_near, bias, order_near, local
    )
    first_c = pair_swap(f1)
    out_rows, gate_grad, router_part = row_step(
        out_body,
        "out_rows",
        r(own_rows, attn, cot, gate, m0, mlp_c, after(mlp_x, f1)),
        [row_shape, gate_shape, vec_shape],
    )
    o2 = swap(out_rows, "tensor", 2)
    o1 = swap(out_rows, "tensor", 1)

    attn_args = (
        (n0, n1, n2, *n3),
        (a0, a1, a2, *a3),
        (dqkv_near, dqkv_far),
        (ctx_near, ctx_far),
    )
    if grid:
        info = jnp.stack([(zi + o) % (fsdp // 2) for o in SHIFTS + (0,)] + [yi])
        first_b, other_b, keeps = attn_grads(*attn_args, after(info, out_rows), depth)
        first_y = swap(first_b, "fsdp", 1)
        other_y = swap(other_b, "fsdp", 1)
        first_x = after(first_x, first_b)

    half = rows // 2
    grad_rows, vec_part = pl.pallas_call(
        first_back_body,
        grid=(2,),
        in_specs=[
            pl.BlockSpec((half, width), lambda i: (i, 0)),
            pl.BlockSpec((half, width), lambda i: (i, 0)),
            pl.BlockSpec((half, 128), lambda i: (i, 0)),
        ]
        + [pl.BlockSpec((half, width), lambda i: (i, 0))] * 2
        + [pl.BlockSpec((half, width), lambda i: (0, 0))] * 2
        + [pl.BlockSpec((half, width), lambda i: (i, 0))]
        + [pl.BlockSpec((8, width), lambda i: (0, 0))] * 3,
        out_specs=[
            pl.BlockSpec((half, width), lambda i: (i, 0)),
            pl.BlockSpec((8, width), lambda i: (0, 0)),
        ],
        out_shape=[shape((rows, width), BF16), shape((8, width), F32)],
        scratch_shapes=[pltpu.VMEM((8, width), F32)],
        compiler_params=params(12),
        cost_estimate=COST,
        name="first_back",
    )(own_rows, cot, gate_grad, hidden_grad, f0, *first_c, first_x, vec, router_part, second_part)
    t2 = swap(grad_rows, "tensor", 2)
    t1 = swap(grad_rows, "tensor", 1)
    onehot_t = (
        after(place, grad_rows)[:, None, :] == positions[None, :, None]
    ).astype(BF16)
    o3 = pair_swap(after(o2, grad_rows))
    mixed = place_rows(tokens, onehot_t, [after(out_rows, grad_rows), o1], order_near)
    if grid:
        z_first = to_z(keeps[0], after(first_y, grad_rows), SHIFTS[0])
    mixed = place_rows(tokens, onehot_t, [o2, *o3], order_far, mixed)
    near_gate = mixed
    if grid:
        other_y = after(other_y, near_gate)
        z_second = to_z(keeps[1], other_y[0:depth], SHIFTS[1])
        z_third = to_z(keeps[2], other_y[depth : 2 * depth], SHIFTS[2])
    token_grad = place_rows(cotangent, onehot_t, [after(grad_rows, near_gate), t1], order_near)
    t3 = pair_swap(after(t2, token_grad))
    token_grad = place_rows(cotangent, onehot_t, [t2, *t3], order_far, token_grad)
    up_grad, down_grad = finish(
        finish_mlp_kernel, "finish_mlp", [(depth, ff), (ff, depth)], after(mlp_total, token_grad)
    )

    if grid:
        vec_sum = vec_part
        for axis, mask in (("tensor", 1), ("tensor", 2)):
            vec_sum = vec_sum + swap(vec_sum, axis, mask)
        vec_sum = vec_sum + after(swap(vec_sum, "fsdp", 1), token_grad)
        vec_sum = vec_sum + z_move(vec_sum, 1) + z_move(vec_sum, 3) + z_move(vec_sum, 2)
        wide = (depth, local)
        attn_out = finish(
            finish_attn_kernel,
            "finish_attn",
            [wide, wide, wide, (local, depth)],
            keeps[3],
            after(other_y[2 * depth :], token_grad),
            z_first,
            z_second,
            z_third,
        )
    else:

        def reduced(xs, ys):
            x = t_mm(jnp.concatenate(xs, axis=0), jnp.concatenate(ys, axis=0))
            return lax.psum_scatter(x, "fsdp", scatter_dimension=0, tiled=True)

        qkv_grad = reduced(attn_args[0], attn_args[2])
        o_grad = reduced(attn_args[1], attn_args[3])
        attn_out = jnp.split(qkv_grad, 3, axis=1) + [o_grad.T]
        vec_sum = lax.psum(vec_part, ("fsdp", "tensor"))
    vec_own = lax.dynamic_slice(vec_sum, (0, me_f * depth), (3, depth))

    return (mixed, token_grad, *attn_out, up_grad, down_grad, vec_own[0], vec_own[1], vec_own[2])


def solution(mesh):
    in_specs = (
        P("fsdp", "tensor", None),
        P("fsdp", "tensor", None),
        P("fsdp", None),
        P("fsdp", "tensor"),
        P("fsdp", "tensor"),
        P("fsdp", "tensor"),
        P("tensor", "fsdp"),
        P("fsdp", "tensor"),
        P("tensor", "fsdp"),
        P("fsdp"),
        P("fsdp"),
        P("fsdp"),
    )
    out_specs = (
        P("fsdp", "tensor", None),
        P("fsdp", "tensor", None),
        P("fsdp", "tensor"),
        P("fsdp", "tensor"),
        P("fsdp", "tensor"),
        P("tensor", "fsdp"),
        P("fsdp", "tensor"),
        P("tensor", "fsdp"),
        P("fsdp"),
        P("fsdp"),
        P("fsdp"),
    )
    return jax.shard_map(shards, mesh=mesh, in_specs=in_specs, out_specs=out_specs, check_vma=False)
```

```python
import functools

import jax
import jax.numpy as jnp
from jax import lax
from jax.experimental import pallas as pl
from jax.experimental.pallas import tpu as pltpu
from jax.sharding import PartitionSpec as P

HEAD_DIM = 64
BLOCK = 256
EPS = 1e-06
NEG = -1e30
F32 = jnp.float32
BF16 = jnp.bfloat16
GELU_C = 0.7978845608028654
GELU_A = 0.044715

VMEM_SPEC = pl.BlockSpec(memory_space=pltpu.VMEM)
SMEM_SPEC = pl.BlockSpec(memory_space=pltpu.SMEM)
HBM_SPEC = pl.BlockSpec(memory_space=pltpu.HBM)


def mm(a, b):
    return jnp.dot(a, b, preferred_element_type=F32)


def mm_t(a, b):
    return lax.dot_general(a, b, (((1,), (1,)), ((), ())), preferred_element_type=F32)


def t_mm(a, b):
    return lax.dot_general(a, b, (((0,), (0,)), ((), ())), preferred_element_type=F32)


def shape(dims, dtype):
    return jax.ShapeDtypeStruct(dims, dtype)


def after(value, *others):
    return lax.optimization_barrier((value,) + others)[0]


COST = pl.CostEstimate(flops=1, bytes_accessed=1, transcendentals=0)


def in_hbm(value):
    return pltpu.with_memory_space_constraint(value, pltpu.HBM)


def params(mib):
    return pltpu.CompilerParams(vmem_limit_bytes=max(mib, 40) << 20)


def tiles(total, width, step):
    def body(j, carry):
        step(pl.ds(pl.multiple_of(j * width, width), width), j)
        return carry

    lax.fori_loop(0, total // width, body, 0)


def pick_kernel(order, onehot, values, out, buf, sems):
    routed = onehot.shape[1]
    count = buf.shape[0]
    copies = [
        pltpu.make_async_copy(values.at[order[i]], buf.at[i], sems.at[i]) for i in range(count)
    ]
    for copy in copies:
        copy.start()
    for i, copy in enumerate(copies):
        copy.wait()
        out[i * routed : (i + 1) * routed, :] = mm(onehot[order[i]], buf[i]).astype(BF16)


def pick_rows(values, onehot, order):
    count = order.shape[0]
    _, routed, span = onehot.shape
    width = values.shape[2]
    return pl.pallas_call(
        pick_kernel,
        in_specs=[SMEM_SPEC, VMEM_SPEC, HBM_SPEC],
        out_specs=VMEM_SPEC,
        out_shape=shape((count * routed, width), BF16),
        scratch_shapes=[
            pltpu.VMEM((count, span, width), BF16),
            pltpu.SemaphoreType.DMA((count,)),
        ],
        compiler_params=params(8),
        cost_estimate=COST,
        name="pick_rows",
    )(order, onehot, in_hbm(values))


def place_kernel(order, onehot_t, *refs, blocks):
    out, buf, sums, loads, stores = refs[-5:]
    row_refs = refs[:blocks]
    base = refs[blocks]
    count = buf.shape[0]
    routed = onehot_t.shape[2]
    found = [(ref, at) for ref in row_refs for at in range(0, ref.shape[0], routed)]
    reads = [
        pltpu.make_async_copy(base.at[order[i]], buf.at[i], loads.at[i]) for i in range(count)
    ]
    writes = [
        pltpu.make_async_copy(sums.at[i], out.at[order[i]], stores.at[i]) for i in range(count)
    ]
    for copy in reads:
        copy.start()
    for i in range(count):
        ref, at = found[i]
        rows = ref[at : at + routed, :]
        hot = onehot_t[order[i]]
        keep = 1.0 - jnp.sum(hot.astype(F32), axis=1, keepdims=True)
        reads[i].wait()
        sums[i] = buf[i] * keep.astype(BF16) + mm(hot, rows).astype(BF16)
        writes[i].start()
    for copy in writes:
        copy.wait()


def place_rows(base, onehot_t, rows, order, into=None):
    _, span, width = base.shape
    count = order.shape[0]
    extra = [] if into is None else [into]
    return pl.pallas_call(
        functools.partial(place_kernel, blocks=len(rows)),
        in_specs=[SMEM_SPEC, VMEM_SPEC]
        + [VMEM_SPEC] * len(rows)
        + [HBM_SPEC] * (1 + len(extra)),
        out_specs=HBM_SPEC,
        out_shape=shape(base.shape, BF16),
        scratch_shapes=[
            pltpu.VMEM((count, span, width), BF16),
            pltpu.VMEM((count, span, width), BF16),
            pltpu.SemaphoreType.DMA((count,)),
            pltpu.SemaphoreType.DMA((count,)),
        ],
        input_output_aliases={3 + len(rows): 0} if extra else {},
        compiler_params=params(8),
        cost_estimate=COST,
        name="place_rows",
    )(order, onehot_t, *rows, in_hbm(base), *extra)


def row_call(body, name, inputs, outputs, rows, width, steps=2):
    block = rows // steps
    in_specs = []
    for array, kind in inputs:
        if kind == "w":
            in_specs.append(pl.BlockSpec(array.shape, lambda i: (0, 0)))
        elif kind == "h":
            in_specs.append(pl.BlockSpec((block, array.shape[1]), lambda i: (0, 0)))
        else:
            in_specs.append(pl.BlockSpec((block, array.shape[1]), lambda i: (i, 0)))
    out_specs = []
    out_shapes = []
    for dims, dtype, kind in outputs:
        out_shapes.append(shape(dims, dtype))
        if kind == "w":
            out_specs.append(pl.BlockSpec(dims, lambda i: (0, 0)))
        else:
            out_specs.append(pl.BlockSpec((block, dims[1]), lambda i: (i, 0)))
    return pl.pallas_call(
        body,
        grid=(steps,),
        in_specs=in_specs,
        out_specs=out_specs,
        out_shape=out_shapes,
        compiler_params=params(10),
        cost_estimate=COST,
        name=name,
    )(*[array for array, _ in inputs])


def row_mean(x):
    return jnp.mean(x, axis=-1, keepdims=True)


def total3(a, b0, b1, c):
    b = jnp.where(pl.program_id(0) == 0, b0[...].astype(F32), b1[...].astype(F32))
    return a[...].astype(F32) + b + c[...].astype(F32)


def lanes(col):
    return jnp.broadcast_to(col, (col.shape[0], 128))


def fold(x):
    return jnp.sum(x.reshape(-1, 8, x.shape[1]), axis=0)


def accumulate(ref, value):
    @pl.when(pl.program_id(0) == 0)
    def _():
        ref[...] = value

    @pl.when(pl.program_id(0) > 0)
    def _():
        ref[...] += value


def first_norm_body(a, b0, b1, c, vec, rows_out, normed_out, gate_out):
    rows = total3(a, b0, b1, c)
    rows_out[...] = rows.astype(BF16)
    logit = jnp.sum(rows * vec[0:1, :], axis=-1, keepdims=True)
    gate_out[...] = lanes(jax.nn.sigmoid(logit))
    scale = lax.rsqrt(row_mean(rows * rows) + EPS)
    normed_out[...] = (rows * scale * vec[1:2, :]).astype(BF16)


def cot_body(a, b0, b1, c, gate, cot_out, grad_out):
    cot = total3(a, b0, b1, c)
    cot_out[...] = cot.astype(BF16)
    grad_out[...] = (cot * gate[:, 0:1]).astype(BF16)


def second_norm_body(rows, a, b0, b1, c, vec, attn_out, normed_out):
    attn = total3(a, b0, b1, c)
    attn_out[...] = attn
    hidden = rows[...].astype(F32) + attn
    scale = lax.rsqrt(row_mean(hidden * hidden) + EPS)
    normed_out[...] = (hidden * scale * vec[2:3, :]).astype(BF16)


def second_back_body(rows, attn, cot, gate, a, b0, b1, c, vec, grad_out, hidden_out, gain_out):
    second_grad = total3(a, b0, b1, c)
    hidden = rows[...].astype(F32) + attn[...]
    scale = lax.rsqrt(row_mean(hidden * hidden) + EPS)
    normal = hidden * scale
    grad = second_grad * vec[2:3, :]
    hidden_grad = scale * (grad - normal * row_mean(grad * normal))
    hidden_out[...] = hidden_grad
    grad_out[...] = (cot[...].astype(F32) * gate[:, 0:1] + hidden_grad).astype(BF16)
    accumulate(gain_out, fold(second_grad * normal))


def out_body(rows, attn, cot, gate, a, b0, b1, c, rows_out, gate_grad_out, router_out):
    branch = attn[...] + total3(a, b0, b1, c)
    x = rows[...].astype(F32)
    g = gate[:, 0:1]
    rows_out[...] = (x + g * branch).astype(BF16)
    gate_grad = jnp.sum(cot[...].astype(F32) * branch, axis=-1, keepdims=True) * g * (1.0 - g)
    gate_grad_out[...] = lanes(gate_grad)
    accumulate(router_out, fold(x * gate_grad))


def first_back_body(
    rows, cot, gate_grad, hidden_grad, a, b0, b1, c, vec, router_part, second_part, grad_out, vec_out, acc
):
    first_grad = total3(a, b0, b1, c)
    x = rows[...].astype(F32)
    scale = lax.rsqrt(row_mean(x * x) + EPS)
    normal = x * scale
    grad = first_grad * vec[1:2, :]
    norm_grad = scale * (grad - normal * row_mean(grad * normal))
    grad_out[...] = (
        cot[...].astype(F32) + gate_grad[:, 0:1] * vec[0:1, :] + hidden_grad[...] + norm_grad
    ).astype(BF16)
    accumulate(acc, fold(first_grad * normal))

    @pl.when(pl.program_id(0) == pl.num_programs(0) - 1)
    def _():
        vec_out[0:1, :] = jnp.sum(router_part[...], axis=0, keepdims=True)
        vec_out[1:2, :] = jnp.sum(acc[...], axis=0, keepdims=True)
        vec_out[2:3, :] = jnp.sum(second_part[...], axis=0, keepdims=True)
        vec_out[3:8, :] = jnp.zeros_like(vec_out[3:8, :])


def pack_mlp_kernel(up, down, out, buf, sems):
    depth = up.shape[0]
    copies = [
        pltpu.make_async_copy(up, out.at[0:depth, :], sems.at[0]),
        pltpu.make_async_copy(down, buf, sems.at[1]),
    ]
    for copy in copies:
        copy.start()
    copies[1].wait()
    out[depth : 2 * depth, :] = buf[...].T
    copies[0].wait()


def pack_attn_kernel(q, k, v, o, small, out, buf, sems):
    depth, local = q.shape
    copies = [
        pltpu.make_async_copy(
            x, out.at[0:depth, i * local : (i + 1) * local], sems.at[i]
        )
        for i, x in enumerate((q, k, v))
    ]
    copies.append(pltpu.make_async_copy(o, buf, sems.at[3]))
    for copy in copies:
        copy.start()
    out[depth:, :] = jnp.zeros_like(out[depth:, :])
    out[depth:, 0:depth] = small[...]
    copies[3].wait()
    out[0:depth, 3 * local : 4 * local] = buf[...].T
    for copy in copies[:3]:
        copy.wait()


def pack_mlp(up, down):
    return pl.pallas_call(
        pack_mlp_kernel,
        in_specs=[HBM_SPEC] * 2,
        out_specs=VMEM_SPEC,
        out_shape=shape((2 * up.shape[0], up.shape[1]), BF16),
        scratch_shapes=[pltpu.VMEM(down.shape, BF16), pltpu.SemaphoreType.DMA((2,))],
        compiler_params=params(4),
        cost_estimate=COST,
        name="pack_mlp",
    )(in_hbm(up), in_hbm(down))


def pack_attn(q, k, v, o, small):
    depth, local = q.shape
    return pl.pallas_call(
        pack_attn_kernel,
        in_specs=[HBM_SPEC] * 4 + [VMEM_SPEC],
        out_specs=VMEM_SPEC,
        out_shape=shape((depth + 16, 4 * local), BF16),
        scratch_shapes=[pltpu.VMEM(o.shape, BF16), pltpu.SemaphoreType.DMA((4,))],
        compiler_params=params(4),
        cost_estimate=COST,
        name="pack_attn",
    )(in_hbm(q), in_hbm(k), in_hbm(v), in_hbm(o), small)


def finish_mlp_kernel(total, up_out, down_out):
    depth = up_out.shape[0]
    total = total[...].astype(F32)
    up_out[...] = total[0:depth]
    down_out[...] = total[depth:].T


def finish_attn_kernel(own, got, p1, p2, p3, q_out, k_out, v_out, o_out):
    local = q_out.shape[1]
    total = own[...] + got[...].astype(F32)
    for part in (p1, p2, p3):
        total = total + part[...].astype(F32)
    q_out[...] = total[:, 0:local]
    k_out[...] = total[:, local : 2 * local]
    v_out[...] = total[:, 2 * local : 3 * local]
    o_out[...] = total[:, 3 * local :].T


def finish(body, name, dims, *arrays):
    return pl.pallas_call(
        body,
        in_specs=[VMEM_SPEC] * len(arrays),
        out_specs=[VMEM_SPEC] * len(dims),
        out_shape=[shape(d, F32) for d in dims],
        compiler_params=params(8),
        cost_estimate=COST,
        name=name,
    )(*arrays)


def join_kernel(places, *refs):
    *pieces, out, vec = refs
    depth = out.shape[0] // (len(pieces) - 1)
    vec[...] = jnp.zeros_like(vec)
    for number, piece in enumerate(pieces):
        if number > 0:
            out[(number - 1) * depth : number * depth, :] = piece[0:depth, :]
        place = places[number] * 2 + places[4]
        lanes_at = pl.ds(pl.multiple_of(place * depth, depth), depth)
        vec[:, lanes_at] = piece[depth : depth + 16, 0:depth]


def join(pieces, places, depth):
    width = pieces[0].shape[1]
    return pl.pallas_call(
        join_kernel,
        in_specs=[SMEM_SPEC] + [VMEM_SPEC] * len(pieces),
        out_specs=[VMEM_SPEC] * 2,
        out_shape=[
            shape((depth * (len(pieces) - 1), width), BF16),
            shape((16, width), BF16),
        ],
        compiler_params=params(6),
        cost_estimate=COST,
        name="join",
    )(places, *pieces)


def assemble_kernel(places, near_own, near, far_own, far, out):
    depth = 128
    for side, halves in enumerate(((near_own, near), (far_own, far))):
        for number in range(4):
            ref = halves[min(number, 1)]
            row = max(number - 1, 0) * depth
            place = places[number] * 2 + (places[4] ^ side)
            at = pl.multiple_of(place * depth, depth)
            out[pl.ds(at, depth), :] = ref[row : row + depth, :]


def assemble(near_own, near, far_own, far, places):
    rows, width = near.shape
    return pl.pallas_call(
        assemble_kernel,
        in_specs=[SMEM_SPEC] + [VMEM_SPEC] * 4,
        out_specs=VMEM_SPEC,
        out_shape=shape((rows * 8 // 3, width), BF16),
        compiler_params=params(6),
        cost_estimate=COST,
        name="assemble",
    )(places, near_own, near, far_own, far)


def head_masks(width):
    lane = lax.broadcasted_iota(jnp.int32, (1, width), 1) // HEAD_DIM
    return [(lane == h).astype(BF16) for h in range(width // HEAD_DIM)]


def spread(x, masks):
    return jnp.concatenate([x * mask for mask in masks], axis=0)


def side_by_side(x, count):
    rows = x.shape[0] // count
    return jnp.concatenate([x[h * rows : (h + 1) * rows] for h in range(count)], axis=1)


def seq_probs(q4, k, bias, count):
    scores = mm_t(q4, k) * (HEAD_DIM**-0.5)
    scores = scores + jnp.concatenate([bias] * count, axis=0)
    top = jnp.max(scores, axis=-1, keepdims=True)
    weight = jnp.exp(scores - top)
    return weight / jnp.sum(weight, axis=-1, keepdims=True)


def fill(ref, parts):
    at = 0
    for part in parts:
        ref[at : at + part.shape[0], :] = part[...]
        at += part.shape[0]


def attn_fwd_kernel(order, *refs, parts):
    w, bias, qkv, ctx, pa, pb, x = refs[parts:]
    fill(x, refs[:parts])
    half = pa.shape[0]
    local = ctx.shape[1]
    routed = bias.shape[1]
    heads = local // HEAD_DIM
    masks = head_masks(local)

    def project(cols, j):
        qkv[:, cols] = mm(x[...], w[:, cols]).astype(BF16)

    tiles(3 * local, local, project)

    def seq(rows, s):
        q = qkv[rows, 0:local]
        k = qkv[rows, local : 2 * local]
        v = qkv[rows, 2 * local : 3 * local]
        probs = seq_probs(spread(q, masks), k, bias[order[s]], heads).astype(BF16)
        ctx[rows, :] = mm(side_by_side(probs, heads), spread(v, masks)).astype(BF16)

    tiles(qkv.shape[0], routed, seq)

    def emit(cols, j):
        part = mm_t(ctx[...], w[cols, 3 * local : 4 * local]).astype(BF16)
        pa[:, cols] = part[0:half]
        pb[:, cols] = part[half:]

    tiles(pa.shape[1], 256, emit)


def attn_fwd(xa, xb, w, bias, order, local):
    rows, width = xa.shape
    return pl.pallas_call(
        functools.partial(attn_fwd_kernel, parts=1 + len(xb)),
        in_specs=[SMEM_SPEC] + [VMEM_SPEC] * (3 + len(xb)),
        out_specs=[VMEM_SPEC] * 4,
        out_shape=[
            shape((2 * rows, 3 * local), BF16),
            shape((2 * rows, local), BF16),
            shape((rows, width), BF16),
            shape((rows, width), BF16),
        ],
        scratch_shapes=[pltpu.VMEM((2 * rows, width), BF16)],
        compiler_params=params(12),
        cost_estimate=COST,
        name="attn_fwd",
    )(order, xa, *xb, w, bias)


def attn_bwd_kernel(order, *refs, parts):
    w, qkv, bias, dqkv, fa, fb, cg, g = refs[parts:]
    fill(g, refs[:parts])
    half = fa.shape[0]
    local = cg.shape[1]
    routed = bias.shape[1]
    heads = local // HEAD_DIM
    masks = head_masks(local)
    cg[...] = mm(g[...], w[:, 3 * local : 4 * local]).astype(BF16)

    def seq(rows, s):
        q4 = spread(qkv[rows, 0:local], masks)
        k = qkv[rows, local : 2 * local]
        v = qkv[rows, 2 * local : 3 * local]
        exact = seq_probs(q4, k, bias[order[s]], heads)
        c4 = spread(cg[rows, :], masks)
        prob_grad = mm_t(c4, v)
        dqkv[rows, 2 * local : 3 * local] = t_mm(exact.astype(BF16), c4).astype(BF16)
        inner = jnp.sum(exact * prob_grad, axis=-1, keepdims=True)
        score_grad = (exact * (prob_grad - inner)).astype(BF16)
        scale = HEAD_DIM**-0.5
        dq = mm(side_by_side(score_grad, heads), spread(k, masks)) * scale
        dqkv[rows, 0:local] = dq.astype(BF16)
        dqkv[rows, local : 2 * local] = (t_mm(score_grad, q4) * scale).astype(BF16)

    tiles(qkv.shape[0], routed, seq)

    def emit(cols, j):
        part = mm_t(dqkv[...], w[cols, 0 : 3 * local]).astype(BF16)
        fa[:, cols] = part[0:half]
        fb[:, cols] = part[half:]

    tiles(fa.shape[1], 256, emit)


def attn_bwd(ga, gb, w, qkv, bias, order, local):
    rows, width = ga.shape
    return pl.pallas_call(
        functools.partial(attn_bwd_kernel, parts=1 + len(gb)),
        in_specs=[SMEM_SPEC] + [VMEM_SPEC] * (4 + len(gb)),
        out_specs=[VMEM_SPEC] * 3,
        out_shape=[
            shape((2 * rows, 3 * local), BF16),
            shape((rows, width), BF16),
            shape((rows, width), BF16),
        ],
        scratch_shapes=[
            pltpu.VMEM((2 * rows, local), BF16),
            pltpu.VMEM((2 * rows, width), BF16),
        ],
        compiler_params=params(12),
        cost_estimate=COST,
        name="attn_bwd",
    )(order, ga, *gb, w, qkv, bias)


def mlp_kernel(*refs, parts):
    w, act, ug, da, db, ma, mb, n, g = refs[2 * parts :]
    fill(n, refs[:parts])
    fill(g, refs[parts : 2 * parts])
    rows, width = da.shape
    part, both, ff = w.shape
    depth = both // 2

    def up(cols, j):
        x = mm(n[...], w[:, 0:depth, cols].reshape(width, -1))
        inner = jnp.tanh(GELU_C * (x + GELU_A * (x * x * x)))
        half_in = 0.5 * (1.0 + inner)
        act[:, cols] = (x * half_in).astype(BF16)
        slope = half_in + (0.5 * GELU_C) * x * (1.0 - inner * inner) * (
            1.0 + (3.0 * GELU_A) * (x * x)
        )
        grad = mm(g[...], w[:, depth:both, cols].reshape(width, -1))
        ug[:, cols] = (grad * slope).astype(BF16)

    tiles(ff, 256, up)
    group = part * 256 // width

    def back(cols, j):
        wu = w[pl.ds(j * group, group), 0:depth, :].reshape(256, -1)
        out = mm_t(ug[...], wu).astype(BF16)
        da[:, cols] = out[0:rows]
        db[:, cols] = out[rows:]

    tiles(width, 256, back)

    def down(cols, j):
        wd = w[pl.ds(j * group, group), depth:both, :].reshape(256, -1)
        out = mm_t(act[...], wd).astype(BF16)
        ma[:, cols] = out[0:rows]
        mb[:, cols] = out[rows:]

    tiles(width, 256, down)


def mlp_both(na, nb, ga, gb, w):
    rows, width = na.shape
    ff = w.shape[2]
    return pl.pallas_call(
        functools.partial(mlp_kernel, parts=1 + len(nb)),
        in_specs=[VMEM_SPEC] * (3 + 2 * len(nb)),
        out_specs=[VMEM_SPEC] * 6,
        out_shape=[shape((2 * rows, ff), BF16)] * 2 + [shape((rows, width), BF16)] * 4,
        scratch_shapes=[pltpu.VMEM((2 * rows, width), BF16)] * 2,
        compiler_params=params(16),
        cost_estimate=COST,
        name="mlp",
    )(na, *nb, in_hbm(ga), *[in_hbm(x) for x in gb], in_hbm(w))


def turn(xt, pieces, cols):
    at = 0
    for piece in pieces:
        size = piece.shape[0]
        xt[:, at : at + size] = piece[:, cols].T
        at += size


def mlp_grads_kernel(*refs, depth, pieces):
    normed, grads = refs[:pieces], refs[pieces : 2 * pieces]
    un, uf, an, af, out, xt = refs[2 * pieces :]
    half = un.shape[0]
    width = normed[0].shape[1]
    for side, (xs, near, far) in enumerate(((normed, un, uf), (grads, an, af))):
        tiles(
            width,
            256,
            lambda cols, j, xs=xs: turn(
                xt.at[pl.ds(pl.multiple_of(j * 256, 256), 256), :], xs, cols
            ),
        )

        def block(ncols, j, near=near, far=far, side=side):
            total = mm(xt[:, 0:half], near[:, ncols]) + mm(xt[:, half:], far[:, ncols])
            for f in range(width // depth):
                at = (2 * f + side) * depth
                out[at : at + depth, ncols] = total[f * depth : (f + 1) * depth].astype(BF16)

        tiles(near.shape[1], 256, block)


def mlp_grads(normed, grads, ug, act, depth):
    width = normed[0].shape[1]
    rows, ff = ug[0].shape
    return pl.pallas_call(
        functools.partial(mlp_grads_kernel, depth=depth, pieces=len(normed)),
        in_specs=[VMEM_SPEC] * (2 * len(normed) + 4),
        out_specs=VMEM_SPEC,
        out_shape=shape((2 * width, ff), BF16),
        scratch_shapes=[pltpu.VMEM((width, 2 * rows), BF16)],
        compiler_params=params(20),
        cost_estimate=COST,
        name="mlp_grads",
    )(*normed, *grads, *ug, *act)


def attn_grads_kernel(info, *refs, pieces):
    normed, grads = refs[:pieces], refs[pieces : 2 * pieces]
    dn, df, cn, cf, first, others, *keeps, xt = refs[2 * pieces :]
    half = dn.shape[0]
    local = cn.shape[1]
    depth = first.shape[0]
    count = len(keeps)
    low = info[count] == 0
    for lane, wide, xs, near, far in (
        (0, 3 * local, normed, dn, df),
        (3 * local, local, grads, cn, cf),
    ):
        for o in range(count):
            cols = pl.ds(pl.multiple_of(info[o] * 256, 256), 256)
            turn(xt.at[o * 256 : (o + 1) * 256, :], xs, cols)

        def block(ncols, j, near=near, far=far, lane=lane):
            total = mm(xt[:, 0:half], near[:, ncols]) + mm(xt[:, half:], far[:, ncols])
            dst = pl.ds(pl.multiple_of(j * 256, 256) + lane, 256)
            for o in range(count):
                one = total[o * 256 : o * 256 + depth]
                two = total[o * 256 + depth : (o + 1) * 256]
                send, row = (first, 0) if o == 0 else (others, (o - 1) * depth)
                send[row : row + depth, dst] = jnp.where(low, two, one).astype(BF16)
                keeps[o][:, dst] = jnp.where(low, one, two)

        tiles(wide, 256, block)


def attn_grads(normed, grads, dqkv, ctx, info, depth):
    rows, local = ctx[0].shape
    count = info.shape[0] - 1
    first, others, *keeps = pl.pallas_call(
        functools.partial(attn_grads_kernel, pieces=len(normed)),
        in_specs=[SMEM_SPEC] + [VMEM_SPEC] * (2 * len(normed) + 4),
        out_specs=[VMEM_SPEC] * (2 + count),
        out_shape=[
            shape((depth, 4 * local), BF16),
            shape(((count - 1) * depth, 4 * local), BF16),
        ]
        + [shape((depth, 4 * local), F32)] * count,
        scratch_shapes=[pltpu.VMEM((count * 256, 2 * rows), BF16)],
        compiler_params=params(14),
        cost_estimate=COST,
        name="attn_grads",
    )(info, *normed, *grads, *dqkv, *ctx)
    return first, others, keeps


def swap(x, axis, mask):
    size = lax.axis_size(axis)
    return lax.ppermute(x, axis, [(i, i ^ mask) for i in range(size)])


def halves(x):
    step = x.shape[0] // 2
    return x[:step], x[step:]


def pair_swap(x):
    return tuple(swap(h, "tensor", 1) for h in halves(x))


def pair_sum(near, diag):
    return jnp.concatenate(
        [
            (n.astype(F32) + g.astype(F32)).astype(BF16)
            for n, g in zip(halves(near), pair_swap(diag))
        ],
        axis=0,
    )


def z_perm(size, shift):
    places = size // 2
    return [((f // 2 + shift) % places * 2 + f % 2, f) for f in range(size)]


def z_move(x, shift):
    return lax.ppermute(x, "fsdp", z_perm(lax.axis_size("fsdp"), shift))


SHIFTS = (2, 1, 3)


def shards(
    tokens,
    cotangent,
    routed_index,
    query_weight,
    key_weight,
    value_weight,
    output_weight,
    up_weight,
    down_weight,
    router_weight,
    attn_gain,
    mlp_gain,
):
    fsdp = lax.axis_size("fsdp")
    grid = fsdp == 8
    me_f = lax.axis_index("fsdp")
    me_t = lax.axis_index("tensor")
    seqs, span, width = tokens.shape
    routed = routed_index.shape[1]
    per = seqs // lax.axis_size("tensor")
    local = query_weight.shape[1]
    depth = query_weight.shape[0]
    ff = up_weight.shape[1]
    rows = per * routed

    place = routed_index - me_t * span
    positions = jnp.arange(span, dtype=jnp.int32)
    onehot = (place[:, :, None] == positions[None, None, :]).astype(BF16)
    order = jnp.stack([(me_t ^ m) * per + j for m in range(4) for j in range(per)])
    order_keep = jnp.concatenate([order[0:per], order[2 * per : 3 * per]])
    order_send = jnp.concatenate([order[per : 2 * per], order[3 * per :]])
    order_near = order[: 2 * per]
    order_far = order[2 * per :]

    row_shape = ((rows, width), BF16, "r")
    f32_shape = ((rows, width), F32, "r")
    gate_shape = ((rows, 128), F32, "r")
    vec_shape = ((8, width), F32, "w")

    def row_step(body, name, ins, outs):
        return row_call(body, name, ins, outs, rows, width)

    def r(*arrays):
        found = []
        for a in arrays:
            found += [(h, "h") for h in a] if isinstance(a, tuple) else [(a, "r")]
        return found

    zi = me_f // 2
    yi = me_f % 2

    small = jnp.stack([router_weight, attn_gain, mlp_gain])
    if grid:
        small = jnp.concatenate([small, jnp.zeros((13, depth), BF16)], axis=0)
        attn_piece = pack_attn(query_weight, key_weight, value_weight, output_weight, small)
        z_pieces = [z_move(attn_piece, o) for o in SHIFTS]
        far_own = swap(attn_piece, "fsdp", 1)
        z_at = jnp.stack([zi] + [(zi + o) % (fsdp // 2) for o in SHIFTS] + [yi])
    else:
        attn_piece = jnp.concatenate(
            [query_weight, key_weight, value_weight, output_weight.T], axis=1
        )
        z_pieces = []
        vec = lax.all_gather(small, "fsdp", axis=1, tiled=True)
        vec = jnp.concatenate([vec, jnp.zeros((5, width), BF16)], axis=0).astype(F32)
    tok_send = pick_rows(tokens, onehot, after(order_send, attn_piece))
    tok_got = pair_swap(tok_send)
    tok_keep = pick_rows(tokens, onehot, after(order_keep, tok_send))
    tok_sum = tok_keep[rows:] + tok_got[1]
    tok_far = [swap(h, "tensor", 2) for h in halves(tok_sum)]
    cot_send = pick_rows(cotangent, onehot, after(order_send, tok_sum))
    cot_got = pair_swap(cot_send)
    cot_keep = pick_rows(cotangent, onehot, after(order_keep, cot_send))
    cot_sum = cot_keep[rows:] + cot_got[1]
    cot_far = [swap(h, "tensor", 2) for h in halves(cot_sum)]
    if grid:
        mlp_piece = pack_mlp(up_weight, after(down_weight, cot_keep))
        gated = [after(z, mlp_piece, *tok_far, *cot_far) for z in z_pieces]
        near_w, vec_near = join([attn_piece] + gated, z_at, depth)
        vec = vec_near + swap(vec_near, "fsdp", 1)
        far_w = swap(after(near_w, vec), "fsdp", 1)
        vec = vec[0:8].astype(F32)
        mlp_piece = after(mlp_piece, near_w)
    else:
        mlp_piece = jnp.concatenate([up_weight, down_weight.T], axis=0)
    up_down = lax.all_gather(mlp_piece, "fsdp", axis=0, tiled=True)
    up_down = up_down.reshape(fsdp, 2 * depth, ff)

    def with_halves(body):
        def whole(keep, got, far0, far1, *rest):
            far = jnp.where(pl.program_id(0) == 0, far0[...], far1[...])
            return body(keep, got, got, far, *rest)

        return whole

    own_rows, n0, gate = row_step(
        with_halves(first_norm_body),
        "first_norm",
        [(tok_keep, "r"), (tok_got[0], "r")] + r(tuple(tok_far)) + [(vec, "w")],
        [row_shape, row_shape, gate_shape],
    )
    n2 = swap(n0, "tensor", 2)
    n1 = swap(n0, "tensor", 1)
    cot, g0 = row_step(
        with_halves(cot_body),
        "cot_rows",
        [(cot_keep, "r"), (cot_got[0], "r")] + r(tuple(cot_far)) + [(after(gate, n0), "r")],
        [row_shape, row_shape],
    )
    g2 = swap(after(g0, n2), "tensor", 2)
    g1 = swap(g0, "tensor", 1)
    blocks = after(routed_index, g0) // BLOCK
    bias = jnp.where(blocks[:, None, :] <= blocks[:, :, None], 0.0, NEG).astype(F32)
    if grid:
        attn_w = assemble(attn_piece, after(near_w, g0), far_own, far_w, z_at)
    else:
        attn_w = lax.all_gather(attn_piece, "fsdp", axis=0, tiled=True)
    n3 = pair_swap(after(n2, attn_w))

    qkv_far, ctx_far, p2, p3 = attn_fwd(
        after(n2, g2), n3, attn_w, bias, order_far, local
    )
    attn_sum = pair_sum(p2, p3)
    attn_x = swap(attn_sum, "tensor", 2)
    qkv_near, ctx_near, p0, p1 = attn_fwd(
        after(n0, attn_sum), (n1,), attn_w, bias, order_near, local
    )
    attn_c = pair_swap(p1)
    attn, s0 = row_step(
        second_norm_body,
        "second_norm",
        r(own_rows, p0, attn_c, attn_x) + [(vec, "w")],
        [f32_shape, row_shape],
    )
    s2 = swap(s0, "tensor", 2)
    s1 = swap(s0, "tensor", 1)
    s3 = pair_swap(s2)
    g3 = pair_swap(after(g2, s0))

    act_far, ug_far, d2, d3, m2, m3 = mlp_both(s2, s3, g2, g3, up_down)
    second_sum = pair_sum(d2, d3)
    second_x = swap(second_sum, "tensor", 2)
    act_near, ug_near, d0, d1, m0, m1 = mlp_both(
        after(s0, second_sum), (s1,), g0, (g1,), up_down
    )
    second_c = pair_swap(d1)

    attn_grad, hidden_grad, second_part = row_step(
        second_back_body,
        "second_back",
        r(own_rows, attn, cot, gate, d0, second_c, second_x) + [(vec, "w")],
        [row_shape, f32_shape, vec_shape],
    )
    a0 = attn_grad
    a2 = swap(a0, "tensor", 2)
    a1 = swap(a0, "tensor", 1)
    mlp_all = mlp_grads(
        (after(s0, a0), s1, s2, *s3),
        (g0, g1, g2, *g3),
        (ug_near, ug_far),
        (act_near, act_far),
        depth,
    )
    a2 = after(a2, mlp_all)
    mlp_total = lax.psum_scatter(after(mlp_all, a2), "fsdp", scatter_dimension=0, tiled=True)
    a3 = pair_swap(a2)
    mlp_c = pair_swap(after(m1, mlp_all))
    mlp_sum = pair_sum(m2, after(m3, mlp_all))
    mlp_x = swap(after(mlp_sum, a2), "tensor", 2)

    def to_z(keep, got, shift):
        return z_move((keep + got.astype(F32)).astype(BF16), 4 - shift)

    dqkv_far, f2, f3 = attn_bwd(a2, a3, attn_w, qkv_far, bias, order_far, local)
    first_sum = pair_sum(f2, f3)
    first_x = swap(first_sum, "tensor", 2)
    dqkv_near, f0, f1 = attn_bwd(
        after(a0, first_sum), (a1,), attn_w, qkv_near, bias, order_near, local
    )
    first_c = pair_swap(f1)
    out_rows, gate_grad, router_part = row_step(
        out_body,
        "out_rows",
        r(own_rows, attn, cot, gate, m0, mlp_c, after(mlp_x, f1)),
        [row_shape, gate_shape, vec_shape],
    )
    o2 = swap(out_rows, "tensor", 2)
    o1 = swap(out_rows, "tensor", 1)

    attn_args = (
        (n0, n1, n2, *n3),
        (a0, a1, a2, *a3),
        (dqkv_near, dqkv_far),
        (ctx_near, ctx_far),
    )
    if grid:
        info = jnp.stack([(zi + o) % (fsdp // 2) for o in SHIFTS + (0,)] + [yi])
        first_b, other_b, keeps = attn_grads(*attn_args, after(info, out_rows), depth)
        first_y = swap(first_b, "fsdp", 1)
        other_y = swap(other_b, "fsdp", 1)
        first_x = after(first_x, first_b)

    half = rows // 2
    grad_rows, vec_part = pl.pallas_call(
        first_back_body,
        grid=(2,),
        in_specs=[
            pl.BlockSpec((half, width), lambda i: (i, 0)),
            pl.BlockSpec((half, width), lambda i: (i, 0)),
            pl.BlockSpec((half, 128), lambda i: (i, 0)),
        ]
        + [pl.BlockSpec((half, width), lambda i: (i, 0))] * 2
        + [pl.BlockSpec((half, width), lambda i: (0, 0))] * 2
        + [pl.BlockSpec((half, width), lambda i: (i, 0))]
        + [pl.BlockSpec((8, width), lambda i: (0, 0))] * 3,
        out_specs=[
            pl.BlockSpec((half, width), lambda i: (i, 0)),
            pl.BlockSpec((8, width), lambda i: (0, 0)),
        ],
        out_shape=[shape((rows, width), BF16), shape((8, width), F32)],
        scratch_shapes=[pltpu.VMEM((8, width), F32)],
        compiler_params=params(12),
        cost_estimate=COST,
        name="first_back",
    )(own_rows, cot, gate_grad, hidden_grad, f0, *first_c, first_x, vec, router_part, second_part)
    t2 = swap(grad_rows, "tensor", 2)
    t1 = swap(grad_rows, "tensor", 1)
    onehot_t = (
        after(place, grad_rows)[:, None, :] == positions[None, :, None]
    ).astype(BF16)
    o3 = pair_swap(after(o2, grad_rows))
    mixed = place_rows(tokens, onehot_t, [after(out_rows, grad_rows), o1], order_near)
    if grid:
        z_first = to_z(keeps[0], after(first_y, grad_rows), SHIFTS[0])
    mixed = place_rows(tokens, onehot_t, [o2, *o3], order_far, mixed)
    near_gate = mixed
    if grid:
        other_y = after(other_y, near_gate)
        z_second = to_z(keeps[1], other_y[0:depth], SHIFTS[1])
        z_third = to_z(keeps[2], other_y[depth : 2 * depth], SHIFTS[2])
    token_grad = place_rows(cotangent, onehot_t, [after(grad_rows, near_gate), t1], order_near)
    t3 = pair_swap(after(t2, token_grad))
    token_grad = place_rows(cotangent, onehot_t, [t2, *t3], order_far, token_grad)
    up_grad, down_grad = finish(
        finish_mlp_kernel, "finish_mlp", [(depth, ff), (ff, depth)], after(mlp_total, token_grad)
    )

    if grid:
        vec_sum = vec_part
        for axis, mask in (("tensor", 1), ("tensor", 2)):
            vec_sum = vec_sum + swap(vec_sum, axis, mask)
        vec_sum = vec_sum + after(swap(vec_sum, "fsdp", 1), token_grad)
        vec_sum = vec_sum + z_move(vec_sum, 1) + z_move(vec_sum, 3) + z_move(vec_sum, 2)
        wide = (depth, local)
        attn_out = finish(
            finish_attn_kernel,
            "finish_attn",
            [wide, wide, wide, (local, depth)],
            keeps[3],
            after(other_y[2 * depth :], token_grad),
            z_first,
            z_second,
            z_third,
        )
    else:

        def reduced(xs, ys):
            x = t_mm(jnp.concatenate(xs, axis=0), jnp.concatenate(ys, axis=0))
            return lax.psum_scatter(x, "fsdp", scatter_dimension=0, tiled=True)

        qkv_grad = reduced(attn_args[0], attn_args[2])
        o_grad = reduced(attn_args[1], attn_args[3])
        attn_out = jnp.split(qkv_grad, 3, axis=1) + [o_grad.T]
        vec_sum = lax.psum(vec_part, ("fsdp", "tensor"))
    vec_own = lax.dynamic_slice(vec_sum, (0, me_f * depth), (3, depth))

    return (mixed, token_grad, *attn_out, up_grad, down_grad, vec_own[0], vec_own[1], vec_own[2])


def solution(mesh):
    in_specs = (
        P("fsdp", "tensor", None),
        P("fsdp", "tensor", None),
        P("fsdp", None),
        P("fsdp", "tensor"),
        P("fsdp", "tensor"),
        P("fsdp", "tensor"),
        P("tensor", "fsdp"),
        P("fsdp", "tensor"),
        P("tensor", "fsdp"),
        P("fsdp"),
        P("fsdp"),
        P("fsdp"),
    )
    out_specs = (
        P("fsdp", "tensor", None),
        P("fsdp", "tensor", None),
        P("fsdp", "tensor"),
        P("fsdp", "tensor"),
        P("fsdp", "tensor"),
        P("tensor", "fsdp"),
        P("fsdp", "tensor"),
        P("tensor", "fsdp"),
        P("fsdp"),
        P("fsdp"),
        P("fsdp"),
    )
    return jax.shard_map(shards, mesh=mesh, in_specs=in_specs, out_specs=out_specs, check_vma=False)
```

```python
import functools

import jax
import jax.numpy as jnp
from jax import lax
from jax.experimental import pallas as pl
from jax.experimental.pallas import tpu as pltpu
from jax.sharding import PartitionSpec as P

HEAD_DIM = 64
BLOCK = 256
EPS = 1e-06
NEG = -1e30
F32 = jnp.float32
BF16 = jnp.bfloat16
GELU_C = 0.7978845608028654
GELU_A = 0.044715

VMEM_SPEC = pl.BlockSpec(memory_space=pltpu.VMEM)
SMEM_SPEC = pl.BlockSpec(memory_space=pltpu.SMEM)
HBM_SPEC = pl.BlockSpec(memory_space=pltpu.HBM)


def mm(a, b):
    return jnp.dot(a, b, preferred_element_type=F32)


def mm_t(a, b):
    return lax.dot_general(a, b, (((1,), (1,)), ((), ())), preferred_element_type=F32)


def t_mm(a, b):
    return lax.dot_general(a, b, (((0,), (0,)), ((), ())), preferred_element_type=F32)


def shape(dims, dtype):
    return jax.ShapeDtypeStruct(dims, dtype)


def after(value, *others):
    return lax.optimization_barrier((value,) + others)[0]


COST = pl.CostEstimate(flops=1, bytes_accessed=1, transcendentals=0)


def in_hbm(value):
    return pltpu.with_memory_space_constraint(value, pltpu.HBM)


def params(mib):
    return pltpu.CompilerParams(vmem_limit_bytes=max(mib, 40) << 20)


def tiles(total, width, step):
    def body(j, carry):
        step(pl.ds(pl.multiple_of(j * width, width), width), j)
        return carry

    lax.fori_loop(0, total // width, body, 0)


def pick_kernel(order, onehot, values, out, buf, sems):
    routed = onehot.shape[1]
    count = buf.shape[0]
    copies = [
        pltpu.make_async_copy(values.at[order[i]], buf.at[i], sems.at[i]) for i in range(count)
    ]
    for copy in copies:
        copy.start()
    for i, copy in enumerate(copies):
        copy.wait()
        out[i * routed : (i + 1) * routed, :] = mm(onehot[order[i]], buf[i]).astype(BF16)


def pick_rows(values, onehot, order):
    count = order.shape[0]
    _, routed, span = onehot.shape
    width = values.shape[2]
    return pl.pallas_call(
        pick_kernel,
        in_specs=[SMEM_SPEC, VMEM_SPEC, HBM_SPEC],
        out_specs=VMEM_SPEC,
        out_shape=shape((count * routed, width), BF16),
        scratch_shapes=[
            pltpu.VMEM((count, span, width), BF16),
            pltpu.SemaphoreType.DMA((count,)),
        ],
        compiler_params=params(8),
        cost_estimate=COST,
        name="pick_rows",
    )(order, onehot, in_hbm(values))


def place_kernel(order, onehot_t, *refs, blocks):
    out, buf, sums, loads, stores = refs[-5:]
    row_refs = refs[:blocks]
    base = refs[blocks]
    count = buf.shape[0]
    routed = onehot_t.shape[2]
    found = [(ref, at) for ref in row_refs for at in range(0, ref.shape[0], routed)]
    reads = [
        pltpu.make_async_copy(base.at[order[i]], buf.at[i], loads.at[i]) for i in range(count)
    ]
    writes = [
        pltpu.make_async_copy(sums.at[i], out.at[order[i]], stores.at[i]) for i in range(count)
    ]
    for copy in reads:
        copy.start()
    for i in range(count):
        ref, at = found[i]
        rows = ref[at : at + routed, :]
        hot = onehot_t[order[i]]
        keep = 1.0 - jnp.sum(hot.astype(F32), axis=1, keepdims=True)
        reads[i].wait()
        sums[i] = buf[i] * keep.astype(BF16) + mm(hot, rows).astype(BF16)
        writes[i].start()
    for copy in writes:
        copy.wait()


def place_rows(base, onehot_t, rows, order, into=None):
    _, span, width = base.shape
    count = order.shape[0]
    extra = [] if into is None else [into]
    return pl.pallas_call(
        functools.partial(place_kernel, blocks=len(rows)),
        in_specs=[SMEM_SPEC, VMEM_SPEC]
        + [VMEM_SPEC] * len(rows)
        + [HBM_SPEC] * (1 + len(extra)),
        out_specs=HBM_SPEC,
        out_shape=shape(base.shape, BF16),
        scratch_shapes=[
            pltpu.VMEM((count, span, width), BF16),
            pltpu.VMEM((count, span, width), BF16),
            pltpu.SemaphoreType.DMA((count,)),
            pltpu.SemaphoreType.DMA((count,)),
        ],
        input_output_aliases={3 + len(rows): 0} if extra else {},
        compiler_params=params(8),
        cost_estimate=COST,
        name="place_rows",
    )(order, onehot_t, *rows, in_hbm(base), *extra)


def row_call(body, name, inputs, outputs, rows, width, steps=2):
    block = rows // steps
    in_specs = []
    for array, kind in inputs:
        if kind == "w":
            in_specs.append(pl.BlockSpec(array.shape, lambda i: (0, 0)))
        elif kind == "h":
            in_specs.append(pl.BlockSpec((block, array.shape[1]), lambda i: (0, 0)))
        else:
            in_specs.append(pl.BlockSpec((block, array.shape[1]), lambda i: (i, 0)))
    out_specs = []
    out_shapes = []
    for dims, dtype, kind in outputs:
        out_shapes.append(shape(dims, dtype))
        if kind == "w":
            out_specs.append(pl.BlockSpec(dims, lambda i: (0, 0)))
        else:
            out_specs.append(pl.BlockSpec((block, dims[1]), lambda i: (i, 0)))
    return pl.pallas_call(
        body,
        grid=(steps,),
        in_specs=in_specs,
        out_specs=out_specs,
        out_shape=out_shapes,
        compiler_params=params(10),
        cost_estimate=COST,
        name=name,
    )(*[array for array, _ in inputs])


def row_mean(x):
    return jnp.mean(x, axis=-1, keepdims=True)


def total3(a, b0, b1, c):
    b = jnp.where(pl.program_id(0) == 0, b0[...].astype(F32), b1[...].astype(F32))
    return a[...].astype(F32) + b + c[...].astype(F32)


def lanes(col):
    return jnp.broadcast_to(col, (col.shape[0], 128))


def fold(x):
    return jnp.sum(x.reshape(-1, 8, x.shape[1]), axis=0)


def accumulate(ref, value):
    @pl.when(pl.program_id(0) == 0)
    def _():
        ref[...] = value

    @pl.when(pl.program_id(0) > 0)
    def _():
        ref[...] += value


def first_norm_body(a, b0, b1, c, vec, rows_out, normed_out, gate_out):
    rows = total3(a, b0, b1, c)
    rows_out[...] = rows.astype(BF16)
    logit = jnp.sum(rows * vec[0:1, :], axis=-1, keepdims=True)
    gate_out[...] = lanes(jax.nn.sigmoid(logit))
    scale = lax.rsqrt(row_mean(rows * rows) + EPS)
    normed_out[...] = (rows * scale * vec[1:2, :]).astype(BF16)


def cot_body(a, b0, b1, c, gate, cot_out, grad_out):
    cot = total3(a, b0, b1, c)
    cot_out[...] = cot.astype(BF16)
    grad_out[...] = (cot * gate[:, 0:1]).astype(BF16)


def second_norm_body(rows, a, b0, b1, c, vec, attn_out, normed_out):
    attn = total3(a, b0, b1, c)
    attn_out[...] = attn
    hidden = rows[...].astype(F32) + attn
    scale = lax.rsqrt(row_mean(hidden * hidden) + EPS)
    normed_out[...] = (hidden * scale * vec[2:3, :]).astype(BF16)


def second_back_body(rows, attn, cot, gate, a, b0, b1, c, vec, grad_out, hidden_out, gain_out):
    second_grad = total3(a, b0, b1, c)
    hidden = rows[...].astype(F32) + attn[...]
    scale = lax.rsqrt(row_mean(hidden * hidden) + EPS)
    normal = hidden * scale
    grad = second_grad * vec[2:3, :]
    hidden_grad = scale * (grad - normal * row_mean(grad * normal))
    hidden_out[...] = hidden_grad
    grad_out[...] = (cot[...].astype(F32) * gate[:, 0:1] + hidden_grad).astype(BF16)
    accumulate(gain_out, fold(second_grad * normal))


def out_body(rows, attn, cot, gate, a, b0, b1, c, rows_out, gate_grad_out, router_out):
    branch = attn[...] + total3(a, b0, b1, c)
    x = rows[...].astype(F32)
    g = gate[:, 0:1]
    rows_out[...] = (x + g * branch).astype(BF16)
    gate_grad = jnp.sum(cot[...].astype(F32) * branch, axis=-1, keepdims=True) * g * (1.0 - g)
    gate_grad_out[...] = lanes(gate_grad)
    accumulate(router_out, fold(x * gate_grad))


def first_back_body(
    rows, cot, gate_grad, hidden_grad, a, b0, b1, c, vec, router_part, second_part, grad_out, vec_out, acc
):
    first_grad = total3(a, b0, b1, c)
    x = rows[...].astype(F32)
    scale = lax.rsqrt(row_mean(x * x) + EPS)
    normal = x * scale
    grad = first_grad * vec[1:2, :]
    norm_grad = scale * (grad - normal * row_mean(grad * normal))
    grad_out[...] = (
        cot[...].astype(F32) + gate_grad[:, 0:1] * vec[0:1, :] + hidden_grad[...] + norm_grad
    ).astype(BF16)
    accumulate(acc, fold(first_grad * normal))

    @pl.when(pl.program_id(0) == pl.num_programs(0) - 1)
    def _():
        vec_out[0:1, :] = jnp.sum(router_part[...], axis=0, keepdims=True)
        vec_out[1:2, :] = jnp.sum(acc[...], axis=0, keepdims=True)
        vec_out[2:3, :] = jnp.sum(second_part[...], axis=0, keepdims=True)
        vec_out[3:8, :] = jnp.zeros_like(vec_out[3:8, :])


def pack_mlp_kernel(up, down, out, buf, sems):
    depth = up.shape[0]
    copies = [
        pltpu.make_async_copy(up, out.at[0:depth, :], sems.at[0]),
        pltpu.make_async_copy(down, buf, sems.at[1]),
    ]
    for copy in copies:
        copy.start()
    copies[1].wait()
    out[depth : 2 * depth, :] = buf[...].T
    copies[0].wait()


def pack_attn_kernel(q, k, v, o, small, out, buf, sems):
    depth, local = q.shape
    copies = [
        pltpu.make_async_copy(
            x, out.at[0:depth, i * local : (i + 1) * local], sems.at[i]
        )
        for i, x in enumerate((q, k, v))
    ]
    copies.append(pltpu.make_async_copy(o, buf, sems.at[3]))
    for copy in copies:
        copy.start()
    out[depth:, :] = jnp.zeros_like(out[depth:, :])
    out[depth:, 0:depth] = small[...]
    copies[3].wait()
    out[0:depth, 3 * local : 4 * local] = buf[...].T
    for copy in copies[:3]:
        copy.wait()


def pack_mlp(up, down):
    return pl.pallas_call(
        pack_mlp_kernel,
        in_specs=[HBM_SPEC] * 2,
        out_specs=VMEM_SPEC,
        out_shape=shape((2 * up.shape[0], up.shape[1]), BF16),
        scratch_shapes=[pltpu.VMEM(down.shape, BF16), pltpu.SemaphoreType.DMA((2,))],
        compiler_params=params(4),
        cost_estimate=COST,
        name="pack_mlp",
    )(in_hbm(up), in_hbm(down))


def pack_attn(q, k, v, o, small):
    depth, local = q.shape
    return pl.pallas_call(
        pack_attn_kernel,
        in_specs=[HBM_SPEC] * 4 + [VMEM_SPEC],
        out_specs=VMEM_SPEC,
        out_shape=shape((depth + 16, 4 * local), BF16),
        scratch_shapes=[pltpu.VMEM(o.shape, BF16), pltpu.SemaphoreType.DMA((4,))],
        compiler_params=params(4),
        cost_estimate=COST,
        name="pack_attn",
    )(in_hbm(q), in_hbm(k), in_hbm(v), in_hbm(o), small)


def finish_mlp_kernel(total, up_out, down_out):
    depth = up_out.shape[0]
    total = total[...].astype(F32)
    up_out[...] = total[0:depth]
    down_out[...] = total[depth:].T


def finish_attn_kernel(own, got, p1, p2, p3, q_out, k_out, v_out, o_out):
    local = q_out.shape[1]
    total = own[...] + got[...].astype(F32)
    for part in (p1, p2, p3):
        total = total + part[...].astype(F32)
    q_out[...] = total[:, 0:local]
    k_out[...] = total[:, local : 2 * local]
    v_out[...] = total[:, 2 * local : 3 * local]
    o_out[...] = total[:, 3 * local :].T


def finish(body, name, dims, *arrays):
    return pl.pallas_call(
        body,
        in_specs=[VMEM_SPEC] * len(arrays),
        out_specs=[VMEM_SPEC] * len(dims),
        out_shape=[shape(d, F32) for d in dims],
        compiler_params=params(8),
        cost_estimate=COST,
        name=name,
    )(*arrays)


def join_kernel(places, *refs):
    *pieces, out, vec = refs
    depth = out.shape[0] // (len(pieces) - 1)
    vec[...] = jnp.zeros_like(vec)
    for number, piece in enumerate(pieces):
        if number > 0:
            out[(number - 1) * depth : number * depth, :] = piece[0:depth, :]
        place = places[number] * 2 + places[4]
        lanes_at = pl.ds(pl.multiple_of(place * depth, depth), depth)
        vec[:, lanes_at] = piece[depth : depth + 16, 0:depth]


def join(pieces, places, depth):
    width = pieces[0].shape[1]
    return pl.pallas_call(
        join_kernel,
        in_specs=[SMEM_SPEC] + [VMEM_SPEC] * len(pieces),
        out_specs=[VMEM_SPEC] * 2,
        out_shape=[
            shape((depth * (len(pieces) - 1), width), BF16),
            shape((16, width), BF16),
        ],
        compiler_params=params(6),
        cost_estimate=COST,
        name="join",
    )(places, *pieces)


def assemble_kernel(places, near_own, near, far_own, far, out):
    depth = 128
    for side, halves in enumerate(((near_own, near), (far_own, far))):
        for number in range(4):
            ref = halves[min(number, 1)]
            row = max(number - 1, 0) * depth
            place = places[number] * 2 + (places[4] ^ side)
            at = pl.multiple_of(place * depth, depth)
            out[pl.ds(at, depth), :] = ref[row : row + depth, :]


def assemble(near_own, near, far_own, far, places):
    rows, width = near.shape
    return pl.pallas_call(
        assemble_kernel,
        in_specs=[SMEM_SPEC] + [VMEM_SPEC] * 4,
        out_specs=VMEM_SPEC,
        out_shape=shape((rows * 8 // 3, width), BF16),
        compiler_params=params(6),
        cost_estimate=COST,
        name="assemble",
    )(places, near_own, near, far_own, far)


def head_masks(width):
    lane = lax.broadcasted_iota(jnp.int32, (1, width), 1) // HEAD_DIM
    return [(lane == h).astype(BF16) for h in range(width // HEAD_DIM)]


def spread(x, masks):
    return jnp.concatenate([x * mask for mask in masks], axis=0)


def side_by_side(x, count):
    rows = x.shape[0] // count
    return jnp.concatenate([x[h * rows : (h + 1) * rows] for h in range(count)], axis=1)


def seq_probs(q4, k, bias, count):
    scores = mm_t(q4, k) * (HEAD_DIM**-0.5)
    scores = scores + jnp.concatenate([bias] * count, axis=0)
    top = jnp.max(scores, axis=-1, keepdims=True)
    weight = jnp.exp(scores - top)
    return weight / jnp.sum(weight, axis=-1, keepdims=True)


def fill(ref, parts):
    at = 0
    for part in parts:
        ref[at : at + part.shape[0], :] = part[...]
        at += part.shape[0]


def attn_fwd_kernel(order, *refs, parts):
    w, bias, qkv, ctx, pa, pb, x = refs[parts:]
    fill(x, refs[:parts])
    half = pa.shape[0]
    local = ctx.shape[1]
    routed = bias.shape[1]
    heads = local // HEAD_DIM
    masks = head_masks(local)

    def project(cols, j):
        qkv[:, cols] = mm(x[...], w[:, cols]).astype(BF16)

    tiles(3 * local, local, project)

    def seq(rows, s):
        q = qkv[rows, 0:local]
        k = qkv[rows, local : 2 * local]
        v = qkv[rows, 2 * local : 3 * local]
        probs = seq_probs(spread(q, masks), k, bias[order[s]], heads).astype(BF16)
        ctx[rows, :] = mm(side_by_side(probs, heads), spread(v, masks)).astype(BF16)

    tiles(qkv.shape[0], routed, seq)

    def emit(cols, j):
        part = mm_t(ctx[...], w[cols, 3 * local : 4 * local]).astype(BF16)
        pa[:, cols] = part[0:half]
        pb[:, cols] = part[half:]

    tiles(pa.shape[1], 256, emit)


def attn_fwd(xa, xb, w, bias, order, local):
    rows, width = xa.shape
    return pl.pallas_call(
        functools.partial(attn_fwd_kernel, parts=1 + len(xb)),
        in_specs=[SMEM_SPEC] + [VMEM_SPEC] * (3 + len(xb)),
        out_specs=[VMEM_SPEC] * 4,
        out_shape=[
            shape((2 * rows, 3 * local), BF16),
            shape((2 * rows, local), BF16),
            shape((rows, width), BF16),
            shape((rows, width), BF16),
        ],
        scratch_shapes=[pltpu.VMEM((2 * rows, width), BF16)],
        compiler_params=params(12),
        cost_estimate=COST,
        name="attn_fwd",
    )(order, xa, *xb, w, bias)


def attn_bwd_kernel(order, *refs, parts):
    w, qkv, bias, dqkv, fa, fb, cg, g = refs[parts:]
    fill(g, refs[:parts])
    half = fa.shape[0]
    local = cg.shape[1]
    routed = bias.shape[1]
    heads = local // HEAD_DIM
    masks = head_masks(local)
    cg[...] = mm(g[...], w[:, 3 * local : 4 * local]).astype(BF16)

    def seq(rows, s):
        q4 = spread(qkv[rows, 0:local], masks)
        k = qkv[rows, local : 2 * local]
        v = qkv[rows, 2 * local : 3 * local]
        exact = seq_probs(q4, k, bias[order[s]], heads)
        c4 = spread(cg[rows, :], masks)
        prob_grad = mm_t(c4, v)
        dqkv[rows, 2 * local : 3 * local] = t_mm(exact.astype(BF16), c4).astype(BF16)
        inner = jnp.sum(exact * prob_grad, axis=-1, keepdims=True)
        score_grad = (exact * (prob_grad - inner)).astype(BF16)
        scale = HEAD_DIM**-0.5
        dq = mm(side_by_side(score_grad, heads), spread(k, masks)) * scale
        dqkv[rows, 0:local] = dq.astype(BF16)
        dqkv[rows, local : 2 * local] = (t_mm(score_grad, q4) * scale).astype(BF16)

    tiles(qkv.shape[0], routed, seq)

    def emit(cols, j):
        part = mm_t(dqkv[...], w[cols, 0 : 3 * local]).astype(BF16)
        fa[:, cols] = part[0:half]
        fb[:, cols] = part[half:]

    tiles(fa.shape[1], 256, emit)


def attn_bwd(ga, gb, w, qkv, bias, order, local):
    rows, width = ga.shape
    return pl.pallas_call(
        functools.partial(attn_bwd_kernel, parts=1 + len(gb)),
        in_specs=[SMEM_SPEC] + [VMEM_SPEC] * (4 + len(gb)),
        out_specs=[VMEM_SPEC] * 3,
        out_shape=[
            shape((2 * rows, 3 * local), BF16),
            shape((rows, width), BF16),
            shape((rows, width), BF16),
        ],
        scratch_shapes=[
            pltpu.VMEM((2 * rows, local), BF16),
            pltpu.VMEM((2 * rows, width), BF16),
        ],
        compiler_params=params(12),
        cost_estimate=COST,
        name="attn_bwd",
    )(order, ga, *gb, w, qkv, bias)


def mlp_kernel(*refs, parts):
    w, act, ug, da, db, ma, mb, n, g = refs[2 * parts :]
    fill(n, refs[:parts])
    fill(g, refs[parts : 2 * parts])
    rows, width = da.shape
    part, both, ff = w.shape
    depth = both // 2

    def up(cols, j):
        x = mm(n[...], w[:, 0:depth, cols].reshape(width, -1))
        inner = jnp.tanh(GELU_C * (x + GELU_A * (x * x * x)))
        half_in = 0.5 * (1.0 + inner)
        act[:, cols] = (x * half_in).astype(BF16)
        slope = half_in + (0.5 * GELU_C) * x * (1.0 - inner * inner) * (
            1.0 + (3.0 * GELU_A) * (x * x)
        )
        grad = mm(g[...], w[:, depth:both, cols].reshape(width, -1))
        ug[:, cols] = (grad * slope).astype(BF16)

    tiles(ff, 256, up)
    group = part * 256 // width

    def back(cols, j):
        wu = w[pl.ds(j * group, group), 0:depth, :].reshape(256, -1)
        out = mm_t(ug[...], wu).astype(BF16)
        da[:, cols] = out[0:rows]
        db[:, cols] = out[rows:]

    tiles(width, 256, back)

    def down(cols, j):
        wd = w[pl.ds(j * group, group), depth:both, :].reshape(256, -1)
        out = mm_t(act[...], wd).astype(BF16)
        ma[:, cols] = out[0:rows]
        mb[:, cols] = out[rows:]

    tiles(width, 256, down)


def mlp_both(na, nb, ga, gb, w):
    rows, width = na.shape
    ff = w.shape[2]
    return pl.pallas_call(
        functools.partial(mlp_kernel, parts=1 + len(nb)),
        in_specs=[VMEM_SPEC] * (3 + 2 * len(nb)),
        out_specs=[VMEM_SPEC] * 6,
        out_shape=[shape((2 * rows, ff), BF16)] * 2 + [shape((rows, width), BF16)] * 4,
        scratch_shapes=[pltpu.VMEM((2 * rows, width), BF16)] * 2,
        compiler_params=params(16),
        cost_estimate=COST,
        name="mlp",
    )(na, *nb, in_hbm(ga), *[in_hbm(x) for x in gb], in_hbm(w))


def turn(xt, pieces, cols):
    at = 0
    for piece in pieces:
        size = piece.shape[0]
        xt[:, at : at + size] = piece[:, cols].T
        at += size


def mlp_grads_kernel(*refs, depth, pieces):
    normed, grads = refs[:pieces], refs[pieces : 2 * pieces]
    un, uf, an, af, out, xt = refs[2 * pieces :]
    half = un.shape[0]
    width = normed[0].shape[1]
    for side, (xs, near, far) in enumerate(((normed, un, uf), (grads, an, af))):
        tiles(
            width,
            256,
            lambda cols, j, xs=xs: turn(
                xt.at[pl.ds(pl.multiple_of(j * 256, 256), 256), :], xs, cols
            ),
        )

        def block(ncols, j, near=near, far=far, side=side):
            total = mm(xt[:, 0:half], near[:, ncols]) + mm(xt[:, half:], far[:, ncols])
            for f in range(width // depth):
                at = (2 * f + side) * depth
                out[at : at + depth, ncols] = total[f * depth : (f + 1) * depth].astype(BF16)

        tiles(near.shape[1], 256, block)


def mlp_grads(normed, grads, ug, act, depth):
    width = normed[0].shape[1]
    rows, ff = ug[0].shape
    return pl.pallas_call(
        functools.partial(mlp_grads_kernel, depth=depth, pieces=len(normed)),
        in_specs=[VMEM_SPEC] * (2 * len(normed) + 4),
        out_specs=VMEM_SPEC,
        out_shape=shape((2 * width, ff), BF16),
        scratch_shapes=[pltpu.VMEM((width, 2 * rows), BF16)],
        compiler_params=params(20),
        cost_estimate=COST,
        name="mlp_grads",
    )(*normed, *grads, *ug, *act)


def attn_grads_kernel(info, *refs, pieces):
    normed, grads = refs[:pieces], refs[pieces : 2 * pieces]
    dn, df, cn, cf, first, others, *keeps, xt = refs[2 * pieces :]
    half = dn.shape[0]
    local = cn.shape[1]
    depth = first.shape[0]
    count = len(keeps)
    low = info[count] == 0
    for lane, wide, xs, near, far in (
        (0, 3 * local, normed, dn, df),
        (3 * local, local, grads, cn, cf),
    ):
        for o in range(count):
            cols = pl.ds(pl.multiple_of(info[o] * 256, 256), 256)
            turn(xt.at[o * 256 : (o + 1) * 256, :], xs, cols)

        def block(ncols, j, near=near, far=far, lane=lane):
            total = mm(xt[:, 0:half], near[:, ncols]) + mm(xt[:, half:], far[:, ncols])
            dst = pl.ds(pl.multiple_of(j * 256, 256) + lane, 256)
            for o in range(count):
                one = total[o * 256 : o * 256 + depth]
                two = total[o * 256 + depth : (o + 1) * 256]
                send, row = (first, 0) if o == 0 else (others, (o - 1) * depth)
                send[row : row + depth, dst] = jnp.where(low, two, one).astype(BF16)
                keeps[o][:, dst] = jnp.where(low, one, two)

        tiles(wide, 256, block)


def attn_grads(normed, grads, dqkv, ctx, info, depth):
    rows, local = ctx[0].shape
    count = info.shape[0] - 1
    first, others, *keeps = pl.pallas_call(
        functools.partial(attn_grads_kernel, pieces=len(normed)),
        in_specs=[SMEM_SPEC] + [VMEM_SPEC] * (2 * len(normed) + 4),
        out_specs=[VMEM_SPEC] * (2 + count),
        out_shape=[
            shape((depth, 4 * local), BF16),
            shape(((count - 1) * depth, 4 * local), BF16),
        ]
        + [shape((depth, 4 * local), F32)] * count,
        scratch_shapes=[pltpu.VMEM((count * 256, 2 * rows), BF16)],
        compiler_params=params(14),
        cost_estimate=COST,
        name="attn_grads",
    )(info, *normed, *grads, *dqkv, *ctx)
    return first, others, keeps


def swap(x, axis, mask):
    size = lax.axis_size(axis)
    return lax.ppermute(x, axis, [(i, i ^ mask) for i in range(size)])


def halves(x):
    step = x.shape[0] // 2
    return x[:step], x[step:]


def pair_swap(x):
    return tuple(swap(h, "tensor", 1) for h in halves(x))


def pair_sum(near, diag):
    return jnp.concatenate(
        [
            (n.astype(F32) + g.astype(F32)).astype(BF16)
            for n, g in zip(halves(near), pair_swap(diag))
        ],
        axis=0,
    )


def z_perm(size, shift):
    places = size // 2
    return [((f // 2 + shift) % places * 2 + f % 2, f) for f in range(size)]


def z_move(x, shift):
    return lax.ppermute(x, "fsdp", z_perm(lax.axis_size("fsdp"), shift))


SHIFTS = (2, 1, 3)


def shards(
    tokens,
    cotangent,
    routed_index,
    query_weight,
    key_weight,
    value_weight,
    output_weight,
    up_weight,
    down_weight,
    router_weight,
    attn_gain,
    mlp_gain,
):
    fsdp = lax.axis_size("fsdp")
    grid = fsdp == 8
    me_f = lax.axis_index("fsdp")
    me_t = lax.axis_index("tensor")
    seqs, span, width = tokens.shape
    routed = routed_index.shape[1]
    per = seqs // lax.axis_size("tensor")
    local = query_weight.shape[1]
    depth = query_weight.shape[0]
    ff = up_weight.shape[1]
    rows = per * routed

    place = routed_index - me_t * span
    positions = jnp.arange(span, dtype=jnp.int32)
    onehot = (place[:, :, None] == positions[None, None, :]).astype(BF16)
    order = jnp.stack([(me_t ^ m) * per + j for m in range(4) for j in range(per)])
    order_keep = jnp.concatenate([order[0:per], order[2 * per : 3 * per]])
    order_send = jnp.concatenate([order[per : 2 * per], order[3 * per :]])
    order_near = order[: 2 * per]
    order_far = order[2 * per :]

    row_shape = ((rows, width), BF16, "r")
    f32_shape = ((rows, width), F32, "r")
    gate_shape = ((rows, 128), F32, "r")
    vec_shape = ((8, width), F32, "w")

    def row_step(body, name, ins, outs):
        return row_call(body, name, ins, outs, rows, width)

    def r(*arrays):
        found = []
        for a in arrays:
            found += [(h, "h") for h in a] if isinstance(a, tuple) else [(a, "r")]
        return found

    zi = me_f // 2
    yi = me_f % 2

    small = jnp.stack([router_weight, attn_gain, mlp_gain])
    if grid:
        small = jnp.concatenate([small, jnp.zeros((13, depth), BF16)], axis=0)
        attn_piece = pack_attn(query_weight, key_weight, value_weight, output_weight, small)
        z_pieces = [z_move(attn_piece, o) for o in SHIFTS]
        far_own = swap(attn_piece, "fsdp", 1)
        z_at = jnp.stack([zi] + [(zi + o) % (fsdp // 2) for o in SHIFTS] + [yi])
    else:
        attn_piece = jnp.concatenate(
            [query_weight, key_weight, value_weight, output_weight.T], axis=1
        )
        z_pieces = []
        vec = lax.all_gather(small, "fsdp", axis=1, tiled=True)
        vec = jnp.concatenate([vec, jnp.zeros((5, width), BF16)], axis=0).astype(F32)
    tok_send = pick_rows(tokens, onehot, after(order_send, attn_piece))
    tok_got = pair_swap(tok_send)
    tok_keep = pick_rows(tokens, onehot, after(order_keep, tok_send))
    tok_sum = tok_keep[rows:] + tok_got[1]
    tok_far = [swap(h, "tensor", 2) for h in halves(tok_sum)]
    cot_send = pick_rows(cotangent, onehot, after(order_send, tok_sum))
    cot_got = pair_swap(cot_send)
    cot_keep = pick_rows(cotangent, onehot, after(order_keep, cot_send))
    cot_sum = cot_keep[rows:] + cot_got[1]
    cot_far = [swap(h, "tensor", 2) for h in halves(cot_sum)]
    if grid:
        mlp_piece = pack_mlp(up_weight, after(down_weight, cot_keep))
        gated = [after(z, mlp_piece, *tok_far, *cot_far) for z in z_pieces]
        near_w, vec_near = join([attn_piece] + gated, z_at, depth)
        vec = vec_near + swap(vec_near, "fsdp", 1)
        far_w = swap(after(near_w, vec), "fsdp", 1)
        vec = vec[0:8].astype(F32)
        mlp_piece = after(mlp_piece, near_w)
    else:
        mlp_piece = jnp.concatenate([up_weight, down_weight.T], axis=0)
    up_down = lax.all_gather(mlp_piece, "fsdp", axis=0, tiled=True)
    up_down = up_down.reshape(fsdp, 2 * depth, ff)

    def with_halves(body):
        def whole(keep, got, far0, far1, *rest):
            far = jnp.where(pl.program_id(0) == 0, far0[...], far1[...])
            return body(keep, got, got, far, *rest)

        return whole

    own_rows, n0, gate = row_step(
        with_halves(first_norm_body),
        "first_norm",
        [(tok_keep, "r"), (tok_got[0], "r")] + r(tuple(tok_far)) + [(vec, "w")],
        [row_shape, row_shape, gate_shape],
    )
    n2 = swap(n0, "tensor", 2)
    n1 = swap(n0, "tensor", 1)
    cot, g0 = row_step(
        with_halves(cot_body),
        "cot_rows",
        [(cot_keep, "r"), (cot_got[0], "r")] + r(tuple(cot_far)) + [(after(gate, n0), "r")],
        [row_shape, row_shape],
    )
    g2 = swap(after(g0, n2), "tensor", 2)
    g1 = swap(g0, "tensor", 1)
    blocks = after(routed_index, g0) // BLOCK
    bias = jnp.where(blocks[:, None, :] <= blocks[:, :, None], 0.0, NEG).astype(F32)
    if grid:
        attn_w = assemble(attn_piece, after(near_w, g0), far_own, far_w, z_at)
    else:
        attn_w = lax.all_gather(attn_piece, "fsdp", axis=0, tiled=True)
    n3 = pair_swap(after(n2, attn_w))

    qkv_far, ctx_far, p2, p3 = attn_fwd(
        after(n2, g2), n3, attn_w, bias, order_far, local
    )
    attn_sum = pair_sum(p2, p3)
    attn_x = swap(attn_sum, "tensor", 2)
    qkv_near, ctx_near, p0, p1 = attn_fwd(
        after(n0, attn_sum), (n1,), attn_w, bias, order_near, local
    )
    attn_c = pair_swap(p1)
    attn, s0 = row_step(
        second_norm_body,
        "second_norm",
        r(own_rows, p0, attn_c, attn_x) + [(vec, "w")],
        [f32_shape, row_shape],
    )
    s2 = swap(s0, "tensor", 2)
    s1 = swap(s0, "tensor", 1)
    s3 = pair_swap(s2)
    g3 = pair_swap(after(g2, s0))

    act_far, ug_far, d2, d3, m2, m3 = mlp_both(s2, s3, g2, g3, up_down)
    second_sum = pair_sum(d2, d3)
    second_x = swap(second_sum, "tensor", 2)
    act_near, ug_near, d0, d1, m0, m1 = mlp_both(
        after(s0, second_sum), (s1,), g0, (g1,), up_down
    )
    second_c = pair_swap(d1)

    attn_grad, hidden_grad, second_part = row_step(
        second_back_body,
        "second_back",
        r(own_rows, attn, cot, gate, d0, second_c, second_x) + [(vec, "w")],
        [row_shape, f32_shape, vec_shape],
    )
    a0 = attn_grad
    a2 = swap(a0, "tensor", 2)
    a1 = swap(a0, "tensor", 1)
    mlp_all = mlp_grads(
        (after(s0, a0), s1, s2, *s3),
        (g0, g1, g2, *g3),
        (ug_near, ug_far),
        (act_near, act_far),
        depth,
    )
    a2 = after(a2, mlp_all)
    mlp_total = lax.psum_scatter(after(mlp_all, a2), "fsdp", scatter_dimension=0, tiled=True)
    a3 = pair_swap(a2)
    mlp_c = pair_swap(after(m1, mlp_all))
    mlp_sum = pair_sum(m2, after(m3, mlp_all))
    mlp_x = swap(after(mlp_sum, a2), "tensor", 2)

    def to_z(keep, got, shift):
        return z_move((keep + got.astype(F32)).astype(BF16), 4 - shift)

    dqkv_far, f2, f3 = attn_bwd(a2, a3, attn_w, qkv_far, bias, order_far, local)
    first_sum = pair_sum(f2, f3)
    first_x = swap(first_sum, "tensor", 2)
    dqkv_near, f0, f1 = attn_bwd(
        after(a0, first_sum), (a1,), attn_w, qkv_near, bias, order_near, local
    )
    first_c = pair_swap(f1)
    out_rows, gate_grad, router_part = row_step(
        out_body,
        "out_rows",
        r(own_rows, attn, cot, gate, m0, mlp_c, after(mlp_x, f1)),
        [row_shape, gate_shape, vec_shape],
    )
    o2 = swap(out_rows, "tensor", 2)
    o1 = swap(out_rows, "tensor", 1)

    attn_args = (
        (n0, n1, n2, *n3),
        (a0, a1, a2, *a3),
        (dqkv_near, dqkv_far),
        (ctx_near, ctx_far),
    )
    if grid:
        info = jnp.stack([(zi + o) % (fsdp // 2) for o in SHIFTS + (0,)] + [yi])
        first_b, other_b, keeps = attn_grads(*attn_args, after(info, out_rows), depth)
        first_y = swap(first_b, "fsdp", 1)
        other_y = swap(other_b, "fsdp", 1)
        first_x = after(first_x, first_b)

    half = rows // 2
    grad_rows, vec_part = pl.pallas_call(
        first_back_body,
        grid=(2,),
        in_specs=[
            pl.BlockSpec((half, width), lambda i: (i, 0)),
            pl.BlockSpec((half, width), lambda i: (i, 0)),
            pl.BlockSpec((half, 128), lambda i: (i, 0)),
        ]
        + [pl.BlockSpec((half, width), lambda i: (i, 0))] * 2
        + [pl.BlockSpec((half, width), lambda i: (0, 0))] * 2
        + [pl.BlockSpec((half, width), lambda i: (i, 0))]
        + [pl.BlockSpec((8, width), lambda i: (0, 0))] * 3,
        out_specs=[
            pl.BlockSpec((half, width), lambda i: (i, 0)),
            pl.BlockSpec((8, width), lambda i: (0, 0)),
        ],
        out_shape=[shape((rows, width), BF16), shape((8, width), F32)],
        scratch_shapes=[pltpu.VMEM((8, width), F32)],
        compiler_params=params(12),
        cost_estimate=COST,
        name="first_back",
    )(own_rows, cot, gate_grad, hidden_grad, f0, *first_c, first_x, vec, router_part, second_part)
    t2 = swap(grad_rows, "tensor", 2)
    t1 = swap(grad_rows, "tensor", 1)
    onehot_t = (
        after(place, grad_rows)[:, None, :] == positions[None, :, None]
    ).astype(BF16)
    o3 = pair_swap(after(o2, grad_rows))
    mixed = place_rows(tokens, onehot_t, [after(out_rows, grad_rows), o1], order_near)
    if grid:
        z_first = to_z(keeps[0], after(first_y, grad_rows), SHIFTS[0])
    mixed = place_rows(tokens, onehot_t, [o2, *o3], order_far, mixed)
    near_gate = mixed
    if grid:
        other_y = after(other_y, near_gate)
        z_second = to_z(keeps[1], other_y[0:depth], SHIFTS[1])
        z_third = to_z(keeps[2], other_y[depth : 2 * depth], SHIFTS[2])
    token_grad = place_rows(cotangent, onehot_t, [after(grad_rows, near_gate), t1], order_near)
    t3 = pair_swap(after(t2, token_grad))
    token_grad = place_rows(cotangent, onehot_t, [t2, *t3], order_far, token_grad)
    up_grad, down_grad = finish(
        finish_mlp_kernel, "finish_mlp", [(depth, ff), (ff, depth)], after(mlp_total, token_grad)
    )

    if grid:
        vec_sum = after(vec_part, token_grad)
        for axis, mask in (("tensor", 1), ("tensor", 2)):
            vec_sum = vec_sum + swap(vec_sum, axis, mask)
        vec_sum = vec_sum + after(swap(vec_sum, "fsdp", 1), token_grad)
        vec_sum = vec_sum + z_move(vec_sum, 1) + z_move(vec_sum, 3) + z_move(vec_sum, 2)
        wide = (depth, local)
        attn_out = finish(
            finish_attn_kernel,
            "finish_attn",
            [wide, wide, wide, (local, depth)],
            keeps[3],
            after(other_y[2 * depth :], token_grad),
            z_first,
            z_second,
            z_third,
        )
    else:

        def reduced(xs, ys):
            x = t_mm(jnp.concatenate(xs, axis=0), jnp.concatenate(ys, axis=0))
            return lax.psum_scatter(x, "fsdp", scatter_dimension=0, tiled=True)

        qkv_grad = reduced(attn_args[0], attn_args[2])
        o_grad = reduced(attn_args[1], attn_args[3])
        attn_out = jnp.split(qkv_grad, 3, axis=1) + [o_grad.T]
        vec_sum = lax.psum(vec_part, ("fsdp", "tensor"))
    vec_own = lax.dynamic_slice(vec_sum, (0, me_f * depth), (3, depth))

    return (mixed, token_grad, *attn_out, up_grad, down_grad, vec_own[0], vec_own[1], vec_own[2])


def solution(mesh):
    in_specs = (
        P("fsdp", "tensor", None),
        P("fsdp", "tensor", None),
        P("fsdp", None),
        P("fsdp", "tensor"),
        P("fsdp", "tensor"),
        P("fsdp", "tensor"),
        P("tensor", "fsdp"),
        P("fsdp", "tensor"),
        P("tensor", "fsdp"),
        P("fsdp"),
        P("fsdp"),
        P("fsdp"),
    )
    out_specs = (
        P("fsdp", "tensor", None),
        P("fsdp", "tensor", None),
        P("fsdp", "tensor"),
        P("fsdp", "tensor"),
        P("fsdp", "tensor"),
        P("tensor", "fsdp"),
        P("fsdp", "tensor"),
        P("tensor", "fsdp"),
        P("fsdp"),
        P("fsdp"),
        P("fsdp"),
    )
    return jax.shard_map(shards, mesh=mesh, in_specs=in_specs, out_specs=out_specs, check_vma=False)
```
